128 devices in a mesh: section: 4 (over y_hi, core), seq: 32 (over y_lo, x, z).
Axes of the slice: x: 4, y: 4 (y_hi: 2, y_lo: 2; y = y_hi * 2 + y_lo), z: 4, core: 2. Of those that a mesh axis runs over, the one named last changes fastest.
Arguments:
- activations: bfloat16 [4, 4352, 1024], P('section', 'seq'), may hold values from -60 to 60
- incoming: bfloat16 [4, 4352, 1024], P('section', 'seq'), may hold values from -6 to 6
- w_query: bfloat16 [4, 1024, 512], P('section'), may hold values from -0.1875 to 0.1875
- w_key: bfloat16 [4, 1024, 512], P('section'), may hold values from -0.1875 to 0.1875
- w_value: bfloat16 [4, 1024, 512], P('section'), may hold values from -0.1875 to 0.1875
- w_out: bfloat16 [4, 512, 2048], P('section'), may hold values from -0.25 to 0.25
- block_ids: int32 [4352], replicated, may hold values from 0 to 135, never falling along the last dimension, each value on 1 to 256 neighbouring positions
- flip_order: int32 [4, 136], P('section'), may hold values from 0 to 135, each once within a row
Outputs:
- carry_out: bfloat16 [4, 4352, 1024], P('section', 'seq')
- grad_query: float32 [4, 1024, 512], P('section', 'seq')
- grad_key: float32 [4, 1024, 512], P('section', 'seq')
- grad_value: float32 [4, 1024, 512], P('section', 'seq')
- grad_out: float32 [4, 512, 2048], P('section', 'seq')
The draws below stay inside these ranges and needn't reach their ends.
Inputs may be any that keep to these rules, and one draw needn't show every extreme that they name: `block_ids`: block ids never fall along the sequence; each block holds 1 to 256 tokens, one exactly 256. `flip_order`: each row is a permutation.
All inputs are finite; a program needn't handle non-finite values.
Results may differ from the reference program's by a relative error of at most 0.03.
Values may be sent and summed in bfloat16 or wider, within the bound.
A program may use at most 128 MiB of HBM per device.

```python
import math
import jax
import jax.numpy as jnp
import numpy as np
from jax import lax

D = 1024
HEADS = 8
HEAD_DIM = 64
BLOCK_MOST = 256
TOK_DEV = 136
INNER = 512
TOKENS = 4352
SECTIONS = 4
BLOCKS = 136
N_SEQ = 32


def draw_activations(key, part):
    base_key, row_key, column_key = jax.random.split(key, 3)
    shape = (SECTIONS, TOKENS, D)
    base = jnp.clip(jax.random.normal(base_key, shape, jnp.float32), -6.0, 6.0)
    row_scale = jnp.exp(jax.random.uniform(row_key, (SECTIONS, TOKENS, 1), jnp.float32, math.log(0.3), math.log(3.0)))
    column_scale = jnp.exp(jax.random.uniform(column_key, (SECTIONS, 1, D), jnp.float32, math.log(0.3), math.log(3.0)))
    return (base * row_scale * column_scale).astype(jnp.bfloat16)


def steps_of(stream_key, extent, cuts, smallest, high):
    def one(position, blocks):
        draws = jax.random.uniform(jax.random.fold_in(jax.random.fold_in(stream_key, 6), position), (blocks,), jnp.float32, smallest / len(cuts), high / len(cuts))
        return jnp.repeat(jnp.exp(draws), extent[position] // blocks).reshape((-1,) + (1,) * (len(extent) - position - 1))

    level = one(*cuts[0])
    for cut in cuts[1:]:
        level = level * one(*cut)
    return level


def split_up(number_of, total, most, lean):
    weights = [(1 << 20) // math.isqrt(standing ** lean) + 1 for standing in range(2, number_of + 1)]
    spare, counts = total - most - (number_of - 1), [1] * (number_of - 1)
    while spare > 0:
        candidates = [i for i in range(number_of - 1) if counts[i] < most]
        whole, remaining = sum([weights[i] for i in candidates]), spare
        for i in candidates:
            more = min(most - counts[i], max(1, remaining * weights[i] // whole), spare)
            counts[i] = counts[i] + more
            spare = spare - more
    return np.array([most] + counts)


def ragged(key, count, total, bound, lean):
    if count == 2:
        one = jax.random.randint(key, (), max(1, total - bound), min(bound, total - 1) + 1)
        return jnp.stack([one, total - one])
    sizes = jnp.asarray(split_up(count, total, bound, lean), jnp.int32)
    pairs = (count - 1) // 2
    donor, taker = sizes[1:1 + 2 * pairs:2], sizes[2:2 + 2 * pairs:2]
    margin = jnp.minimum(donor - 1, bound - taker)
    shifted = jax.random.randint(jax.random.fold_in(key, 1), (pairs,), 0, 1 << 20) % (margin + 1)
    sizes = sizes.at[1:1 + 2 * pairs:2].set(donor - shifted).at[2:2 + 2 * pairs:2].set(taker + shifted)
    return sizes[jax.random.permutation(jax.random.fold_in(key, 2), count)]


def noise(key, shape, deviation, limit, cuts=(), dtype=jnp.bfloat16):
    drawn = deviation * jax.random.normal(key, shape, jnp.float32)
    if cuts:
        drawn = drawn * steps_of(key, shape, cuts, -0.22, 0.18)
    return jnp.clip(drawn, -limit, limit).astype(dtype)


def setup_inputs(seed: int = 0) -> dict:
    seeds = jax.random.split(jax.random.key(seed), 9)
    return {
        "activations": draw_activations(jax.random.fold_in(seeds[8], 71), 0),
        "incoming": noise(seeds[1], (SECTIONS, TOKENS, D), 1.0, 6.0, ((0, 4), (1, 32))),
        "w_query": noise(seeds[2], (SECTIONS, D, INNER), D ** -0.5, 0.1875, ((0, 4),)),
        "w_key": noise(seeds[3], (SECTIONS, D, INNER), D ** -0.5, 0.1875, ((0, 4),)),
        "w_value": noise(seeds[4], (SECTIONS, D, INNER), D ** -0.5, 0.1875, ((0, 4),)),
        "w_out": noise(seeds[5], (SECTIONS, INNER, 2 * D), INNER ** -0.5, 0.25, ((0, 4),)),
        "block_ids": jnp.searchsorted(jnp.cumsum(ragged(seeds[6], BLOCKS, TOKENS, BLOCK_MOST, 2)), jnp.arange(TOKENS), side="right").astype(jnp.int32),
        "flip_order": jax.vmap(lambda own: jax.random.permutation(own, TOK_DEV))(jax.random.split(seeds[7], SECTIONS)).reshape((SECTIONS, TOK_DEV)).astype(jnp.int32),
    }


EPSILON = 1e-06

def unit_heads(projected):
    parts = projected.reshape(projected.shape[0], HEADS, HEAD_DIM)
    factor = lax.rsqrt(lax.optimization_barrier(jnp.mean(parts * parts, axis=-1, keepdims=True)) + EPSILON)
    return (parts * factor, factor)

def unit_back(grad_heads, unit, factor):
    return factor * (grad_heads - unit * lax.optimization_barrier(jnp.mean(grad_heads * unit, axis=-1, keepdims=True)))

def head_major(matrix):
    return jnp.transpose(matrix.reshape(matrix.shape[0], HEADS, HEAD_DIM), (1, 0, 2))

def group_sum(left, right):
    left_groups = left.astype(jnp.float32).reshape(N_SEQ, TOK_DEV, left.shape[1])
    right_groups = right.astype(jnp.float32).reshape(N_SEQ, TOK_DEV, right.shape[1])
    terms = jnp.einsum('ntc,nte->nce', left_groups, right_groups)
    rounded = lax.optimization_barrier(terms.astype(jnp.bfloat16))
    return lax.optimization_barrier(jnp.sum(rounded.astype(jnp.float32), axis=0))

def layer_backward(field_low, cotangent, weight_query, weight_key, weight_value, weight_out, block_ids):
    field = field_low.astype(jnp.float32)
    upstream = cotangent.astype(jnp.float32)
    length = field.shape[0]
    scale = HEAD_DIM ** (-0.5)
    row_scale = lax.rsqrt(lax.optimization_barrier(jnp.mean(field * field, axis=-1, keepdims=True)) + EPSILON)
    unit_rows = field * row_scale
    normed = unit_rows.astype(jnp.bfloat16)
    query_raw = jnp.dot(normed, weight_query, preferred_element_type=jnp.float32)
    key_raw = jnp.dot(normed, weight_key, preferred_element_type=jnp.float32)
    values = jnp.dot(normed, weight_value, preferred_element_type=jnp.float32).astype(jnp.bfloat16)
    query_unit, query_scale = unit_heads(query_raw)
    key_unit, key_scale = unit_heads(key_raw)
    queries = query_unit.astype(jnp.bfloat16).reshape(length, INNER)
    keys = key_unit.astype(jnp.bfloat16).reshape(length, INNER)
    allowed = block_ids[None, :] <= block_ids[:, None]

    def probabilities(query_part, key_part):
        scores = jnp.dot(query_part, key_part.T, preferred_element_type=jnp.float32) * scale
        numerator = jnp.where(allowed, jnp.exp(scores), 0.0)
        return numerator / lax.optimization_barrier(jnp.sum(numerator, axis=-1, keepdims=True))

    def forward_head(operands):
        query_part, key_part, value_part = operands
        probs = probabilities(query_part, key_part)
        return jnp.dot(probs.astype(jnp.bfloat16), value_part, preferred_element_type=jnp.float32).astype(jnp.bfloat16)
    query_heads = head_major(queries)
    key_heads = head_major(keys)
    value_heads = head_major(values)
    heads_out = lax.map(forward_head, (query_heads, key_heads, value_heads))
    attended = jnp.transpose(heads_out, (1, 0, 2)).reshape(length, INNER)
    affine = jnp.dot(attended, weight_out, preferred_element_type=jnp.float32)
    shift_part = affine[:, :D]
    log_scale = affine[:, D:]
    factor = jnp.exp(-log_scale)
    latent = (field - shift_part) * factor
    grad_affine = jnp.concatenate([-upstream * factor, 1.0 - upstream * latent], axis=-1).astype(jnp.bfloat16)
    grad_out = group_sum(attended, grad_affine)
    grad_attn = jnp.dot(grad_affine, weight_out.T, preferred_element_type=jnp.float32).astype(jnp.bfloat16)
    grad_heads = head_major(grad_attn)

    def backward_head(operands):
        query_part, key_part, value_part, grad_part, out_part = operands
        probs = probabilities(query_part, key_part)
        grad_probs = jnp.dot(grad_part, value_part.T, preferred_element_type=jnp.float32)
        correction = lax.optimization_barrier(jnp.sum(grad_part.astype(jnp.float32) * out_part.astype(jnp.float32), axis=-1, keepdims=True))
        grad_scores = (probs * (grad_probs - correction)).astype(jnp.bfloat16)
        grad_qpart = jnp.dot(grad_scores, key_part, preferred_element_type=jnp.float32) * scale
        grad_kpart = jnp.dot(grad_scores.T, query_part, preferred_element_type=jnp.float32) * scale
        grad_vpart = jnp.dot(probs.astype(jnp.bfloat16).T, grad_part, preferred_element_type=jnp.float32)
        return (grad_qpart, grad_kpart, grad_vpart)
    grad_qheads, grad_kheads, grad_vheads = lax.map(backward_head, (query_heads, key_heads, value_heads, grad_heads, heads_out))
    grad_queries = unit_back(jnp.transpose(grad_qheads, (1, 0, 2)), query_unit, query_scale).reshape(length, INNER).astype(jnp.bfloat16)
    grad_keys = unit_back(jnp.transpose(grad_kheads, (1, 0, 2)), key_unit, key_scale).reshape(length, INNER).astype(jnp.bfloat16)
    grad_values = jnp.transpose(grad_vheads, (1, 0, 2)).reshape(length, INNER).astype(jnp.bfloat16)
    grad_query = group_sum(normed, grad_queries)
    grad_key = group_sum(normed, grad_keys)
    grad_value = group_sum(normed, grad_values)
    grad_normed = jnp.dot(grad_queries, weight_query.T, preferred_element_type=jnp.float32)
    grad_normed = grad_normed + jnp.dot(grad_keys, weight_key.T, preferred_element_type=jnp.float32)
    grad_normed = grad_normed + jnp.dot(grad_values, weight_value.T, preferred_element_type=jnp.float32)
    grad_input = upstream * factor + row_scale * (grad_normed - unit_rows * lax.optimization_barrier(jnp.mean(grad_normed * unit_rows, axis=-1, keepdims=True)))
    return (grad_input.astype(jnp.bfloat16), grad_query, grad_key, grad_value, grad_out)

def reference(activations, incoming, w_query, w_key, w_value, w_out, block_ids, flip_order):
    results = []
    for layer in range(SECTIONS):
        results.append(layer_backward(activations[layer], incoming[layer], w_query[layer], w_key[layer], w_value[layer], w_out[layer], block_ids))
    carries = []
    for layer in range(SECTIONS):
        if layer + 1 < SECTIONS:
            grouped = results[layer + 1][0].reshape(N_SEQ, TOK_DEV, D)[::-1]
            carries.append(grouped[:, flip_order[layer], :].reshape(TOKENS, D))
        else:
            carries.append(jnp.zeros((TOKENS, D), jnp.bfloat16))
    carry_out = jnp.stack(carries)
    grad_query = jnp.stack([item[1] for item in results])
    grad_key = jnp.stack([item[2] for item in results])
    grad_value = jnp.stack([item[3] for item in results])
    grad_out = jnp.stack([item[4] for item in results])
    return (carry_out, grad_query, grad_key, grad_value, grad_out)
```

```python
import jax
import jax.numpy as jnp
from jax import lax
from jax.experimental import pallas as pl
from jax.experimental.pallas import tpu as pltpu
from jax.sharding import PartitionSpec as P

HEADS = 8
HEAD_DIM = 64
EPSILON = 1e-06
N_SEQ = 32
TOK = 136
TOKENS = 4352
D = 1024
INNER = 512
KT = 256
REACH = TOK + 255
BF = jnp.bfloat16
F32 = jnp.float32
MESH = pl.DeviceIdType.MESH
VMEM = pl.BlockSpec(memory_space=pltpu.VMEM)
ANY = pl.BlockSpec(memory_space=pl.ANY)
BIG = 60 * 1024 * 1024


def dot(a, b):
    return jnp.dot(a, b, preferred_element_type=F32)


def dot_t(a, b):
    return lax.dot_general(a, b, (((1,), (1,)), ((), ())), preferred_element_type=F32)


def left_half(shape):
    return lax.broadcasted_iota(jnp.int32, shape, 1) < HEAD_DIM


def swap(slab):
    return pltpu.roll(slab, HEAD_DIM, 1)


def per_head_sum(slab, left):
    low = jnp.sum(jnp.where(left, slab, 0.0), axis=-1, keepdims=True)
    high = jnp.sum(jnp.where(left, 0.0, slab), axis=-1, keepdims=True)
    return jnp.where(left, low, high)


def unit_scale(slab, left):
    return lax.rsqrt(per_head_sum(slab * slab, left) * (1.0 / HEAD_DIM) + EPSILON)


def project_body(act, wq, wk, wv, normed, q_raw, k_raw, q_pack, kv_pack):
    field = act[...].astype(F32)
    scale = lax.rsqrt(jnp.mean(field * field, axis=-1, keepdims=True) + EPSILON)
    normed[...] = (field * scale).astype(BF)
    left = left_half((TOK, 128))
    for block in range(2):
        columns = pl.ds(256 * block, 256)
        q = dot(normed[...], wq[:, columns])
        k = dot(normed[...], wk[:, columns])
        v = dot(normed[...], wv[:, columns])
        q_raw[:, columns] = q
        k_raw[:, columns] = k
        for half in range(2):
            head = 4 * block + 2 * half
            q_slab = q[:, 128 * half : 128 * half + 128]
            k_slab = k[:, 128 * half : 128 * half + 128]
            v_slab = v[:, 128 * half : 128 * half + 128]
            q_slab = (q_slab * unit_scale(q_slab, left)).astype(BF).astype(F32) * 0.125
            k_slab = k_slab * unit_scale(k_slab, left)
            q_pack[head] = jnp.where(left, q_slab, 0.0).astype(BF)
            q_pack[head + 1] = jnp.where(left, swap(q_slab), 0.0).astype(BF)
            kv_pack[head] = jnp.where(left, k_slab, swap(v_slab)).astype(BF)
            kv_pack[head + 1] = jnp.where(left, swap(k_slab), v_slab).astype(BF)


def tile_bounds(first):
    whole = lax.div(first, KT)
    end = lax.min(lax.div(first + REACH + KT - 1, KT), TOKENS // KT)
    return whole, end


def forward_body(q_all, kv, q_ids, k_ids, out, inverse):
    group = lax.rem(lax.axis_index("seq"), 4)

    def chunk(i, _):
        whole, end = tile_bounds((4 * i + group) * TOK)
        q = q_all[i]
        ids = q_ids[i]

        def tile(j, carry, masked):
            total, mass = carry
            block = kv[pl.ds(pl.multiple_of(j * KT, KT), KT), :]
            p = jnp.exp(dot_t(q, block))
            if masked:
                p = jnp.where(k_ids[j] <= ids, p, 0.0)
            mass = mass + (p[:, :128] + p[:, 128:])
            total = total + dot(p.astype(BF), block)
            return total, mass

        zero = jnp.zeros((TOK, 128), F32)
        carry = lax.fori_loop(0, whole, lambda j, c: tile(j, c, False), (zero, zero))
        total, mass = lax.fori_loop(whole, end, lambda j, c: tile(j, c, True), carry)
        one_over = 1.0 / jnp.sum(mass, axis=-1, keepdims=True)
        out[i] = (total * one_over).astype(BF)
        inverse[i] = jnp.broadcast_to(one_over, (TOK, 128))
        return 0

    lax.fori_loop(0, HEADS, chunk, 0)


def backward_body(q_all, g_all, out, inverse, kv, q_ids, k_ids, dq, dkv, total):
    group = lax.rem(lax.axis_index("seq"), 4)
    total[...] = jnp.zeros_like(total)

    def chunk(i, _):
        whole, end = tile_bounds((4 * i + group) * TOK)
        q = q_all[i]
        g = g_all[i]
        ids = q_ids[i]
        one_over = inverse[i][:, :1]
        correction = jnp.sum(g.astype(F32) * out[i].astype(F32), axis=-1, keepdims=True)
        q_turned = jnp.transpose(q.astype(F32))[:HEAD_DIM].astype(BF)
        g_turned = jnp.transpose(g.astype(F32))[HEAD_DIM:].astype(BF)

        def tile(j, acc, masked):
            at = pl.ds(pl.multiple_of(j * KT, KT), KT)
            block = kv[at, :]
            p = jnp.exp(dot_t(q, block)) * one_over
            if masked:
                p = jnp.where(k_ids[j] <= ids, p, 0.0)
            ds = (p * (dot_t(g, block) - correction)).astype(BF)
            total[:HEAD_DIM, at] += dot(q_turned, ds)
            total[HEAD_DIM:, at] += dot(g_turned, p.astype(BF))
            return acc + dot(ds, block)

        acc = jnp.zeros((TOK, 128), F32)
        acc = lax.fori_loop(0, whole, lambda j, c: tile(j, c, False), acc)
        acc = lax.fori_loop(whole, end, lambda j, c: tile(j, c, True), acc)
        dq[i] = (acc * 0.125).astype(BF)
        return 0

    lax.fori_loop(0, HEADS, chunk, 0)

    def turn(j, _):
        at = pl.ds(pl.multiple_of(j * KT, KT), KT)
        dkv[at, :] = jnp.transpose(total[:, at]).astype(BF)
        return 0

    lax.fori_loop(0, TOKENS // KT, turn, 0)


def affine_body(act, up, att_all, w_out, g_pack, carry_part, out_term, att, att_turned, grad):
    left = left_half((TOK, 128))
    for pair in range(HEADS // 2):
        low = att_all[2 * pair].astype(F32)
        high = att_all[2 * pair + 1].astype(F32)
        slab = jnp.where(left, swap(low), high)
        att[:, 128 * pair : 128 * pair + 128] = slab.astype(BF)
        att_turned[128 * pair : 128 * pair + 128, :] = jnp.transpose(slab).astype(BF)
    for block in range(4):
        columns = pl.ds(256 * block, 256)
        behind = pl.ds(D + 256 * block, 256)
        shift = dot(att[...], w_out[:, columns])
        factor = jnp.exp(-dot(att[...], w_out[:, behind]))
        upstream = up[:, columns].astype(F32)
        latent = (act[:, columns].astype(F32) - shift) * factor
        scaled = upstream * factor
        carry_part[:, columns] = scaled
        grad[:, columns] = (-scaled).astype(BF)
        grad[:, behind] = (1.0 - upstream * latent).astype(BF)
    for block in range(2):
        g = dot_t(grad[...], w_out[pl.ds(256 * block, 256), :])
        for half in range(2):
            head = 4 * block + 2 * half
            slab = g[:, 128 * half : 128 * half + 128]
            g_pack[head] = jnp.where(left, 0.0, swap(slab)).astype(BF)
            g_pack[head + 1] = jnp.where(left, 0.0, slab).astype(BF)
    for block in range(8):
        columns = pl.ds(256 * block, 256)
        out_term[:, columns] = dot(att_turned[...], grad[:, columns]).astype(BF)


def finish_body(act, normed, carry_part, q_raw, k_raw, dq_all, dkv_parts, wq, wk, wv,
                grad_input, terms, grads, gn, normed_turned):
    left = left_half((TOK, 128))

    def unit_back(grad, raw):
        scale = unit_scale(raw, left)
        unit = raw * scale
        return scale * (grad - unit * (per_head_sum(grad * unit, left) * (1.0 / HEAD_DIM)))

    def keys_of(head):
        part = [dkv_parts[4 * head + i].astype(F32) for i in range(4)]
        return (part[0] + part[1]) + (part[2] + part[3])

    for pair in range(HEADS // 2):
        at = pl.ds(128 * pair, 128)
        low, high = dq_all[2 * pair].astype(F32), dq_all[2 * pair + 1].astype(F32)
        q_grad = jnp.where(left, low, swap(high))
        low, high = keys_of(2 * pair), keys_of(2 * pair + 1)
        k_grad = jnp.where(left, low, swap(high))
        v_grad = jnp.where(left, swap(low), high)
        grads[0, :, at] = unit_back(q_grad, q_raw[:, at]).astype(BF)
        grads[1, :, at] = unit_back(k_grad, k_raw[:, at]).astype(BF)
        grads[2, :, at] = v_grad.astype(BF)
    for block in range(8):
        at = pl.ds(128 * block, 128)
        normed_turned[at, :] = jnp.transpose(normed[:, at].astype(F32)).astype(BF)
    for block in range(4):
        at = pl.ds(256 * block, 256)
        gn[:, at] = dot_t(grads[0], wq[at, :]) + dot_t(grads[1], wk[at, :]) + dot_t(grads[2], wv[at, :])
    field = act[...].astype(F32)
    scale = lax.rsqrt(jnp.mean(field * field, axis=-1, keepdims=True) + EPSILON)
    unit = field * scale
    grad_normed = gn[...]
    mean = jnp.mean(grad_normed * unit, axis=-1, keepdims=True)
    grad_input[...] = (carry_part[...] + scale * (grad_normed - unit * mean)).astype(BF)
    for which in range(3):
        for block in range(2):
            terms[:, INNER * which + 256 * block : INNER * which + 256 * block + 256] = dot(
                normed_turned[...], grads[which, :, 256 * block : 256 * block + 256]
            ).astype(BF)


def local_call(body, outs, scratch=(), name=None):
    return pl.pallas_call(
        body,
        out_shape=[jax.ShapeDtypeStruct(shape, dtype) for shape, dtype in outs],
        out_specs=[VMEM] * len(outs),
        scratch_shapes=[pltpu.VMEM(shape, dtype) for shape, dtype in scratch],
        compiler_params=pltpu.CompilerParams(vmem_limit_bytes=BIG),
        name=name,
    )


def exchange(full, plane, by_head, identity, name):
    n_full, n_plane = (0 if full is None else 1), (0 if plane is None else 1)

    def body(*refs):
        refs = list(refs)
        sources = [refs.pop(0) for _ in range(n_full + n_plane)]
        targets = [refs.pop(0) for _ in range(n_full + n_plane)]
        full_send, full_recv, plane_send, plane_recv, local_sem = refs
        me = lax.axis_index("seq")
        mine = lax.div(me, 4)
        count, stride = (N_SEQ, 1) if n_full else (HEADS, 4)

        barrier = pltpu.get_barrier_semaphore()

        def greet(k, _):
            pl.semaphore_signal(barrier, inc=1, device_id={"seq": lax.rem(me + stride * k, N_SEQ)}, device_id_type=MESH)
            return 0

        lax.fori_loop(1, count, greet, 0)
        pl.semaphore_wait(barrier, count - 1)

        def full_copy(k):
            peer = lax.rem(me + k, N_SEQ)
            return pltpu.make_async_remote_copy(
                src_ref=sources[0].at[lax.div(peer, 4) if by_head else peer],
                dst_ref=targets[0].at[me],
                send_sem=full_send.at[k],
                recv_sem=full_recv.at[k],
                device_id={"seq": peer},
                device_id_type=MESH,
            )

        def plane_copy(k):
            peer = lax.rem(me + 4 * k, N_SEQ)
            return pltpu.make_async_remote_copy(
                src_ref=sources[-1].at[lax.div(peer, 4)],
                dst_ref=targets[-1].at[mine],
                send_sem=plane_send.at[k],
                recv_sem=plane_recv.at[k],
                device_id={"seq": peer},
                device_id_type=MESH,
            )

        local = []
        if n_plane:
            local.append(pltpu.make_async_copy(sources[-1].at[mine], targets[-1].at[mine], local_sem.at[1]))
            lax.fori_loop(1, HEADS, lambda k, c: (plane_copy(k).start(), c)[1], 0)
        if n_full:
            local.append(pltpu.make_async_copy(sources[0].at[mine if by_head else me], targets[0].at[me], local_sem.at[0]))
            lax.fori_loop(1, N_SEQ, lambda k, c: (full_copy(k).start(), c)[1], 0)
        for copy in local:
            copy.start()
        for copy in local:
            copy.wait()
        if n_plane:
            lax.fori_loop(1, HEADS, lambda k, c: (plane_copy(k).wait(), c)[1], 0)
        if n_full:
            lax.fori_loop(1, N_SEQ, lambda k, c: (full_copy(k).wait(), c)[1], 0)

    arrays, outs = [], []
    if n_full:
        arrays.append(full)
        outs.append(jax.ShapeDtypeStruct((N_SEQ, TOK, 128), BF))
    if n_plane:
        arrays.append(plane)
        outs.append(jax.ShapeDtypeStruct((HEADS, TOK, 128), BF))
    return pl.pallas_call(
        body,
        out_shape=outs,
        in_specs=[ANY] * len(arrays),
        out_specs=[ANY] * len(outs),
        scratch_shapes=[
            pltpu.SemaphoreType.DMA((N_SEQ,)),
            pltpu.SemaphoreType.DMA((N_SEQ,)),
            pltpu.SemaphoreType.DMA((HEADS,)),
            pltpu.SemaphoreType.DMA((HEADS,)),
            pltpu.SemaphoreType.DMA((2,)),
        ],
        compiler_params=pltpu.CompilerParams(collective_id=identity, has_side_effects=True),
        name=name,
    )(*arrays)


def sums_body(terms, out_term, rows, sums, out_sum, moved, parts, out_parts,
              send, recv, out_send, out_recv, local_sem, carry_sem):
    me = lax.axis_index("seq")
    section = lax.axis_index("section")
    before, after = lax.rem(section + 3, 4), lax.rem(section + 1, 4)
    across = N_SEQ - 1 - me
    barrier = pltpu.get_barrier_semaphore()

    def greet(k, _):
        pl.semaphore_signal(barrier, inc=1, device_id={"seq": lax.rem(me + k, N_SEQ)}, device_id_type=MESH)
        return 0

    lax.fori_loop(1, N_SEQ, greet, 0)
    for other in (before, after):
        pl.semaphore_signal(barrier, inc=1, device_id={"section": other, "seq": across}, device_id_type=MESH)
    pl.semaphore_wait(barrier, N_SEQ + 1)

    carry = pltpu.make_async_remote_copy(
        src_ref=rows, dst_ref=moved, send_sem=carry_sem.at[0], recv_sem=carry_sem.at[1],
        device_id={"section": before, "seq": across}, device_id_type=MESH,
    )
    carry.start()

    def term_copy(k):
        peer = lax.rem(me + k, N_SEQ)
        return pltpu.make_async_remote_copy(
            src_ref=terms.at[pl.ds(pl.multiple_of(peer * 32, 32), 32), :], dst_ref=parts.at[k],
            send_sem=send.at[k], recv_sem=recv.at[k], device_id={"seq": peer}, device_id_type=MESH,
        )

    def out_copy(k):
        peer = lax.rem(me + k, N_SEQ)
        return pltpu.make_async_remote_copy(
            src_ref=out_term.at[pl.ds(pl.multiple_of(peer * 16, 16), 16), :], dst_ref=out_parts.at[k],
            send_sem=out_send.at[k], recv_sem=out_recv.at[k], device_id={"seq": peer}, device_id_type=MESH,
        )

    def begin(k, _):
        term_copy(k).start()
        out_copy(k).start()
        return 0

    lax.fori_loop(1, N_SEQ, begin, 0)
    own = [
        pltpu.make_async_copy(terms.at[pl.ds(pl.multiple_of(me * 32, 32), 32), :], parts.at[0], local_sem.at[0]),
        pltpu.make_async_copy(out_term.at[pl.ds(pl.multiple_of(me * 16, 16), 16), :], out_parts.at[0], local_sem.at[1]),
    ]
    for copy in own:
        copy.start()
    for copy in own:
        copy.wait()
    sums[...] = parts[0].astype(F32)
    out_sum[...] = out_parts[0].astype(F32)

    def add(k, _):
        term_copy(k).wait()
        sums[...] += parts[k].astype(F32)
        out_copy(k).wait()
        out_sum[...] += out_parts[k].astype(F32)
        return 0

    lax.fori_loop(1, N_SEQ, add, 0)
    carry.wait()


def reduce_terms(terms, out_term, rows):
    return pl.pallas_call(
        sums_body,
        out_shape=[
            jax.ShapeDtypeStruct((32, 3 * INNER), F32),
            jax.ShapeDtypeStruct((16, 2 * D), F32),
            jax.ShapeDtypeStruct((TOK, D), BF),
        ],
        in_specs=[ANY, ANY, ANY],
        out_specs=[VMEM, VMEM, ANY],
        scratch_shapes=[
            pltpu.VMEM((N_SEQ, 32, 3 * INNER), BF),
            pltpu.VMEM((N_SEQ, 16, 2 * D), BF),
            pltpu.SemaphoreType.DMA((N_SEQ,)),
            pltpu.SemaphoreType.DMA((N_SEQ,)),
            pltpu.SemaphoreType.DMA((N_SEQ,)),
            pltpu.SemaphoreType.DMA((N_SEQ,)),
            pltpu.SemaphoreType.DMA((2,)),
            pltpu.SemaphoreType.DMA((2,)),
        ],
        compiler_params=pltpu.CompilerParams(
            collective_id=5, has_side_effects=True, vmem_limit_bytes=BIG
        ),
        name="sums",
    )(terms, out_term, rows)


def shards(activations, incoming, w_query, w_key, w_value, w_out, block_ids, flip_order):
    act, up = activations[0], incoming[0]
    wq, wk, wv, wo = w_query[0], w_key[0], w_value[0], w_out[0]
    group = lax.rem(lax.axis_index("seq"), 4)
    by_chunk = block_ids.reshape(HEADS, 4, TOK)
    q_ids = lax.dynamic_index_in_dim(by_chunk, group, 1, keepdims=False)[:, :, None]
    k_ids = block_ids.reshape(TOKENS // KT, 1, KT)

    normed, q_raw, k_raw, q_pack, kv_pack = local_call(
        project_body,
        [((TOK, D), BF), ((TOK, INNER), F32), ((TOK, INNER), F32), ((HEADS, TOK, 128), BF), ((HEADS, TOK, 128), BF)],
        name="project",
    )(act, wq, wk, wv)
    kv_all, q_all = exchange(kv_pack, q_pack, True, 1, "spread")
    kv = kv_all.reshape(TOKENS, 128)
    out, inverse = local_call(
        forward_body, [((HEADS, TOK, 128), BF), ((HEADS, TOK, 128), F32)], name="attend"
    )(q_all, kv, q_ids, k_ids)
    (att_all,) = exchange(None, out, True, 2, "attended")
    g_pack, carry_part, out_term = local_call(
        affine_body,
        [((HEADS, TOK, 128), BF), ((TOK, D), F32), ((INNER, 2 * D), BF)],
        [((TOK, INNER), BF), ((INNER, TOK), BF), ((TOK, 2 * D), BF)],
        name="affine",
    )(act, up, att_all, wo)
    (g_all,) = exchange(None, g_pack, True, 3, "grad_attn")
    dq, dkv = local_call(
        backward_body,
        [((HEADS, TOK, 128), BF), ((TOKENS, 128), BF)],
        [((128, TOKENS), F32)],
        name="attend_back",
    )(q_all, g_all, out, inverse, kv, q_ids, k_ids)
    dkv_parts, dq_all = exchange(dkv.reshape(N_SEQ, TOK, 128), dq, False, 4, "gather_grads")
    grad_input, terms = local_call(
        finish_body,
        [((TOK, D), BF), ((D, 3 * INNER), BF)],
        [((3, TOK, INNER), BF), ((TOK, D), F32), ((D, TOK), BF)],
        name="finish",
    )(act, normed, carry_part, q_raw, k_raw, dq_all, dkv_parts, wq, wk, wv)
    sums, out_sum, moved = reduce_terms(terms, out_term, grad_input)
    carry = jnp.take(moved, flip_order[0], axis=0)
    carry = jnp.where(lax.axis_index("section") == 3, jnp.zeros_like(carry), carry)
    return (
        carry[None],
        sums[None, :, :INNER],
        sums[None, :, INNER : 2 * INNER],
        sums[None, :, 2 * INNER :],
        out_sum[None],
    )


def solution(mesh):
    by_both = P("section", "seq", None)
    by_layer = P("section", None, None)
    in_specs = (by_both, by_both, by_layer, by_layer, by_layer, by_layer, P(), P("section", None))
    return jax.shard_map(shards, mesh=mesh, in_specs=in_specs, out_specs=(by_both,) * 5, check_vma=False)
```

```python
import jax
import jax.numpy as jnp
from jax import lax
from jax.experimental import pallas as pl
from jax.experimental.pallas import tpu as pltpu
from jax.sharding import PartitionSpec as P

HEADS = 8
HEAD_DIM = 64
EPSILON = 1e-06
N_SEQ = 32
TOK = 136
TOKENS = 4352
D = 1024
INNER = 512
KT = 256
WIDE = 512
BF = jnp.bfloat16
F32 = jnp.float32
MESH = pl.DeviceIdType.MESH
VMEM = pl.BlockSpec(memory_space=pltpu.VMEM)
ANY = pl.BlockSpec(memory_space=pl.ANY)
BIG = 60 * 1024 * 1024


def dot(a, b):
    return jnp.dot(a, b, preferred_element_type=F32)


def dot_t(a, b):
    return lax.dot_general(a, b, (((1,), (1,)), ((), ())), preferred_element_type=F32)


def left_half(shape):
    return lax.broadcasted_iota(jnp.int32, shape, 1) < HEAD_DIM


def swap(slab):
    return pltpu.roll(slab, HEAD_DIM, 1)


def per_head_sum(slab, left):
    low = jnp.sum(jnp.where(left, slab, 0.0), axis=-1, keepdims=True)
    high = jnp.sum(jnp.where(left, 0.0, slab), axis=-1, keepdims=True)
    return jnp.where(left, low, high)


def unit_scale(slab, left):
    return lax.rsqrt(per_head_sum(slab * slab, left) * (1.0 / HEAD_DIM) + EPSILON)


def project_body(act, wq, wk, wv, normed, q_raw, k_raw, q_pack, kv_pack):
    field = act[...].astype(F32)
    scale = lax.rsqrt(jnp.mean(field * field, axis=-1, keepdims=True) + EPSILON)
    normed[...] = (field * scale).astype(BF)
    left = left_half((TOK, 128))
    for block in range(2):
        columns = pl.ds(256 * block, 256)
        q = dot(normed[...], wq[:, columns])
        k = dot(normed[...], wk[:, columns])
        v = dot(normed[...], wv[:, columns])
        q_raw[:, columns] = q
        k_raw[:, columns] = k
        for half in range(2):
            head = 4 * block + 2 * half
            q_slab = q[:, 128 * half : 128 * half + 128]
            k_slab = k[:, 128 * half : 128 * half + 128]
            v_slab = v[:, 128 * half : 128 * half + 128]
            q_slab = (q_slab * unit_scale(q_slab, left)).astype(BF).astype(F32) * 0.125
            k_slab = k_slab * unit_scale(k_slab, left)
            q_pack[head] = jnp.where(left, q_slab, 0.0).astype(BF)
            q_pack[head + 1] = jnp.where(left, swap(q_slab), 0.0).astype(BF)
            kv_pack[head] = jnp.where(left, k_slab, swap(v_slab)).astype(BF)
            kv_pack[head + 1] = jnp.where(left, swap(k_slab), v_slab).astype(BF)


def forward_body(q_all, kv, q_ids, k_ids, out, inverse):
    def pair(a, last):
        rows = pl.ds(2 * TOK * a if last else pl.multiple_of(2 * TOK * a, 2 * TOK), 2 * TOK)
        q = q_all[rows, :]

        def tile(j, carry, masked, width=WIDE):
            total, mass = carry
            block = kv[pl.ds(j * WIDE if last and masked else pl.multiple_of(j * WIDE, WIDE), width), :]
            p = jnp.exp(dot_t(q, block))
            if masked:
                p = jnp.where(k_ids[j][:, :width] <= q_ids[rows, :], p, 0.0)
            for part in range(width // 128):
                mass = mass + p[:, 128 * part : 128 * part + 128]
            total = total + dot(p.astype(BF), block)
            return total, mass

        zero = jnp.zeros((2 * TOK, 128), F32)
        carry = lax.fori_loop(0, 2 * a, lambda j, c: tile(j, c, False), (zero, zero))
        carry = tile(2 * a, carry, True)
        carry = tile(2 * a + 1, carry, True)
        total, mass = tile(2 * a + 2, carry, True, WIDE // 2 if last else WIDE)
        one_over = 1.0 / jnp.sum(mass, axis=-1, keepdims=True)
        out[rows, :] = (total * one_over).astype(BF)
        inverse[rows, :] = jnp.broadcast_to(one_over, (2 * TOK, 128))

    lax.fori_loop(0, 3, lambda a, c: (pair(a, False), c)[1], 0)
    pair(3, True)


def backward_body(q_all, g_all, out, inverse, kv, q_ids, k_ids, dq, dkv, total):
    total[...] = jnp.zeros_like(total)

    def pair(a, last):
        rows = pl.ds(2 * TOK * a if last else pl.multiple_of(2 * TOK * a, 2 * TOK), 2 * TOK)
        q = q_all[rows, :]
        g = g_all[rows, :]
        one_over = inverse[rows, :][:, :1]
        correction = jnp.sum(g.astype(F32) * out[rows, :].astype(F32), axis=-1, keepdims=True)
        q_turned = jnp.transpose(q.astype(F32))[:HEAD_DIM].astype(BF)
        g_turned = jnp.transpose(g.astype(F32))[HEAD_DIM:].astype(BF)

        def tile(j, acc, masked, width=WIDE):
            at = pl.ds(j * WIDE if last and masked else pl.multiple_of(j * WIDE, WIDE), width)
            block = kv[at, :]
            p = jnp.exp(dot_t(q, block)) * one_over
            if masked:
                p = jnp.where(k_ids[j][:, :width] <= q_ids[rows, :], p, 0.0)
            ds = (p * (dot_t(g, block) - correction)).astype(BF)
            total[:HEAD_DIM, at] += dot(q_turned, ds)
            total[HEAD_DIM:, at] += dot(g_turned, p.astype(BF))
            return acc + dot(ds, block)

        acc = jnp.zeros((2 * TOK, 128), F32)
        acc = lax.fori_loop(0, 2 * a, lambda j, c: tile(j, c, False), acc)
        acc = tile(2 * a, acc, True)
        acc = tile(2 * a + 1, acc, True)
        acc = tile(2 * a + 2, acc, True, WIDE // 2 if last else WIDE)
        dq[rows, :] = (acc * 0.125).astype(BF)

    lax.fori_loop(0, 3, lambda a, c: (pair(a, False), c)[1], 0)
    pair(3, True)

    def turn(j, _):
        at = pl.ds(pl.multiple_of(j * KT, KT), KT)
        dkv[at, :] = jnp.transpose(total[:, at]).astype(BF)
        return 0

    lax.fori_loop(0, TOKENS // KT, turn, 0)


def place():
    me = lax.axis_index("seq")
    x, z = lax.rem(lax.div(me, 4), 4), lax.rem(me, 4)
    return ring_bits(lax.div(me, 16), x, z)


def ring_bits(y, x, z):
    return (y, lax.rem(lax.div(x + 1, 2), 2), lax.div(x, 2), lax.rem(lax.div(z + 1, 2), 2), lax.div(z, 2))


def neighbours():
    me = lax.axis_index("seq")
    x, z = lax.rem(lax.div(me, 4), 4), lax.rem(me, 4)
    return (
        lax.rem(me + 16, N_SEQ),
        me + 4 * (1 - 2 * lax.rem(x, 2)),
        me + 4 * (3 - 2 * x),
        me + 1 - 2 * lax.rem(z, 2),
        me + 3 - 2 * z,
    )


def slot(stream, owner, bits):
    y, x, z = owner // 16, owner // 4 % 4, owner % 4
    theirs = (y, (x + 1) // 2 % 2, x // 2, (z + 1) // 2 % 2, z // 2)
    at = 0
    for step in range(5):
        split = (stream + step) % 5
        apart = 1 - bits[split] if theirs[split] else bits[split]
        at = at + apart * (16 >> step)
    return at


def affine_body(act, up, att_all, w_out, g_pack, carry_part, out_term, att, att_turned, grad):
    left = left_half((TOK, 128))
    bits = place()
    for pair in range(HEADS // 2):
        low = att_all[2 * pair].astype(F32)
        high = att_all[2 * pair + 1].astype(F32)
        slab = jnp.where(left, swap(low), high)
        att[:, 128 * pair : 128 * pair + 128] = slab.astype(BF)
        att_turned[128 * pair : 128 * pair + 128, :] = jnp.transpose(slab).astype(BF)
    for block in range(4):
        columns = pl.ds(256 * block, 256)
        behind = pl.ds(D + 256 * block, 256)
        shift = dot(att[...], w_out[:, columns])
        factor = jnp.exp(-dot(att[...], w_out[:, behind]))
        upstream = up[:, columns].astype(F32)
        latent = (act[:, columns].astype(F32) - shift) * factor
        scaled = upstream * factor
        carry_part[:, columns] = scaled
        grad[:, columns] = (-scaled).astype(BF)
        grad[:, behind] = (1.0 - upstream * latent).astype(BF)
    for block in range(2):
        g = dot_t(grad[...], w_out[pl.ds(256 * block, 256), :])
        for half in range(2):
            head = 4 * block + 2 * half
            slab = g[:, 128 * half : 128 * half + 128]
            g_pack[head] = jnp.where(left, 0.0, swap(slab)).astype(BF)
            g_pack[head + 1] = jnp.where(left, 0.0, slab).astype(BF)
    for block in range(8):
        columns = pl.ds(256 * block, 256)
        term = dot(att_turned[...], grad[:, columns]).astype(BF)
        stream = block // 4
        for owner in range(N_SEQ):
            at = slot(3 + stream, owner, bits)
            for half in range(2):
                row = 16 * (2 * (block % 4) + half)
                out_term[stream, at, row : row + 16, :] = term[16 * owner : 16 * owner + 16, 128 * half : 128 * half + 128]


def finish_body(act, normed, carry_part, q_raw, k_raw, dq_all, dkv_parts, wq, wk, wv, out_term, flip,
                carry_out, sum_q, sum_k, sum_v, sum_out,
                grads, gn, normed_turned, grad_input, moved, terms, acc, got0, got1, got2, got3, got4,
                send, recv, carry_sem):
    section = lax.axis_index("section")
    across = N_SEQ - 1 - lax.axis_index("seq")
    before, after = lax.rem(section + 3, 4), lax.rem(section + 1, 4)
    near = neighbours()
    bits = place()
    barrier = pltpu.get_barrier_semaphore()
    for peer in near:
        pl.semaphore_signal(barrier, inc=1, device_id={"seq": peer}, device_id_type=MESH)
    for other in (before, after):
        pl.semaphore_signal(barrier, inc=1, device_id={"section": other, "seq": across}, device_id_type=MESH)
    pl.semaphore_wait(barrier, 7)

    got = (got0, got1, got2, got3, got4)

    def hop(stream, step):
        half = 16 >> step
        if step:
            source = acc.at[stream, pl.ds(half, half)]
        else:
            source = terms.at[stream, pl.ds(half, half)] if stream < 3 else out_term.at[stream - 3, pl.ds(half, half)]
        return pltpu.make_async_remote_copy(
            src_ref=source, dst_ref=got[step].at[stream], send_sem=send.at[stream, step],
            recv_sem=recv.at[stream, step], device_id={"seq": near[(stream + step) % 5]}, device_id_type=MESH,
        )

    for stream in (3, 4):
        hop(stream, 0).start()

    left = left_half((TOK, 128))

    def unit_back(grad, raw):
        scale = unit_scale(raw, left)
        unit = raw * scale
        return scale * (grad - unit * (per_head_sum(grad * unit, left) * (1.0 / HEAD_DIM)))

    def keys_of(head):
        part = [dkv_parts[4 * head + i].astype(F32) for i in range(4)]
        return (part[0] + part[1]) + (part[2] + part[3])

    for pair in range(HEADS // 2):
        at = pl.ds(128 * pair, 128)
        low, high = dq_all[2 * pair].astype(F32), dq_all[2 * pair + 1].astype(F32)
        q_grad = jnp.where(left, low, swap(high))
        low, high = keys_of(2 * pair), keys_of(2 * pair + 1)
        k_grad = jnp.where(left, low, swap(high))
        v_grad = jnp.where(left, swap(low), high)
        grads[0, :, at] = unit_back(q_grad, q_raw[:, at]).astype(BF)
        grads[1, :, at] = unit_back(k_grad, k_raw[:, at]).astype(BF)
        grads[2, :, at] = v_grad.astype(BF)
    for block in range(8):
        at = pl.ds(128 * block, 128)
        normed_turned[at, :] = jnp.transpose(normed[:, at].astype(F32)).astype(BF)
    for stream in range(3):
        for block in range(2):
            term = dot(normed_turned[...], grads[stream, :, 256 * block : 256 * block + 256]).astype(BF)
            for owner in range(N_SEQ):
                at = slot(stream, owner, bits)
                for half in range(2):
                    row = 32 * (2 * block + half)
                    terms[stream, at, row : row + 32, :] = term[32 * owner : 32 * owner + 32, 128 * half : 128 * half + 128]
        hop(stream, 0).start()
    for block in range(4):
        at = pl.ds(256 * block, 256)
        gn[:, at] = dot_t(grads[0], wq[at, :]) + dot_t(grads[1], wk[at, :]) + dot_t(grads[2], wv[at, :])
    field = act[...].astype(F32)
    scale = lax.rsqrt(jnp.mean(field * field, axis=-1, keepdims=True) + EPSILON)
    unit = field * scale
    grad_normed = gn[...]
    mean = jnp.mean(grad_normed * unit, axis=-1, keepdims=True)
    grad_input[...] = (carry_part[...] + scale * (grad_normed - unit * mean)).astype(BF)
    carry = pltpu.make_async_remote_copy(
        src_ref=grad_input, dst_ref=moved, send_sem=carry_sem.at[0], recv_sem=carry_sem.at[1],
        device_id={"section": before, "seq": across}, device_id_type=MESH,
    )
    carry.start()

    def add(stream, step, first, count):
        def one(i, _):
            if step:
                mine = acc[stream, i]
            else:
                mine = terms[stream, i] if stream < 3 else out_term[stream - 3, i]
            acc[stream, i] = (mine.astype(F32) + got[step][stream, i].astype(F32)).astype(BF)
            return 0

        lax.fori_loop(first, first + count, one, 0)

    for step in range(4):
        half = 8 >> step
        for stream in (3, 4, 0, 1, 2):
            hop(stream, step).wait_recv()
            add(stream, step, half, half)
            hop(stream, step + 1).start()
            add(stream, step, 0, half)
    for stream in (3, 4, 0, 1, 2):
        hop(stream, 4).wait_recv()
        result = acc[stream, 0].astype(F32) + got4[stream, 0].astype(F32)
        if stream < 3:
            target = (sum_q, sum_k, sum_v)[stream]
            for part in range(4):
                target[:, 128 * part : 128 * part + 128] = result[32 * part : 32 * part + 32]
        else:
            for part in range(8):
                column = 1024 * (stream - 3) + 128 * part
                sum_out[:, column : column + 128] = result[16 * part : 16 * part + 16]
    carry.wait()
    chosen = (flip[...] == lax.broadcasted_iota(jnp.int32, (TOK, TOK), 1)).astype(BF)
    last = (section + jnp.zeros((TOK, 1), jnp.int32)) == 3
    for block in range(4):
        at = pl.ds(256 * block, 256)
        carry_out[:, at] = jnp.where(last, 0.0, dot(chosen, moved[:, at])).astype(BF)
    for step in range(5):
        for stream in range(5):
            hop(stream, step).wait_send()


def finish(*operands):
    return pl.pallas_call(
        finish_body,
        out_shape=[jax.ShapeDtypeStruct((TOK, D), BF)]
        + [jax.ShapeDtypeStruct((32, INNER), F32)] * 3
        + [jax.ShapeDtypeStruct((16, 2 * D), F32)],
        in_specs=[VMEM] * len(operands),
        out_specs=[VMEM] * 5,
        scratch_shapes=[
            pltpu.VMEM((3, TOK, INNER), BF),
            pltpu.VMEM((TOK, D), F32),
            pltpu.VMEM((D, TOK), BF),
            pltpu.VMEM((TOK, D), BF),
            pltpu.VMEM((TOK, D), BF),
            pltpu.VMEM((3, N_SEQ, 128, 128), BF),
            pltpu.VMEM((5, 16, 128, 128), BF),
        ]
        + [pltpu.VMEM((5, 16 >> step, 128, 128), BF) for step in range(5)]
        + [
            pltpu.SemaphoreType.DMA((5, 5)),
            pltpu.SemaphoreType.DMA((5, 5)),
            pltpu.SemaphoreType.DMA((2,)),
        ],
        compiler_params=pltpu.CompilerParams(collective_id=5, has_side_effects=True, vmem_limit_bytes=BIG),
        name="finish",
    )(*operands)


def local_call(body, outs, scratch=(), name=None):
    return pl.pallas_call(
        body,
        out_shape=[jax.ShapeDtypeStruct(shape, dtype) for shape, dtype in outs],
        out_specs=[VMEM] * len(outs),
        scratch_shapes=[pltpu.VMEM(shape, dtype) for shape, dtype in scratch],
        compiler_params=pltpu.CompilerParams(vmem_limit_bytes=BIG),
        name=name,
    )


def exchange(full, plane, by_head, identity, name):
    n_full, n_plane = (0 if full is None else 1), (0 if plane is None else 1)

    def body(*refs):
        refs = list(refs)
        sources = [refs.pop(0) for _ in range(n_full + n_plane)]
        targets = [refs.pop(0) for _ in range(n_full + n_plane)]
        full_send, full_recv, plane_send, plane_recv, local_sem = refs
        me = lax.axis_index("seq")
        mine = lax.div(me, 4)
        count, stride = (N_SEQ, 1) if n_full else (HEADS, 4)

        barrier = pltpu.get_barrier_semaphore()

        def greet(k, _):
            pl.semaphore_signal(barrier, inc=1, device_id={"seq": lax.rem(me + stride * k, N_SEQ)}, device_id_type=MESH)
            return 0

        lax.fori_loop(1, count, greet, 0)
        pl.semaphore_wait(barrier, count - 1)

        def full_copy(k):
            peer = lax.rem(me + k, N_SEQ)
            return pltpu.make_async_remote_copy(
                src_ref=sources[0].at[lax.div(peer, 4) if by_head else peer],
                dst_ref=targets[0].at[me],
                send_sem=full_send.at[k],
                recv_sem=full_recv.at[k],
                device_id={"seq": peer},
                device_id_type=MESH,
            )

        def plane_copy(k):
            peer = lax.rem(me + 4 * k, N_SEQ)
            return pltpu.make_async_remote_copy(
                src_ref=sources[-1].at[lax.div(peer, 4)],
                dst_ref=targets[-1].at[mine],
                send_sem=plane_send.at[k],
                recv_sem=plane_recv.at[k],
                device_id={"seq": peer},
                device_id_type=MESH,
            )

        local = []
        if n_plane:
            local.append(pltpu.make_async_copy(sources[-1].at[mine], targets[-1].at[mine], local_sem.at[1]))
            lax.fori_loop(1, HEADS, lambda k, c: (plane_copy(k).start(), c)[1], 0)
        if n_full:
            local.append(pltpu.make_async_copy(sources[0].at[mine if by_head else me], targets[0].at[me], local_sem.at[0]))
            lax.fori_loop(1, N_SEQ, lambda k, c: (full_copy(k).start(), c)[1], 0)
        for copy in local:
            copy.start()
        for copy in local:
            copy.wait()
        if n_plane:
            lax.fori_loop(1, HEADS, lambda k, c: (plane_copy(k).wait(), c)[1], 0)
        if n_full:
            lax.fori_loop(1, N_SEQ, lambda k, c: (full_copy(k).wait(), c)[1], 0)

    arrays, outs = [], []
    if n_full:
        arrays.append(full)
        outs.append(jax.ShapeDtypeStruct((N_SEQ, TOK, 128), BF))
    if n_plane:
        arrays.append(plane)
        outs.append(jax.ShapeDtypeStruct((HEADS, TOK, 128), BF))
    return pl.pallas_call(
        body,
        out_shape=outs,
        in_specs=[ANY] * len(arrays),
        out_specs=[ANY] * len(outs),
        scratch_shapes=[
            pltpu.SemaphoreType.DMA((N_SEQ,)),
            pltpu.SemaphoreType.DMA((N_SEQ,)),
            pltpu.SemaphoreType.DMA((HEADS,)),
            pltpu.SemaphoreType.DMA((HEADS,)),
            pltpu.SemaphoreType.DMA((2,)),
        ],
        compiler_params=pltpu.CompilerParams(collective_id=identity, has_side_effects=True),
        name=name,
    )(*arrays)


def shards(activations, incoming, w_query, w_key, w_value, w_out, block_ids, flip_order):
    act, up = activations[0], incoming[0]
    wq, wk, wv, wo = w_query[0], w_key[0], w_value[0], w_out[0]
    group = lax.rem(lax.axis_index("seq"), 4)
    by_chunk = block_ids.reshape(HEADS, 4, TOK)
    q_ids = lax.dynamic_index_in_dim(by_chunk, group, 1, keepdims=False).reshape(HEADS * TOK, 1)
    k_ids = jnp.pad(block_ids, (0, 9 * WIDE - TOKENS)).reshape(9, 1, WIDE)

    normed, q_raw, k_raw, q_pack, kv_pack = local_call(
        project_body,
        [((TOK, D), BF), ((TOK, INNER), F32), ((TOK, INNER), F32), ((HEADS, TOK, 128), BF), ((HEADS, TOK, 128), BF)],
        name="project",
    )(act, wq, wk, wv)
    kv_all, q_all = exchange(kv_pack, q_pack, True, 1, "spread")
    kv = kv_all.reshape(TOKENS, 128)
    q_all = q_all.reshape(HEADS * TOK, 128)
    out, inverse = local_call(
        forward_body, [((HEADS * TOK, 128), BF), ((HEADS * TOK, 128), F32)], name="attend"
    )(q_all, kv, q_ids, k_ids)
    (att_all,) = exchange(None, out.reshape(HEADS, TOK, 128), True, 2, "attended")
    g_pack, carry_part, out_term = local_call(
        affine_body,
        [((HEADS, TOK, 128), BF), ((TOK, D), F32), ((2, N_SEQ, 128, 128), BF)],
        [((TOK, INNER), BF), ((INNER, TOK), BF), ((TOK, 2 * D), BF)],
        name="affine",
    )(act, up, att_all, wo)
    (g_all,) = exchange(None, g_pack, True, 3, "grad_attn")
    dq, dkv = local_call(
        backward_body,
        [((HEADS * TOK, 128), BF), ((TOKENS, 128), BF)],
        [((128, TOKENS), F32)],
        name="attend_back",
    )(q_all, g_all.reshape(HEADS * TOK, 128), out, inverse, kv, q_ids, k_ids)
    dkv_parts, dq_all = exchange(
        dkv.reshape(N_SEQ, TOK, 128), dq.reshape(HEADS, TOK, 128), False, 4, "gather_grads"
    )
    carry, sum_q, sum_k, sum_v, sum_out = finish(
        act, normed, carry_part, q_raw, k_raw, dq_all, dkv_parts, wq, wk, wv, out_term, flip_order.reshape(TOK, 1)
    )
    return carry[None], sum_q[None], sum_k[None], sum_v[None], sum_out[None]


def solution(mesh):
    by_both = P("section", "seq", None)
    by_layer = P("section", None, None)
    in_specs = (by_both, by_both, by_layer, by_layer, by_layer, by_layer, P(), P("section", None))
    return jax.shard_map(shards, mesh=mesh, in_specs=in_specs, out_specs=(by_both,) * 5, check_vma=False)
```

```python
import jax
import jax.numpy as jnp
from jax import lax
from jax.experimental import pallas as pl
from jax.experimental.pallas import tpu as pltpu
from jax.sharding import PartitionSpec as P

HEADS = 8
HEAD_DIM = 64
EPSILON = 1e-06
N_SEQ = 32
TOK = 136
TOKENS = 4352
D = 1024
INNER = 512
WIDE = 512
KEYS = 9 * WIDE
NEAR_ROWS = 64
BF = jnp.bfloat16
F32 = jnp.float32
MESH = pl.DeviceIdType.MESH
VMEM = pl.BlockSpec(memory_space=pltpu.VMEM)
ANY = pl.BlockSpec(memory_space=pl.ANY)
BIG = 60 * 1024 * 1024


def dot(a, b):
    return jnp.dot(a, b, preferred_element_type=F32)


def dot_t(a, b):
    return lax.dot_general(a, b, (((1,), (1,)), ((), ())), preferred_element_type=F32)


def left_half(shape):
    return lax.broadcasted_iota(jnp.int32, shape, 1) < HEAD_DIM


def swap(slab):
    return pltpu.roll(slab, HEAD_DIM, 1)


def per_head_sum(slab, left):
    low = jnp.sum(jnp.where(left, slab, 0.0), axis=-1, keepdims=True)
    high = jnp.sum(jnp.where(left, 0.0, slab), axis=-1, keepdims=True)
    return jnp.where(left, low, high)


def unit_scale(slab, left):
    return lax.rsqrt(per_head_sum(slab * slab, left) * (1.0 / HEAD_DIM) + EPSILON)


def place():
    me = lax.axis_index("seq")
    x, z = lax.rem(lax.div(me, 4), 4), lax.rem(me, 4)
    return ring_bits(lax.div(me, 16), x, z)


def ring_bits(y, x, z):
    return (y, lax.rem(lax.div(x + 1, 2), 2), lax.div(x, 2), lax.rem(lax.div(z + 1, 2), 2), lax.div(z, 2))


def neighbours():
    me = lax.axis_index("seq")
    x, z = lax.rem(lax.div(me, 4), 4), lax.rem(me, 4)
    return (
        lax.rem(me + 16, N_SEQ),
        me + 4 * (1 - 2 * lax.rem(x, 2)),
        me + 4 * (3 - 2 * x),
        me + 1 - 2 * lax.rem(z, 2),
        me + 3 - 2 * z,
    )


def spread_out(groups):
    counts = [groups // 5 + (1 if stream < groups % 5 else 0) for stream in range(5)]
    places = [(stream, 16 * row) for stream in range(5) for row in range(counts[stream])]
    return [16 * count for count in counts], places


TERM_ROWS, TERM_PLACES = spread_out(24)
OUT_ROWS, OUT_PLACES = spread_out(16)


def slot(stream, owner, bits):
    y, x, z = owner // 16, owner // 4 % 4, owner % 4
    theirs = (y, (x + 1) // 2 % 2, x // 2, (z + 1) // 2 % 2, z // 2)
    at = 0
    for step in range(5):
        split = (stream + step) % 5
        apart = 1 - bits[split] if theirs[split] else bits[split]
        at = at + apart * (16 >> step)
    return at


class Halving:
    def __init__(self, terms, acc, got, send, recv, near):
        self.terms, self.acc, self.got, self.send, self.recv, self.near = terms, acc, got, send, recv, near

    def hop(self, stream, step):
        half = 16 >> step
        return pltpu.make_async_remote_copy(
            src_ref=(self.acc if step else self.terms)[stream].at[pl.ds(half, half)],
            dst_ref=self.got[stream].at[pl.ds(32 - (32 >> step), half)],
            send_sem=self.send.at[stream, step],
            recv_sem=self.recv.at[stream, step],
            device_id={"seq": self.near[(stream + step) % 5]},
            device_id_type=MESH,
        )

    def add(self, stream, step, first, count):
        mine = (self.acc if step else self.terms)[stream]
        acc, got = self.acc[stream], self.got[stream]
        behind = 32 - (32 >> step)
        width = min(count, 4)

        def one(i, _):
            at = first + width * i
            total = mine[pl.ds(at, width)].astype(F32) + got[pl.ds(behind + at, width)].astype(F32)
            acc[pl.ds(at, width)] = total.astype(BF)
            return 0

        if count == width:
            one(0, 0)
        else:
            lax.fori_loop(0, count // width, one, 0)

    def advance(self, stream, step):
        half = 8 >> step
        self.hop(stream, step).wait_recv()
        self.add(stream, step, half, half)
        self.hop(stream, step + 1).start()
        self.add(stream, step, 0, half)

    def result(self, stream):
        self.hop(stream, 4).wait_recv()
        return self.acc[stream][0].astype(F32) + self.got[stream][30].astype(F32)

    def drain(self):
        for step in range(5):
            for stream in range(5):
                self.hop(stream, step).wait_send()


def halving_scratch(rows):
    return (
        [pltpu.VMEM((N_SEQ, count, 128), BF) for count in rows]
        + [pltpu.VMEM((16, count, 128), BF) for count in rows]
        + [pltpu.VMEM((31, count, 128), BF) for count in rows]
        + [pltpu.SemaphoreType.DMA((5, 5)), pltpu.SemaphoreType.DMA((5, 5))]
    )


def chunk_rows(index):
    return pl.ds(pl.multiple_of(index * TOK, 8), TOK)


def layer_body(*refs):
    refs = list(refs)

    def take(count):
        taken = refs[:count]
        del refs[:count]
        return taken

    act_in, up_in, wq_in, wk_in, wv_in, wo_in, ids = take(7)
    sum_q, sum_k, sum_v, sum_out, moved = take(5)
    act, up, wq, wk, wv, wo = take(6)
    normed, normed_turned, q_raw, k_raw, q_pack, kv_pack = take(6)
    kv, q_all, g_all, q_ids, out, inverse, att_all, att, att_turned, affine_grad, g_pack, carry_part = take(12)
    total, dkv, dq, dkv_parts, dq_all, grads, gn, grad_input = take(8)
    out_refs = take(17)
    term_refs = take(17)
    (load, kv_send, kv_recv, q_send, q_recv, z_send, z_recv, f_send, f_recv, att_send, att_recv,
     g_send, g_recv, dq_send, dq_recv, dkv_send, dkv_recv, local, carry_sem) = refs

    me = lax.axis_index("seq")
    section = lax.axis_index("section")
    mine, group = lax.div(me, 4), lax.rem(me, 4)
    near, bits = neighbours(), place()
    across = N_SEQ - 1 - me
    before, after = lax.rem(section + 3, 4), lax.rem(section + 1, 4)
    z_next, z_back = 4 * mine + lax.rem(group + 1, 4), 4 * mine + lax.rem(group + 3, 4)

    loads = [
        pltpu.make_async_copy(source, target, load.at[i])
        for i, (source, target) in enumerate(
            ((act_in, act), (wq_in, wq), (wk_in, wk), (wv_in, wv), (wo_in, wo), (up_in, up))
        )
    ]
    for copy in loads:
        copy.start()

    barrier = pltpu.get_barrier_semaphore()

    def greet(k, _):
        pl.semaphore_signal(barrier, inc=1, device_id={"seq": lax.rem(me + k, N_SEQ)}, device_id_type=MESH)
        return 0

    lax.fori_loop(1, N_SEQ, greet, 0)
    for other in (before, after):
        pl.semaphore_signal(barrier, inc=1, device_id={"section": other, "seq": across}, device_id_type=MESH)

    def remote(source, target, send, recv, peer):
        return pltpu.make_async_remote_copy(
            src_ref=source, dst_ref=target, send_sem=send, recv_sem=recv,
            device_id={"seq": peer}, device_id_type=MESH,
        )

    def loop(first, end, do):
        def one(k, c):
            do(k)
            return c

        lax.fori_loop(first, end, one, 0)

    left = left_half((TOK, 128))
    out_sum = Halving(out_refs[:5], out_refs[5:10], out_refs[10:15], out_refs[15], out_refs[16], near)
    term_sum = Halving(term_refs[:5], term_refs[5:10], term_refs[10:15], term_refs[15], term_refs[16], near)

    loads[0].wait()
    field = act[...].astype(F32)
    row_scale = lax.rsqrt(jnp.mean(field * field, axis=-1, keepdims=True) + EPSILON)
    normed[...] = (field * row_scale).astype(BF)
    for copy in loads[1:4]:
        copy.wait()
    for block in range(2):
        columns = pl.ds(256 * block, 256)
        q = dot(normed[...], wq[:, columns])
        k = dot(normed[...], wk[:, columns])
        v = dot(normed[...], wv[:, columns])
        q_raw[:, columns] = q
        k_raw[:, columns] = k
        for half in range(2):
            head = 4 * block + 2 * half
            q_slab = q[:, 128 * half : 128 * half + 128]
            k_slab = k[:, 128 * half : 128 * half + 128]
            v_slab = v[:, 128 * half : 128 * half + 128]
            q_slab = (q_slab * unit_scale(q_slab, left)).astype(BF).astype(F32) * 0.125
            k_slab = k_slab * unit_scale(k_slab, left)
            q_pack[head] = jnp.where(left, q_slab, 0.0).astype(BF)
            q_pack[head + 1] = jnp.where(left, swap(q_slab), 0.0).astype(BF)
            kv_pack[head] = jnp.where(left, k_slab, swap(v_slab)).astype(BF)
            kv_pack[head + 1] = jnp.where(left, swap(k_slab), v_slab).astype(BF)
    pl.semaphore_wait(barrier, N_SEQ + 1)

    def kv_copy(k):
        peer = lax.rem(mine + k, HEADS)
        return remote(kv_pack.at[peer], kv.at[chunk_rows(me)], kv_send.at[k], kv_recv.at[k], 4 * peer + group)

    def q_copy(k):
        peer = lax.rem(mine + k, HEADS)
        return remote(q_pack.at[peer], q_all.at[chunk_rows(mine)], q_send.at[k], q_recv.at[k], 4 * peer + group)

    loop(1, HEADS, lambda k: kv_copy(k).start())
    own = [
        pltpu.make_async_copy(kv_pack.at[mine], kv.at[chunk_rows(me)], local.at[0]),
        pltpu.make_async_copy(q_pack.at[mine], q_all.at[chunk_rows(mine)], local.at[1]),
    ]
    for copy in own:
        copy.start()
    loop(1, HEADS, lambda k: q_copy(k).start())
    kv[pl.ds(TOKENS, KEYS - TOKENS), :] = jnp.zeros((KEYS - TOKENS, 128), BF)
    total[...] = jnp.zeros_like(total)
    own[0].wait()

    def row_of(k, place):
        return 4 * lax.rem(mine - k + HEADS, HEADS) + place

    def z_copy(k, way):
        rows = kv.at[chunk_rows(row_of(k, group))]
        return remote(rows, rows, z_send.at[way, k], z_recv.at[way, k], z_back if way else z_next)

    def f_copy(k, way):
        token = row_of(k, lax.rem(group + (1 if way else 3), 4)) * TOK
        if way:
            rows = kv.at[pl.ds(pl.multiple_of(token + NEAR_ROWS, 8), TOK - NEAR_ROWS)]
        else:
            rows = kv.at[pl.ds(pl.multiple_of(token, 8), NEAR_ROWS)]
        return remote(rows, rows, f_send.at[way, k], f_recv.at[way, k], z_back if way else z_next)

    def relay(k):
        for way in range(2):
            z_copy(k, way).start()

    def forward(k):
        for way in range(2):
            z_copy(k, way).wait_recv()
            f_copy(k, way).start()

    relay(0)

    def pipe(k):
        kv_copy(k).wait_recv()
        relay(k)
        forward(k - 1)

    loop(1, HEADS, pipe)

    turned = jnp.transpose(ids[...].astype(F32)).astype(jnp.int32)
    for row in range(TOKENS // 128):
        q_ids[128 * row : 128 * row + 128, :] = turned[:, row : row + 1]
    for block in range(8):
        at = pl.ds(128 * block, 128)
        normed_turned[at, :] = jnp.transpose(normed[:, at].astype(F32)).astype(BF)
    own[1].wait()
    loop(1, HEADS, lambda k: q_copy(k).wait_recv())
    forward(HEADS - 1)

    def landed(k):
        for way in range(2):
            f_copy(k, way).wait_recv()

    loop(0, HEADS, landed)

    def seen(a, j, width):
        columns = []
        for half in range(2):
            first = pl.multiple_of((4 * (2 * a + half) + group) * TOK, 8)
            columns.append(q_ids[pl.ds(first, TOK), :])
        column = jnp.concatenate(columns, axis=0)
        return jnp.concatenate(
            [ids[pl.ds(4 * j + part, 1), :] <= column for part in range(width // 128)], axis=1
        )

    def pair_rows(a):
        return pl.ds(a * 2 * TOK if isinstance(a, int) else pl.multiple_of(a * 2 * TOK, 16), 2 * TOK)

    def tile_at(j, width):
        return pl.ds(j * WIDE if isinstance(j, int) else pl.multiple_of(j * WIDE, WIDE), width)

    def attend(a, last):
        rows = pair_rows(a)
        q = q_all[rows, :]

        def tile(j, carry, masked, width=WIDE):
            summed, mass = carry
            block = kv[tile_at(j, width), :]
            p = jnp.exp(dot_t(q, block))
            if masked:
                p = jnp.where(seen(a, j, width), p, 0.0)
            for part in range(width // 128):
                mass = mass + p[:, 128 * part : 128 * part + 128]
            return summed + dot(p.astype(BF), block), mass

        zero = jnp.zeros((2 * TOK, 128), F32)
        carry = lax.fori_loop(0, 2 * a, lambda j, c: tile(j, c, False), (zero, zero))
        carry = tile(2 * a, carry, True)
        carry = tile(2 * a + 1, carry, True)
        summed, mass = tile(2 * a + 2, carry, True, WIDE // 2 if last else WIDE)
        one_over = 1.0 / jnp.sum(mass, axis=-1, keepdims=True)
        result = (summed * one_over).astype(BF)
        out[rows, :] = result
        inverse[rows, :] = jnp.broadcast_to(one_over, (2 * TOK, 128))
        return result

    def att_copy(chunk):
        k = lax.rem(chunk - mine + HEADS, HEADS)
        return remote(out.at[chunk_rows(chunk)], att_all.at[mine], att_send.at[k], att_recv.at[k], 4 * chunk + group)

    def attend_and_send(a, last):
        attend(a, last)
        for half in range(2):
            chunk = 2 * a + half

            @pl.when(chunk != mine)
            def _():
                att_copy(chunk).start()

            @pl.when(chunk == mine)
            def _():
                pltpu.make_async_copy(out.at[chunk_rows(chunk)], att_all.at[mine], local.at[0]).start()

    loop(0, 3, lambda a: attend_and_send(a, False))
    attend_and_send(3, True)

    loads[4].wait()
    loads[5].wait()
    pltpu.make_async_copy(out.at[chunk_rows(mine)], att_all.at[mine], local.at[0]).wait()

    def att_arrived(k):
        peer = lax.rem(mine + k, HEADS)
        att_copy(peer).wait_recv()

    loop(1, HEADS, att_arrived)
    for pair in range(HEADS // 2):
        low = att_all[2 * pair].astype(F32)
        high = att_all[2 * pair + 1].astype(F32)
        slab = jnp.where(left, swap(low), high)
        att[:, 128 * pair : 128 * pair + 128] = slab.astype(BF)
        att_turned[128 * pair : 128 * pair + 128, :] = jnp.transpose(slab).astype(BF)
    for block in range(4):
        columns = pl.ds(256 * block, 256)
        behind = pl.ds(D + 256 * block, 256)
        shift = dot(att[...], wo[:, columns])
        factor = jnp.exp(-dot(att[...], wo[:, behind]))
        upstream = up[:, columns].astype(F32)
        latent = (act[:, columns].astype(F32) - shift) * factor
        scaled = upstream * factor
        carry_part[:, columns] = scaled
        affine_grad[:, columns] = (-scaled).astype(BF)
        affine_grad[:, behind] = (1.0 - upstream * latent).astype(BF)

    def g_copy(head):
        k = lax.rem(head - mine + HEADS, HEADS)
        return remote(g_pack.at[head], g_all.at[chunk_rows(mine)], g_send.at[k], g_recv.at[k], 4 * head + group)

    def g_own():
        return pltpu.make_async_copy(g_pack.at[mine], g_all.at[chunk_rows(mine)], local.at[1])

    for block in range(2):
        g = dot_t(affine_grad[...], wo[pl.ds(256 * block, 256), :])
        for half in range(2):
            head = 4 * block + 2 * half
            slab = g[:, 128 * half : 128 * half + 128]
            g_pack[head] = jnp.where(left, 0.0, swap(slab)).astype(BF)
            g_pack[head + 1] = jnp.where(left, 0.0, slab).astype(BF)
        for head in range(4 * block, 4 * block + 4):

            @pl.when(mine != head)
            def _():
                g_copy(head).start()

    g_own().start()
    for block in range(8):
        columns = pl.ds(256 * block, 256)
        term = dot(att_turned[...], affine_grad[:, columns]).astype(BF)
        for owner in range(N_SEQ):
            for half in range(2):
                stream, row = OUT_PLACES[2 * block + half]
                out_sum.terms[stream][slot(stream, owner, bits), row : row + 16, :] = term[
                    16 * owner : 16 * owner + 16, 128 * half : 128 * half + 128
                ]
    for stream in range(5):
        out_sum.hop(stream, 0).start()

    g_own().wait()
    loop(1, HEADS, lambda k: g_copy(lax.rem(mine + k, HEADS)).wait_recv())

    def attend_back(a, last):
        rows = pair_rows(a)
        q = q_all[rows, :]
        g = g_all[rows, :]
        one_over = inverse[rows, :][:, :1]
        correction = jnp.sum(g.astype(F32) * out[rows, :].astype(F32), axis=-1, keepdims=True)
        q_turned = jnp.transpose(q.astype(F32))[:HEAD_DIM].astype(BF)
        g_turned = jnp.transpose(g.astype(F32))[HEAD_DIM:].astype(BF)

        def tile(j, acc, masked, width=WIDE):
            at = tile_at(j, width)
            block = kv[at, :]
            p = jnp.exp(dot_t(q, block)) * one_over
            if masked:
                p = jnp.where(seen(a, j, width), p, 0.0)
            ds = (p * (dot_t(g, block) - correction)).astype(BF)
            total[:HEAD_DIM, at] += dot(q_turned, ds)
            total[HEAD_DIM:, at] += dot(g_turned, p.astype(BF))
            return acc + dot(ds, block)

        acc = jnp.zeros((2 * TOK, 128), F32)
        acc = lax.fori_loop(0, 2 * a, lambda j, c: tile(j, c, False), acc)
        acc = tile(2 * a, acc, True)
        acc = tile(2 * a + 1, acc, True)
        acc = tile(2 * a + 2, acc, True, WIDE // 2 if last else WIDE)
        dq[rows, :] = (acc * 0.125).astype(BF)

    def dq_copy(chunk):
        k = lax.rem(chunk - mine + HEADS, HEADS)
        return remote(dq.at[chunk_rows(chunk)], dq_all.at[mine], dq_send.at[k], dq_recv.at[k], 4 * chunk + group)

    def dq_own():
        return pltpu.make_async_copy(dq.at[chunk_rows(mine)], dq_all.at[mine], local.at[2])

    def dkv_copy(owner):
        k = lax.rem(owner - me + N_SEQ, N_SEQ)
        return remote(dkv.at[chunk_rows(owner)], dkv_parts.at[me], dkv_send.at[k], dkv_recv.at[k], owner)

    def dkv_own():
        return pltpu.make_async_copy(dkv.at[chunk_rows(me)], dkv_parts.at[me], local.at[3])

    def send_keys(owner):
        @pl.when(owner != me)
        def _():
            dkv_copy(owner).start()

        @pl.when(owner == me)
        def _():
            dkv_own().start()

    for a in (3, 2, 1, 0):
        attend_back(a, a == 3)
        for half in range(2):
            chunk = 2 * a + half

            @pl.when(chunk != mine)
            def _():
                dq_copy(chunk).start()

            @pl.when(chunk == mine)
            def _():
                dq_own().start()

        first_tile = 2 * a + 1 if a else 0
        end_tile = 2 * a + 3
        for half_tile in range(2 * first_tile, min(2 * end_tile, TOKENS // 256)):
            at = pl.ds(256 * half_tile, 256)
            dkv[at, :] = jnp.transpose(total[:, at]).astype(BF)
        first_owner = -(-WIDE * first_tile // TOK)
        end_owner = min(-(-WIDE * end_tile // TOK), N_SEQ)
        loop(first_owner, end_owner, send_keys)
        for stream in range(5):
            out_sum.advance(stream, 3 - a)

    def unit_back(grad, raw):
        scale = unit_scale(raw, left)
        unit = raw * scale
        return scale * (grad - unit * (per_head_sum(grad * unit, left) * (1.0 / HEAD_DIM)))

    def keys_of(head):
        part = [dkv_parts[4 * head + i].astype(F32) for i in range(4)]
        return (part[0] + part[1]) + (part[2] + part[3])

    def term_of(which):
        for block in range(2):
            term = dot(normed_turned[...], grads[which, :, 256 * block : 256 * block + 256]).astype(BF)
            for owner in range(N_SEQ):
                for part in range(4):
                    slab, half = part // 2, part % 2
                    stream, row = TERM_PLACES[8 * which + 4 * block + 2 * slab + half]
                    top = 32 * owner + 16 * half
                    term_sum.terms[stream][slot(stream, owner, bits), row : row + 16, :] = term[
                        top : top + 16, 128 * slab : 128 * slab + 128
                    ]

    dq_own().wait()
    loop(1, HEADS, lambda k: dq_copy(lax.rem(mine + k, HEADS)).wait_recv())
    for pair in range(HEADS // 2):
        at = pl.ds(128 * pair, 128)
        low, high = dq_all[2 * pair].astype(F32), dq_all[2 * pair + 1].astype(F32)
        grads[0, :, at] = unit_back(jnp.where(left, low, swap(high)), q_raw[:, at]).astype(BF)
    term_of(0)
    term_sum.hop(0, 0).start()
    for block in range(4):
        at = pl.ds(256 * block, 256)
        gn[:, at] = dot_t(grads[0], wq[at, :])
    dkv_own().wait()
    loop(1, N_SEQ, lambda k: dkv_copy(lax.rem(me + k, N_SEQ)).wait_recv())
    for pair in range(HEADS // 2):
        at = pl.ds(128 * pair, 128)
        low, high = keys_of(2 * pair), keys_of(2 * pair + 1)
        grads[1, :, at] = unit_back(jnp.where(left, low, swap(high)), k_raw[:, at]).astype(BF)
        grads[2, :, at] = jnp.where(left, swap(low), high).astype(BF)
    term_of(1)
    term_sum.hop(1, 0).start()
    term_sum.hop(2, 0).start()
    term_of(2)
    term_sum.hop(3, 0).start()
    term_sum.hop(4, 0).start()
    for block in range(4):
        at = pl.ds(256 * block, 256)
        gn[:, at] += dot_t(grads[1], wk[at, :]) + dot_t(grads[2], wv[at, :])
    field = act[...].astype(F32)
    row_scale = lax.rsqrt(jnp.mean(field * field, axis=-1, keepdims=True) + EPSILON)
    unit = field * row_scale
    grad_normed = gn[...]
    mean = jnp.mean(grad_normed * unit, axis=-1, keepdims=True)
    grad_input[...] = (carry_part[...] + row_scale * (grad_normed - unit * mean)).astype(BF)
    carry = pltpu.make_async_remote_copy(
        src_ref=grad_input, dst_ref=moved, send_sem=carry_sem.at[0], recv_sem=carry_sem.at[1],
        device_id={"section": before, "seq": across}, device_id_type=MESH,
    )
    carry.start()
    for stream in range(5):
        result = out_sum.result(stream)
        for part in range(16):
            if OUT_PLACES[part][0] == stream:
                row = OUT_PLACES[part][1]
                sum_out[:, 128 * part : 128 * part + 128] = result[row : row + 16]
    for step in range(4):
        for stream in range(5):
            term_sum.advance(stream, step)
    for stream in range(5):
        result = term_sum.result(stream)
        for part in range(24):
            if TERM_PLACES[part][0] == stream:
                row = TERM_PLACES[part][1]
                target = (sum_q, sum_k, sum_v)[part // 8]
                column, top = 128 * (part % 8 // 2), 16 * (part % 2)
                target[top : top + 16, column : column + 128] = result[row : row + 16]
    carry.wait()

    def left_all(k):
        kv_copy(k).wait_send()
        q_copy(k).wait_send()
        att_copy(lax.rem(mine + k, HEADS)).wait_send()
        g_copy(lax.rem(mine + k, HEADS)).wait_send()
        dq_copy(lax.rem(mine + k, HEADS)).wait_send()

    loop(1, HEADS, left_all)

    def left_z(k):
        for way in range(2):
            z_copy(k, way).wait_send()
            f_copy(k, way).wait_send()

    loop(0, HEADS, left_z)
    loop(1, N_SEQ, lambda k: dkv_copy(lax.rem(me + k, N_SEQ)).wait_send())
    out_sum.drain()
    term_sum.drain()


def whole_layer(*operands):
    eight, full = (HEADS * TOK, 128), (TOK, D)
    scratch = [
        (full, BF), (full, BF), ((D, INNER), BF), ((D, INNER), BF), ((D, INNER), BF), ((INNER, 2 * D), BF),
        (full, BF), ((D, TOK), BF), ((TOK, INNER), F32), ((TOK, INNER), F32), ((HEADS, TOK, 128), BF), ((HEADS, TOK, 128), BF),
        ((KEYS, 128), BF), (eight, BF), (eight, BF), ((TOKENS, 1), jnp.int32), (eight, BF), (eight, F32),
        ((HEADS, TOK, 128), BF), ((TOK, INNER), BF), ((INNER, TOK), BF), ((TOK, 2 * D), BF), ((HEADS, TOK, 128), BF), (full, F32),
        ((128, KEYS), F32), ((KEYS, 128), BF), (eight, BF), ((N_SEQ, TOK, 128), BF), ((HEADS, TOK, 128), BF),
        ((3, TOK, INNER), BF), (full, F32), (full, BF),
    ]
    dma = pltpu.SemaphoreType.DMA
    return pl.pallas_call(
        layer_body,
        out_shape=[jax.ShapeDtypeStruct((32, INNER), F32)] * 3
        + [jax.ShapeDtypeStruct((16, 2 * D), F32), jax.ShapeDtypeStruct((TOK, D), BF)],
        in_specs=[ANY] * 6 + [VMEM],
        out_specs=[VMEM] * 5,
        scratch_shapes=[pltpu.VMEM(shape, dtype) for shape, dtype in scratch]
        + halving_scratch(OUT_ROWS)
        + halving_scratch(TERM_ROWS)
        + [dma((6,)), dma((8,)), dma((8,)), dma((8,)), dma((8,)), dma((2, 8)), dma((2, 8)), dma((2, 8)), dma((2, 8))]
        + [dma((8,)), dma((8,)), dma((8,)), dma((8,)), dma((8,)), dma((8,)), dma((N_SEQ,)), dma((N_SEQ,)), dma((4,)), dma((2,))],
        compiler_params=pltpu.CompilerParams(collective_id=1, has_side_effects=True, vmem_limit_bytes=BIG),
        name="layer",
    )(*operands)


def hand_out_body(sum_q, sum_k, sum_v, sum_out, moved, flip, carry, out_q, out_k, out_v, out_out):
    out_q[...] = sum_q[...]
    out_k[...] = sum_k[...]
    out_v[...] = sum_v[...]
    out_out[...] = sum_out[...]
    turned = (flip[...] == lax.broadcasted_iota(jnp.int32, (TOK, TOK), 0)).astype(F32)
    chosen = jnp.transpose(turned).astype(BF)
    last = (lax.axis_index("section") + jnp.zeros((TOK, 1), jnp.int32)) == 3
    for block in range(4):
        at = pl.ds(256 * block, 256)
        carry[:, at] = jnp.where(last, 0.0, dot(chosen, moved[:, at])).astype(BF)


def hand_out(*operands):
    return pl.pallas_call(
        hand_out_body,
        out_shape=[jax.ShapeDtypeStruct((TOK, D), BF)]
        + [jax.ShapeDtypeStruct((32, INNER), F32)] * 3
        + [jax.ShapeDtypeStruct((16, 2 * D), F32)],
        in_specs=[VMEM] * 6,
        out_specs=[VMEM] * 5,
        name="hand_out",
    )(*operands)


def shards(activations, incoming, w_query, w_key, w_value, w_out, block_ids, flip_order):
    sums = whole_layer(
        activations[0], incoming[0], w_query[0], w_key[0], w_value[0], w_out[0], block_ids.reshape(TOKENS // 128, 128)
    )
    results = hand_out(*sums, flip_order)
    return tuple(result[None] for result in results)


def solution(mesh):
    by_both = P("section", "seq", None)
    by_layer = P("section", None, None)
    in_specs = (by_both, by_both, by_layer, by_layer, by_layer, by_layer, P(), P("section", None))
    return jax.shard_map(shards, mesh=mesh, in_specs=in_specs, out_specs=(by_both,) * 5, check_vma=False)
```

```python
import jax
import jax.numpy as jnp
from jax import lax
from jax.experimental import pallas as pl
from jax.experimental.pallas import tpu as pltpu
from jax.sharding import PartitionSpec as P

HEADS = 8
HEAD_DIM = 64
EPSILON = 1e-06
N_SEQ = 32
TOK = 136
TOKENS = 4352
D = 1024
INNER = 512
CLASS = 8 * TOK
CLASS_ROWS = 1152
HALF = CLASS // 2
BF = jnp.bfloat16
F32 = jnp.float32
MESH = pl.DeviceIdType.MESH
VMEM = pl.BlockSpec(memory_space=pltpu.VMEM)
ANY = pl.BlockSpec(memory_space=pl.ANY)
BIG = 60 * 1024 * 1024


def dot(a, b):
    return jnp.dot(a, b, preferred_element_type=F32)


def dot_t(a, b):
    return lax.dot_general(a, b, (((1,), (1,)), ((), ())), preferred_element_type=F32)


def left_half(shape):
    return lax.broadcasted_iota(jnp.int32, shape, 1) < HEAD_DIM


def swap(slab):
    return pltpu.roll(slab, HEAD_DIM, 1)


def per_head_sum(slab, left):
    low = jnp.sum(jnp.where(left, slab, 0.0), axis=-1, keepdims=True)
    high = jnp.sum(jnp.where(left, 0.0, slab), axis=-1, keepdims=True)
    return jnp.where(left, low, high)


def unit_scale(slab, left):
    return lax.rsqrt(per_head_sum(slab * slab, left) * (1.0 / HEAD_DIM) + EPSILON)


def place():
    me = lax.axis_index("seq")
    x, z = lax.rem(lax.div(me, 4), 4), lax.rem(me, 4)
    return ring_bits(lax.div(me, 16), x, z)


def ring_bits(y, x, z):
    return (y, lax.rem(lax.div(x + 1, 2), 2), lax.div(x, 2), lax.rem(lax.div(z + 1, 2), 2), lax.div(z, 2))


def neighbours():
    me = lax.axis_index("seq")
    x, z = lax.rem(lax.div(me, 4), 4), lax.rem(me, 4)
    return (
        lax.rem(me + 16, N_SEQ),
        me + 4 * (1 - 2 * lax.rem(x, 2)),
        me + 4 * (3 - 2 * x),
        me + 1 - 2 * lax.rem(z, 2),
        me + 3 - 2 * z,
    )


def spread_out(groups):
    counts = [groups // 5 + (1 if stream < groups % 5 else 0) for stream in range(5)]
    places = [(stream, 16 * row) for stream in range(5) for row in range(counts[stream])]
    return [16 * count for count in counts], places


TERM_ROWS, TERM_PLACES = spread_out(24)
OUT_ROWS, OUT_PLACES = spread_out(16)


def slot(stream, owner, bits):
    y, x, z = owner // 16, owner // 4 % 4, owner % 4
    theirs = (y, (x + 1) // 2 % 2, x // 2, (z + 1) // 2 % 2, z // 2)
    at = 0
    for step in range(5):
        split = (stream + step) % 5
        apart = 1 - bits[split] if theirs[split] else bits[split]
        at = at + apart * (16 >> step)
    return at


class Halving:
    def __init__(self, terms, acc, got, send, recv, near):
        self.terms, self.acc, self.got, self.send, self.recv, self.near = terms, acc, got, send, recv, near

    def hop(self, stream, step):
        half = 16 >> step
        return pltpu.make_async_remote_copy(
            src_ref=(self.acc if step else self.terms)[stream].at[pl.ds(half, half)],
            dst_ref=self.got[stream].at[pl.ds(32 - (32 >> step), half)],
            send_sem=self.send.at[stream, step],
            recv_sem=self.recv.at[stream, step],
            device_id={"seq": self.near[(stream + step) % 5]},
            device_id_type=MESH,
        )

    def add(self, stream, step, first, count):
        mine = (self.acc if step else self.terms)[stream]
        acc, got = self.acc[stream], self.got[stream]
        behind = 32 - (32 >> step)
        width = min(count, 4)

        def one(i, _):
            at = first + width * i
            total = mine[pl.ds(at, width)].astype(F32) + got[pl.ds(behind + at, width)].astype(F32)
            acc[pl.ds(at, width)] = total.astype(BF)
            return 0

        if count == width:
            one(0, 0)
        else:
            lax.fori_loop(0, count // width, one, 0)

    def advance(self, stream, step):
        half = 8 >> step
        self.hop(stream, step).wait_recv()
        self.add(stream, step, half, half)
        self.hop(stream, step + 1).start()
        self.add(stream, step, 0, half)

    def result(self, stream):
        self.hop(stream, 4).wait_recv()
        return self.acc[stream][0].astype(F32) + self.got[stream][30].astype(F32)

    def drain(self):
        for step in range(5):
            for stream in range(5):
                self.hop(stream, step).wait_send()


def halving_scratch(rows):
    return (
        [pltpu.VMEM((N_SEQ, count, 128), BF) for count in rows]
        + [pltpu.VMEM((16, count, 128), BF) for count in rows]
        + [pltpu.VMEM((31, count, 128), BF) for count in rows]
        + [pltpu.SemaphoreType.DMA((5, 5)), pltpu.SemaphoreType.DMA((5, 5))]
    )


def chunk_rows(index):
    return pl.ds(pl.multiple_of(index * TOK, 8), TOK)


def layer_body(*refs):
    refs = list(refs)

    def take(count):
        taken = refs[:count]
        del refs[:count]
        return taken

    act_in, up_in, wq_in, wk_in, wv_in, wo_in, ids = take(7)
    sum_q, sum_k, sum_v, sum_out, moved = take(5)
    act, up, wq, wk, wv, wo = take(6)
    normed, normed_turned, q_raw, k_raw, q_pack, kv_pack = take(6)
    kv, q_all, g_all, q_ids, out, inverse, att_all, att, att_turned, affine_grad, g_pack, carry_part = take(12)
    total, dkv, dq, dkv_all, dq_all, grads, gn, grad_input = take(8)
    padded_ids, q_end, tokens, summed, mass, q_turned, g_turned, correction, from_back, from_next = take(10)
    far_half = take(2)
    out_refs = take(17)
    term_refs = take(17)
    (load, kv_send, kv_recv, q_send, q_recv, z_send, z_recv, f_send, f_recv, att_send, att_recv,
     g_send, g_recv, dq_send, dq_recv, dkv_send, dkv_recv, local, carry_sem, back_send, back_recv) = refs

    me = lax.axis_index("seq")
    section = lax.axis_index("section")
    mine, group = lax.div(me, 4), lax.rem(me, 4)
    near, bits = neighbours(), place()
    across = N_SEQ - 1 - me
    before, after = lax.rem(section + 3, 4), lax.rem(section + 1, 4)
    z_next, z_back = 4 * mine + lax.rem(group + 1, 4), 4 * mine + lax.rem(group + 3, 4)

    loads = [
        pltpu.make_async_copy(source, target, load.at[i])
        for i, (source, target) in enumerate(
            ((act_in, act), (wq_in, wq), (wk_in, wk), (wv_in, wv), (wo_in, wo), (up_in, up))
        )
    ]
    for copy in loads:
        copy.start()

    barrier = pltpu.get_barrier_semaphore()

    def greet(k, _):
        pl.semaphore_signal(barrier, inc=1, device_id={"seq": lax.rem(me + k, N_SEQ)}, device_id_type=MESH)
        return 0

    lax.fori_loop(1, N_SEQ, greet, 0)
    for other in (before, after):
        pl.semaphore_signal(barrier, inc=1, device_id={"section": other, "seq": across}, device_id_type=MESH)

    def remote(source, target, send, recv, peer):
        return pltpu.make_async_remote_copy(
            src_ref=source, dst_ref=target, send_sem=send, recv_sem=recv,
            device_id={"seq": peer}, device_id_type=MESH,
        )

    def loop(first, end, do):
        def one(k, c):
            do(k)
            return c

        lax.fori_loop(first, end, one, 0)

    left = left_half((TOK, 128))
    out_sum = Halving(out_refs[:5], out_refs[5:10], out_refs[10:15], out_refs[15], out_refs[16], near)
    term_sum = Halving(term_refs[:5], term_refs[5:10], term_refs[10:15], term_refs[15], term_refs[16], near)

    loads[0].wait()
    field = act[...].astype(F32)
    row_scale = lax.rsqrt(jnp.mean(field * field, axis=-1, keepdims=True) + EPSILON)
    normed[...] = (field * row_scale).astype(BF)
    for copy in loads[1:4]:
        copy.wait()
    for block in range(2):
        columns = pl.ds(256 * block, 256)
        q = dot(normed[...], wq[:, columns])
        k = dot(normed[...], wk[:, columns])
        v = dot(normed[...], wv[:, columns])
        q_raw[:, columns] = q
        k_raw[:, columns] = k
        for half in range(2):
            head = 4 * block + 2 * half
            q_slab = q[:, 128 * half : 128 * half + 128]
            k_slab = k[:, 128 * half : 128 * half + 128]
            v_slab = v[:, 128 * half : 128 * half + 128]
            q_slab = (q_slab * unit_scale(q_slab, left)).astype(BF).astype(F32) * 0.125
            k_slab = k_slab * unit_scale(k_slab, left)
            q_pack[head] = jnp.where(left, q_slab, 0.0).astype(BF)
            q_pack[head + 1] = jnp.where(left, swap(q_slab), 0.0).astype(BF)
            kv_pack[head] = jnp.where(left, k_slab, swap(v_slab)).astype(BF)
            kv_pack[head + 1] = jnp.where(left, swap(k_slab), v_slab).astype(BF)
    pl.semaphore_wait(barrier, N_SEQ + 1)

    def kv_copy(k):
        peer = lax.rem(mine + k, HEADS)
        return remote(kv_pack.at[peer], kv.at[0, chunk_rows(mine)], kv_send.at[k], kv_recv.at[k], 4 * peer + group)

    def q_copy(k):
        peer = lax.rem(mine + k, HEADS)
        return remote(q_pack.at[peer], q_all.at[chunk_rows(mine)], q_send.at[k], q_recv.at[k], 4 * peer + group)

    loop(1, HEADS, lambda k: kv_copy(k).start())
    own = [
        pltpu.make_async_copy(kv_pack.at[mine], kv.at[0, chunk_rows(mine)], local.at[0]),
        pltpu.make_async_copy(q_pack.at[mine], q_all.at[chunk_rows(mine)], local.at[1]),
    ]
    for copy in own:
        copy.start()
    loop(1, HEADS, lambda k: q_copy(k).start())
    for place_of in range(4):
        kv[place_of, CLASS:, :] = jnp.zeros((CLASS_ROWS - CLASS, 128), BF)
    own[0].wait()

    def z_copy(chunk, way):
        return remote(
            kv.at[0, chunk_rows(chunk)], kv.at[1 + way, chunk_rows(chunk)],
            z_send.at[way, chunk], z_recv.at[way, chunk], z_back if way else z_next,
        )

    def f_copy(chunk, way):
        return remote(
            kv.at[1 + way, chunk_rows(chunk)], kv.at[3, chunk_rows(chunk)],
            f_send.at[chunk], f_recv.at[chunk], z_back if way else z_next,
        )

    def relay(chunk):
        for way in range(2):
            z_copy(chunk, way).start()

    relay(mine)

    def pipe(k):
        kv_copy(k).wait_recv()
        relay(lax.rem(mine - k + HEADS, HEADS))

    loop(1, HEADS, pipe)

    turned = jnp.transpose(ids[...].astype(F32)).astype(jnp.int32)
    for row in range(TOKENS // 128):
        q_ids[128 * row : 128 * row + 128, :] = turned[:, row : row + 1]
    padded_ids[: TOKENS // 128, :] = ids[...]
    padded_ids[TOKENS // 128 :, :] = jnp.full((40 - TOKENS // 128, 128), TOKENS, jnp.int32)
    for chunk in range(HEADS):
        first = pl.multiple_of((4 * chunk + group) * TOK, 8)
        row = lax.div(first, 128)
        column = q_ids[pl.ds(first, TOK), :]
        seen = jnp.zeros((TOK, 128), F32)
        for behind in range(5):
            seen = seen + jnp.where(padded_ids[pl.ds(row + behind, 1), :] <= column, 1.0, 0.0)
        count = jnp.sum(seen, axis=-1, keepdims=True).astype(jnp.int32)
        q_end[TOK * chunk : TOK * chunk + TOK, :] = count + 128 * row
    lane = lax.broadcasted_iota(jnp.int32, (1, CLASS_ROWS), 1)
    skipped = jnp.zeros((1, CLASS_ROWS), jnp.int32)
    for chunk in range(1, HEADS + 1):
        skipped = skipped + jnp.where(lane >= TOK * chunk, 3 * TOK, 0)
    for place_of, apart in enumerate((0, 3, 1, 2)):
        tokens[place_of] = lane + skipped + TOK * lax.rem(group + apart, 4)
    for block in range(8):
        at = pl.ds(128 * block, 128)
        normed_turned[at, :] = jnp.transpose(normed[:, at].astype(F32)).astype(BF)
    own[1].wait()
    loop(1, HEADS, lambda k: q_copy(k).wait_recv())

    def tiles(a):
        whole = [(512 * part, min(512, 256 * a - 512 * part), False) for part in range(-(-a // 2))]
        return whole + [(256 * a, 384 if a == 3 else 512, True)]

    def pair_rows(a):
        return pl.ds(2 * TOK * a, 2 * TOK)

    def shown(a, place_of, first, width):
        return tokens[place_of][:, first : first + width] < q_end[pair_rows(a), :]

    def att_copy(chunk):
        k = lax.rem(chunk - mine + HEADS, HEADS)
        return remote(out.at[chunk_rows(chunk)], att_all.at[mine], att_send.at[k], att_recv.at[k], 4 * chunk + group)

    summed[...] = jnp.zeros_like(summed)
    mass[...] = jnp.zeros_like(mass)

    def attend(place_of):
        @pl.when(place_of == 1)
        def _():
            def pass_on(chunk):
                z_copy(chunk, 0).wait_recv()
                f_copy(chunk, 0).start()
                z_copy(chunk + 4, 1).wait_recv()
                f_copy(chunk + 4, 1).start()

            loop(0, 4, pass_on)
            loop(4, 8, lambda chunk: z_copy(chunk, 0).wait_recv())

        @pl.when(place_of == 2)
        def _():
            loop(0, 4, lambda chunk: z_copy(chunk, 1).wait_recv())

        @pl.when(place_of == 3)
        def _():
            loop(0, 4, lambda chunk: (f_copy(chunk, 0).wait_recv(), f_copy(chunk + 4, 1).wait_recv()))

        for a in range(4):
            rows = pair_rows(a)
            q = q_all[rows, :]
            for first, width, masked in tiles(a):
                block = kv[place_of, first : first + width, :]
                p = jnp.exp(dot_t(q, block))
                if masked:
                    p = jnp.where(shown(a, place_of, first, width), p, 0.0)
                part_mass = p[:, :128]
                for part in range(1, width // 128):
                    part_mass = part_mass + p[:, 128 * part : 128 * part + 128]
                mass[rows, :] += part_mass
                summed[rows, :] += dot(p.astype(BF), block)

            @pl.when(place_of == 3)
            def _():
                one_over = 1.0 / jnp.sum(mass[rows, :], axis=-1, keepdims=True)
                out[rows, :] = (summed[rows, :] * one_over).astype(BF)
                inverse[rows, :] = one_over
                for chunk in (2 * a, 2 * a + 1):

                    @pl.when(mine != chunk)
                    def _():
                        att_copy(chunk).start()

                    @pl.when(mine == chunk)
                    def _():
                        pltpu.make_async_copy(out.at[chunk_rows(chunk)], att_all.at[mine], local.at[0]).start()

    loop(0, 4, attend)

    loads[4].wait()
    loads[5].wait()
    pltpu.make_async_copy(out.at[chunk_rows(mine)], att_all.at[mine], local.at[0]).wait()

    def att_arrived(k):
        peer = lax.rem(mine + k, HEADS)
        att_copy(peer).wait_recv()

    loop(1, HEADS, att_arrived)
    for pair in range(HEADS // 2):
        low = att_all[2 * pair].astype(F32)
        high = att_all[2 * pair + 1].astype(F32)
        slab = jnp.where(left, swap(low), high)
        att[:, 128 * pair : 128 * pair + 128] = slab.astype(BF)
        att_turned[128 * pair : 128 * pair + 128, :] = jnp.transpose(slab).astype(BF)
    for block in range(4):
        columns = pl.ds(256 * block, 256)
        behind = pl.ds(D + 256 * block, 256)
        shift = dot(att[...], wo[:, columns])
        factor = jnp.exp(-dot(att[...], wo[:, behind]))
        upstream = up[:, columns].astype(F32)
        latent = (act[:, columns].astype(F32) - shift) * factor
        scaled = upstream * factor
        carry_part[:, columns] = scaled
        affine_grad[:, columns] = (-scaled).astype(BF)
        affine_grad[:, behind] = (1.0 - upstream * latent).astype(BF)

    def g_copy(head):
        k = lax.rem(head - mine + HEADS, HEADS)
        return remote(g_pack.at[head], g_all.at[chunk_rows(mine)], g_send.at[k], g_recv.at[k], 4 * head + group)

    def g_own():
        return pltpu.make_async_copy(g_pack.at[mine], g_all.at[chunk_rows(mine)], local.at[1])

    for block in range(2):
        g = dot_t(affine_grad[...], wo[pl.ds(256 * block, 256), :])
        for half in range(2):
            head = 4 * block + 2 * half
            slab = g[:, 128 * half : 128 * half + 128]
            g_pack[head] = jnp.where(left, 0.0, swap(slab)).astype(BF)
            g_pack[head + 1] = jnp.where(left, 0.0, slab).astype(BF)
        for head in range(4 * block, 4 * block + 4):

            @pl.when(mine != head)
            def _():
                g_copy(head).start()

    g_own().start()
    for block in range(8):
        columns = pl.ds(256 * block, 256)
        term = dot(att_turned[...], affine_grad[:, columns]).astype(BF)
        for owner in range(N_SEQ):
            for half in range(2):
                stream, row = OUT_PLACES[2 * block + half]
                out_sum.terms[stream][slot(stream, owner, bits), row : row + 16, :] = term[
                    16 * owner : 16 * owner + 16, 128 * half : 128 * half + 128
                ]
    for stream in range(5):
        out_sum.hop(stream, 0).start()

    g_own().wait()
    loop(1, HEADS, lambda k: g_copy(lax.rem(mine + k, HEADS)).wait_recv())

    for a in range(4):
        rows = pair_rows(a)
        g = g_all[rows, :].astype(F32)
        correction[rows, :] = jnp.sum(g * out[rows, :].astype(F32), axis=-1, keepdims=True)
        q_turned[a] = jnp.transpose(q_all[rows, :].astype(F32))[:HEAD_DIM].astype(BF)
        g_turned[a] = jnp.transpose(g)[HEAD_DIM:].astype(BF)
    summed[...] = jnp.zeros_like(summed)

    def dq_copy(chunk):
        k = lax.rem(chunk - mine + HEADS, HEADS)
        return remote(dq.at[chunk_rows(chunk)], dq_all.at[mine], dq_send.at[k], dq_recv.at[k], 4 * chunk + group)

    def dq_own():
        return pltpu.make_async_copy(dq.at[chunk_rows(mine)], dq_all.at[mine], local.at[2])

    def far_copy(way):
        rows = pl.ds(HALF * way, HALF)
        return remote(dkv.at[3, rows], far_half[way], back_send.at[way], back_recv.at[way], z_back if way else z_next)

    def class_copy(way):
        if way:
            return remote(dkv.at[1], from_next, back_send.at[2], back_recv.at[2], z_back)
        return remote(dkv.at[2], from_back, back_send.at[3], back_recv.at[3], z_next)

    def dkv_copy(k):
        peer = lax.rem(mine + k, HEADS)
        return remote(dkv.at[0, chunk_rows(peer)], dkv_all.at[mine], dkv_send.at[k], dkv_recv.at[k], 4 * peer + group)

    def dkv_own():
        return pltpu.make_async_copy(dkv.at[0, chunk_rows(mine)], dkv_all.at[mine], local.at[3])

    blocks = [(128 * part, 128) for part in range(8)] + [(1024, CLASS - 1024)]

    def settle(place_of, extra):
        for first, width in blocks:
            value = jnp.transpose(total[:, first : first + 128])[:width]
            for source, low, high in extra:
                begin, end = max(first, low), min(first + width, high)
                if begin == first and end == first + width:
                    value = value + source[first - low : first - low + width, :].astype(F32)
                elif begin < end:
                    inside = source[begin - low : end - low, :].astype(F32)
                    zeros = [jnp.zeros((begin - first, 128), F32), inside, jnp.zeros((first + width - end, 128), F32)]
                    value = value + jnp.concatenate([z for z in zeros if z.shape[0]], axis=0)
            dkv[place_of, first : first + width, :] = value.astype(BF)

    def attend_back(n):
        place_of = 3 - n
        total[...] = jnp.zeros_like(total)
        for a in (3, 2, 1, 0):
            rows = pair_rows(a)
            q = q_all[rows, :]
            g = g_all[rows, :]
            one_over = inverse[rows, :]
            corr = correction[rows, :]
            for first, width, masked in tiles(a):
                block = kv[place_of, first : first + width, :]
                p = jnp.exp(dot_t(q, block)) * one_over
                if masked:
                    p = jnp.where(shown(a, place_of, first, width), p, 0.0)
                ds = (p * (dot_t(g, block) - corr)).astype(BF)
                total[:HEAD_DIM, first : first + width] += dot(q_turned[a], ds)
                total[HEAD_DIM:, first : first + width] += dot(g_turned[a], p.astype(BF))
                summed[rows, :] += dot(ds, block)

            @pl.when(n == 3)
            def _():
                dq[rows, :] = (summed[rows, :] * 0.125).astype(BF)
                for chunk in (2 * a, 2 * a + 1):

                    @pl.when(mine != chunk)
                    def _():
                        dq_copy(chunk).start()

                    @pl.when(mine == chunk)
                    def _():
                        dq_own().start()

        @pl.when(n == 0)
        def _():
            settle(3, [])
            for way in range(2):
                far_copy(way).start()

        @pl.when(n == 1)
        def _():
            far_copy(0).wait_recv()
            settle(2, [(far_half[0], 0, HALF)])
            class_copy(0).start()

        @pl.when(n == 2)
        def _():
            far_copy(1).wait_recv()
            settle(1, [(far_half[1], HALF, CLASS)])
            class_copy(1).start()

        @pl.when(n == 3)
        def _():
            for way in range(2):
                class_copy(way).wait_recv()
            settle(0, [(from_back, 0, CLASS), (from_next, 0, CLASS)])
            loop(1, HEADS, lambda k: dkv_copy(k).start())
            dkv_own().start()

        for step in range(4):

            @pl.when(n == step)
            def _():
                for stream in range(5):
                    out_sum.advance(stream, step)

    loop(0, 4, attend_back)

    def unit_back(grad, raw):
        scale = unit_scale(raw, left)
        unit = raw * scale
        return scale * (grad - unit * (per_head_sum(grad * unit, left) * (1.0 / HEAD_DIM)))

    def keys_of(head):
        return dkv_all[head].astype(F32)

    def term_of(which):
        for block in range(2):
            term = dot(normed_turned[...], grads[which, :, 256 * block : 256 * block + 256]).astype(BF)
            for owner in range(N_SEQ):
                for part in range(4):
                    slab, half = part // 2, part % 2
                    stream, row = TERM_PLACES[8 * which + 4 * block + 2 * slab + half]
                    top = 32 * owner + 16 * half
                    term_sum.terms[stream][slot(stream, owner, bits), row : row + 16, :] = term[
                        top : top + 16, 128 * slab : 128 * slab + 128
                    ]

    dq_own().wait()
    loop(1, HEADS, lambda k: dq_copy(lax.rem(mine + k, HEADS)).wait_recv())
    for pair in range(HEADS // 2):
        at = pl.ds(128 * pair, 128)
        low, high = dq_all[2 * pair].astype(F32), dq_all[2 * pair + 1].astype(F32)
        grads[0, :, at] = unit_back(jnp.where(left, low, swap(high)), q_raw[:, at]).astype(BF)
    term_of(0)
    term_sum.hop(0, 0).start()
    for block in range(4):
        at = pl.ds(256 * block, 256)
        gn[:, at] = dot_t(grads[0], wq[at, :])
    dkv_own().wait()
    loop(1, HEADS, lambda k: dkv_copy(k).wait_recv())
    for pair in range(HEADS // 2):
        at = pl.ds(128 * pair, 128)
        low, high = keys_of(2 * pair), keys_of(2 * pair + 1)
        grads[1, :, at] = unit_back(jnp.where(left, low, swap(high)), k_raw[:, at]).astype(BF)
        grads[2, :, at] = jnp.where(left, swap(low), high).astype(BF)
    term_of(1)
    term_sum.hop(1, 0).start()
    term_sum.hop(2, 0).start()
    term_of(2)
    term_sum.hop(3, 0).start()
    term_sum.hop(4, 0).start()
    for block in range(4):
        at = pl.ds(256 * block, 256)
        gn[:, at] += dot_t(grads[1], wk[at, :]) + dot_t(grads[2], wv[at, :])
    field = act[...].astype(F32)
    row_scale = lax.rsqrt(jnp.mean(field * field, axis=-1, keepdims=True) + EPSILON)
    unit = field * row_scale
    grad_normed = gn[...]
    mean = jnp.mean(grad_normed * unit, axis=-1, keepdims=True)
    grad_input[...] = (carry_part[...] + row_scale * (grad_normed - unit * mean)).astype(BF)
    carry = pltpu.make_async_remote_copy(
        src_ref=grad_input, dst_ref=moved, send_sem=carry_sem.at[0], recv_sem=carry_sem.at[1],
        device_id={"section": before, "seq": across}, device_id_type=MESH,
    )
    carry.start()
    for stream in range(5):
        result = out_sum.result(stream)
        for part in range(16):
            if OUT_PLACES[part][0] == stream:
                row = OUT_PLACES[part][1]
                sum_out[:, 128 * part : 128 * part + 128] = result[row : row + 16]
    for step in range(4):
        for stream in range(5):
            term_sum.advance(stream, step)
    for stream in range(5):
        result = term_sum.result(stream)
        for part in range(24):
            if TERM_PLACES[part][0] == stream:
                row = TERM_PLACES[part][1]
                target = (sum_q, sum_k, sum_v)[part // 8]
                column, top = 128 * (part % 8 // 2), 16 * (part % 2)
                target[top : top + 16, column : column + 128] = result[row : row + 16]
    carry.wait()

    def left_all(k):
        kv_copy(k).wait_send()
        q_copy(k).wait_send()
        att_copy(lax.rem(mine + k, HEADS)).wait_send()
        g_copy(lax.rem(mine + k, HEADS)).wait_send()
        dq_copy(lax.rem(mine + k, HEADS)).wait_send()
        dkv_copy(k).wait_send()

    loop(1, HEADS, left_all)

    def left_z(chunk):
        for way in range(2):
            z_copy(chunk, way).wait_send()

    loop(0, HEADS, left_z)
    loop(0, 4, lambda chunk: (f_copy(chunk, 0).wait_send(), f_copy(chunk + 4, 1).wait_send()))
    for way in range(2):
        far_copy(way).wait_send()
        class_copy(way).wait_send()
    out_sum.drain()
    term_sum.drain()


def whole_layer(*operands):
    eight, full = (HEADS * TOK, 128), (TOK, D)
    scratch = [
        (full, BF), (full, BF), ((D, INNER), BF), ((D, INNER), BF), ((D, INNER), BF), ((INNER, 2 * D), BF),
        (full, BF), ((D, TOK), BF), ((TOK, INNER), F32), ((TOK, INNER), F32), ((HEADS, TOK, 128), BF), ((HEADS, TOK, 128), BF),
        ((4, CLASS_ROWS, 128), BF), (eight, BF), (eight, BF), ((TOKENS, 1), jnp.int32), (eight, BF), ((CLASS, 1), F32),
        ((HEADS, TOK, 128), BF), ((TOK, INNER), BF), ((INNER, TOK), BF), ((TOK, 2 * D), BF), ((HEADS, TOK, 128), BF), (full, F32),
        ((128, CLASS_ROWS), F32), ((4, CLASS, 128), BF), (eight, BF), ((HEADS, TOK, 128), BF), ((HEADS, TOK, 128), BF),
        ((3, TOK, INNER), BF), (full, F32), (full, BF),
        ((40, 128), jnp.int32), ((CLASS, 1), jnp.int32), ((4, 1, CLASS_ROWS), jnp.int32), (eight, F32), (eight, F32),
        ((4, HEAD_DIM, 2 * TOK), BF), ((4, HEAD_DIM, 2 * TOK), BF), ((CLASS, 1), F32), (eight, BF), (eight, BF),
        ((HALF, 128), BF), ((HALF, 128), BF),
    ]
    dma = pltpu.SemaphoreType.DMA
    return pl.pallas_call(
        layer_body,
        out_shape=[jax.ShapeDtypeStruct((32, INNER), F32)] * 3
        + [jax.ShapeDtypeStruct((16, 2 * D), F32), jax.ShapeDtypeStruct((TOK, D), BF)],
        in_specs=[ANY] * 6 + [VMEM],
        out_specs=[VMEM] * 5,
        scratch_shapes=[pltpu.VMEM(shape, dtype) for shape, dtype in scratch]
        + halving_scratch(OUT_ROWS)
        + halving_scratch(TERM_ROWS)
        + [dma((6,)), dma((8,)), dma((8,)), dma((8,)), dma((8,)), dma((2, 8)), dma((2, 8)), dma((8,)), dma((8,))]
        + [dma((8,))] * 8
        + [dma((4,)), dma((2,)), dma((4,)), dma((4,))],
        compiler_params=pltpu.CompilerParams(collective_id=1, has_side_effects=True, vmem_limit_bytes=BIG),
        name="layer",
    )(*operands)


def hand_out_body(sum_q, sum_k, sum_v, sum_out, moved, flip, carry, out_q, out_k, out_v, out_out):
    out_q[...] = sum_q[...]
    out_k[...] = sum_k[...]
    out_v[...] = sum_v[...]
    out_out[...] = sum_out[...]
    turned = (flip[...] == lax.broadcasted_iota(jnp.int32, (TOK, TOK), 0)).astype(F32)
    chosen = jnp.transpose(turned).astype(BF)
    last = (lax.axis_index("section") + jnp.zeros((TOK, 1), jnp.int32)) == 3
    for block in range(4):
        at = pl.ds(256 * block, 256)
        carry[:, at] = jnp.where(last, 0.0, dot(chosen, moved[:, at])).astype(BF)


def hand_out(*operands):
    return pl.pallas_call(
        hand_out_body,
        out_shape=[jax.ShapeDtypeStruct((TOK, D), BF)]
        + [jax.ShapeDtypeStruct((32, INNER), F32)] * 3
        + [jax.ShapeDtypeStruct((16, 2 * D), F32)],
        in_specs=[VMEM] * 6,
        out_specs=[VMEM] * 5,
        name="hand_out",
    )(*operands)


def shards(activations, incoming, w_query, w_key, w_value, w_out, block_ids, flip_order):
    sums = whole_layer(
        activations[0], incoming[0], w_query[0], w_key[0], w_value[0], w_out[0], block_ids.reshape(TOKENS // 128, 128)
    )
    results = hand_out(*sums, flip_order)
    return tuple(result[None] for result in results)


def solution(mesh):
    by_both = P("section", "seq", None)
    by_layer = P("section", None, None)
    in_specs = (by_both, by_both, by_layer, by_layer, by_layer, by_layer, P(), P("section", None))
    return jax.shard_map(shards, mesh=mesh, in_specs=in_specs, out_specs=(by_both,) * 5, check_vma=False)
```

```python
import jax
import jax.numpy as jnp
from jax import lax
from jax.experimental import pallas as pl
from jax.experimental.pallas import tpu as pltpu
from jax.sharding import PartitionSpec as P

HEADS = 8
HEAD_DIM = 64
EPSILON = 1e-06
N_SEQ = 32
TOK = 136
TOKENS = 4352
D = 1024
INNER = 512
CLASS = 8 * TOK
CLASS_ROWS = 1152
LOW = 512
LONG = 80
BF = jnp.bfloat16
F32 = jnp.float32
MESH = pl.DeviceIdType.MESH
VMEM = pl.BlockSpec(memory_space=pltpu.VMEM)
ANY = pl.BlockSpec(memory_space=pl.ANY)
BIG = 60 * 1024 * 1024


def dot(a, b):
    return jnp.dot(a, b, preferred_element_type=F32)


def dot_t(a, b):
    return lax.dot_general(a, b, (((1,), (1,)), ((), ())), preferred_element_type=F32)


def left_half(shape):
    return lax.broadcasted_iota(jnp.int32, shape, 1) < HEAD_DIM


def swap(slab):
    return pltpu.roll(slab, HEAD_DIM, 1)


def per_head_sum(slab, left):
    low = jnp.sum(jnp.where(left, slab, 0.0), axis=-1, keepdims=True)
    high = jnp.sum(jnp.where(left, 0.0, slab), axis=-1, keepdims=True)
    return jnp.where(left, low, high)


def packed(near, far, left):
    rest = jnp.concatenate([far[LONG:], jnp.zeros((2 * LONG - TOK, 128), F32)], axis=0)
    return jnp.where(left[:LONG], near[:LONG], rest).astype(BF)


def unpacked_pair(low, high, left):
    low, high = low.astype(F32), high.astype(F32)
    top = jnp.where(left[:LONG], low, swap(high))
    rest = jnp.where(left[:LONG], swap(low), high)[: TOK - LONG]
    return jnp.concatenate([top, rest], axis=0)


def unit_scale(slab, left):
    return lax.rsqrt(per_head_sum(slab * slab, left) * (1.0 / HEAD_DIM) + EPSILON)


def place():
    me = lax.axis_index("seq")
    x, z = lax.rem(lax.div(me, 4), 4), lax.rem(me, 4)
    return ring_bits(lax.div(me, 16), x, z)


def ring_bits(y, x, z):
    return (y, lax.rem(lax.div(x + 1, 2), 2), lax.div(x, 2), lax.rem(lax.div(z + 1, 2), 2), lax.div(z, 2))


def neighbours():
    me = lax.axis_index("seq")
    x, z = lax.rem(lax.div(me, 4), 4), lax.rem(me, 4)
    return (
        lax.rem(me + 16, N_SEQ),
        me + 4 * (1 - 2 * lax.rem(x, 2)),
        me + 4 * (3 - 2 * x),
        me + 1 - 2 * lax.rem(z, 2),
        me + 3 - 2 * z,
    )


ALL_LINKS = tuple(tuple((first + step) % 5 for step in range(5)) for first in range(5))
FLAT_FIRST = ((0, 1, 2, 3, 4), (1, 2, 0, 4, 3), (2, 0, 1, 3, 4))


def spread_out(groups, orders):
    streams = len(orders)
    counts = [groups // streams + (1 if stream < groups % streams else 0) for stream in range(streams)]
    places = [(stream, 16 * row) for stream in range(streams) for row in range(counts[stream])]
    return [16 * count for count in counts], places


Q_ROWS, Q_PLACES = spread_out(8, ALL_LINKS)
KV_ROWS, KV_PLACES = spread_out(16, ALL_LINKS)
OUT_ROWS, OUT_PLACES = spread_out(16, FLAT_FIRST)


def slot(order, owner, bits):
    y, x, z = owner // 16, owner // 4 % 4, owner % 4
    theirs = (y, (x + 1) // 2 % 2, x // 2, (z + 1) // 2 % 2, z // 2)
    at = 0
    for step, split in enumerate(order):
        apart = 1 - bits[split] if theirs[split] else bits[split]
        at = at + apart * (16 >> step)
    return at


class Halving:
    def __init__(self, refs, orders, near):
        count = len(orders)
        self.terms, self.acc, self.got = refs[:count], refs[count : 2 * count], refs[2 * count : 3 * count]
        self.send, self.recv = refs[3 * count :]
        self.orders, self.near, self.streams = orders, near, range(count)

    def hop(self, stream, step, part):
        half = 16 >> step
        first, size = (half // 2 * (1 - part), half // 2) if step < 4 else (0, 1)
        return pltpu.make_async_remote_copy(
            src_ref=(self.acc if step else self.terms)[stream].at[pl.ds(half + first, size)],
            dst_ref=self.got[stream].at[pl.ds(32 - (32 >> step) + first, size)],
            send_sem=self.send.at[stream, step, part],
            recv_sem=self.recv.at[stream, step, part],
            device_id={"seq": self.near[self.orders[stream][step]]},
            device_id_type=MESH,
        )

    def start(self, stream, step):
        for part in range(2 if step < 4 else 1):
            self.hop(stream, step, part).start()

    def add(self, stream, step, first, count):
        mine = (self.acc if step else self.terms)[stream]
        acc, got = self.acc[stream], self.got[stream]
        behind = 32 - (32 >> step)
        width = min(count, 4)

        def one(i, _):
            at = first + width * i
            total = mine[pl.ds(at, width)].astype(F32) + got[pl.ds(behind + at, width)].astype(F32)
            acc[pl.ds(at, width)] = total.astype(BF)
            return 0

        if count == width:
            one(0, 0)
        else:
            lax.fori_loop(0, count // width, one, 0)

    def advance(self, step):
        half = 8 >> step
        for stream in self.streams:
            self.hop(stream, step, 0).wait_recv()
            self.add(stream, step, half, half)
            self.start(stream, step + 1)
        for stream in self.streams:
            self.hop(stream, step, 1).wait_recv()
            self.add(stream, step, 0, half)

    def result(self, stream):
        self.hop(stream, 4, 0).wait_recv()
        return self.acc[stream][0].astype(F32) + self.got[stream][30].astype(F32)

    def drain(self):
        for step in range(5):
            for stream in self.streams:
                for part in range(2 if step < 4 else 1):
                    self.hop(stream, step, part).wait_send()


def halving_scratch(rows):
    return (
        [pltpu.VMEM((N_SEQ, count, 128), BF) for count in rows]
        + [pltpu.VMEM((16, count, 128), BF) for count in rows]
        + [pltpu.VMEM((31, count, 128), BF) for count in rows]
        + [pltpu.SemaphoreType.DMA((len(rows), 5, 2)), pltpu.SemaphoreType.DMA((len(rows), 5, 2))]
    )


def chunk_rows(index):
    return pl.ds(pl.multiple_of(index * TOK, 8), TOK)


def layer_body(*refs):
    refs = list(refs)

    def take(count):
        taken = refs[:count]
        del refs[:count]
        return taken

    act_in, up_in, wq_in, wk_in, wv_in, wo_in, ids = take(7)
    sum_q, sum_k, sum_v, sum_out, moved = take(5)
    act, up, wq, wk, wv, wo = take(6)
    normed, normed_turned, q_raw, k_raw, q_pack, kv_pack = take(6)
    kv, q_all, g_all, q_ids, out, inverse, att_all, att, att_turned, affine_grad, g_pack, carry_part = take(12)
    total, dkv, dq, dkv_all, dq_all, grads, gn, grad_input = take(8)
    padded_ids, q_end, tokens, summed, mass, q_turned, g_turned, correction, from_back, from_next = take(10)
    far_half = take(2)
    q_in, g_in, out_pack = take(3)
    out_refs, q_refs, kv_refs = take(11), take(17), take(17)
    (load, kv_send, kv_recv, q_send, q_recv, z_send, z_recv, f_send, f_recv, att_send, att_recv,
     g_send, g_recv, dq_send, dq_recv, dkv_send, dkv_recv, local, carry_sem, back_send, back_recv) = refs

    me = lax.axis_index("seq")
    section = lax.axis_index("section")
    mine, group = lax.div(me, 4), lax.rem(me, 4)
    near, bits = neighbours(), place()
    across = N_SEQ - 1 - me
    before, after = lax.rem(section + 3, 4), lax.rem(section + 1, 4)
    z_next, z_back = 4 * mine + lax.rem(group + 1, 4), 4 * mine + lax.rem(group + 3, 4)

    loads = [
        pltpu.make_async_copy(source, target, load.at[i])
        for i, (source, target) in enumerate(
            ((act_in, act), (wq_in, wq), (wk_in, wk), (wv_in, wv), (wo_in, wo), (up_in, up))
        )
    ]
    for copy in loads:
        copy.start()

    barrier = pltpu.get_barrier_semaphore()

    def greet(k, _):
        peer = 4 * lax.rem(mine + k, HEADS) + group
        pl.semaphore_signal(barrier, inc=1, device_id={"seq": peer}, device_id_type=MESH)
        return 0

    lax.fori_loop(1, HEADS, greet, 0)
    for peer in (z_next, z_back):
        pl.semaphore_signal(barrier, inc=1, device_id={"seq": peer}, device_id_type=MESH)
    for other in (before, after):
        pl.semaphore_signal(barrier, inc=1, device_id={"section": other, "seq": across}, device_id_type=MESH)

    def remote(source, target, send, recv, peer):
        return pltpu.make_async_remote_copy(
            src_ref=source, dst_ref=target, send_sem=send, recv_sem=recv,
            device_id={"seq": peer}, device_id_type=MESH,
        )

    def loop(first, end, do):
        def one(k, c):
            do(k)
            return c

        lax.fori_loop(first, end, one, 0)

    left = left_half((TOK, 128))
    out_sum = Halving(out_refs, FLAT_FIRST, near)
    q_sum = Halving(q_refs, ALL_LINKS, near)
    kv_sum = Halving(kv_refs, ALL_LINKS, near)

    loads[0].wait()
    field = act[...].astype(F32)
    row_scale = lax.rsqrt(jnp.mean(field * field, axis=-1, keepdims=True) + EPSILON)
    normed[...] = (field * row_scale).astype(BF)
    for copy in loads[1:4]:
        copy.wait()
    for block in range(2):
        columns = pl.ds(256 * block, 256)
        q = dot(normed[...], wq[:, columns])
        k = dot(normed[...], wk[:, columns])
        v = dot(normed[...], wv[:, columns])
        q_raw[:, columns] = q
        k_raw[:, columns] = k
        for half in range(2):
            head = 4 * block + 2 * half
            q_slab = q[:, 128 * half : 128 * half + 128]
            k_slab = k[:, 128 * half : 128 * half + 128]
            v_slab = v[:, 128 * half : 128 * half + 128]
            q_slab = (q_slab * unit_scale(q_slab, left)).astype(BF).astype(F32) * 0.125
            k_slab = k_slab * unit_scale(k_slab, left)
            q_swap = swap(q_slab)
            q_pack[head] = packed(q_slab, q_swap, left)
            q_pack[head + 1] = packed(q_swap, q_slab, left)
            kv_pack[head] = jnp.where(left, k_slab, swap(v_slab)).astype(BF)
            kv_pack[head + 1] = jnp.where(left, swap(k_slab), v_slab).astype(BF)
    pl.semaphore_wait(barrier, HEADS + 3)

    def kv_copy(k):
        peer = lax.rem(mine + k, HEADS)
        return remote(kv_pack.at[peer], kv.at[0, chunk_rows(mine)], kv_send.at[k], kv_recv.at[k], 4 * peer + group)

    def q_copy(k):
        peer = lax.rem(mine + k, HEADS)
        return remote(q_pack.at[peer], q_in.at[mine], q_send.at[k], q_recv.at[k], 4 * peer + group)

    loop(1, HEADS, lambda k: kv_copy(k).start())
    own = [
        pltpu.make_async_copy(kv_pack.at[mine], kv.at[0, chunk_rows(mine)], local.at[0]),
        pltpu.make_async_copy(q_pack.at[mine], q_in.at[mine], local.at[1]),
    ]
    for copy in own:
        copy.start()
    loop(1, HEADS, lambda k: q_copy(k).start())
    for place_of in range(4):
        kv[place_of, CLASS:, :] = jnp.zeros((CLASS_ROWS - CLASS, 128), BF)
    own[0].wait()

    def z_copy(chunk, way):
        return remote(
            kv.at[0, chunk_rows(chunk)], kv.at[1 + way, chunk_rows(chunk)],
            z_send.at[way, chunk], z_recv.at[way, chunk], z_back if way else z_next,
        )

    def f_copy(chunk, way):
        return remote(
            kv.at[1 + way, chunk_rows(chunk)], kv.at[3, chunk_rows(chunk)],
            f_send.at[chunk], f_recv.at[chunk], z_back if way else z_next,
        )

    def relay(chunk):
        for way in range(2):
            z_copy(chunk, way).start()

    relay(mine)

    def pipe(k):
        kv_copy(k).wait_recv()
        relay(lax.rem(mine - k + HEADS, HEADS))

    loop(1, HEADS, pipe)

    turned = jnp.transpose(ids[...].astype(F32)).astype(jnp.int32)
    for row in range(TOKENS // 128):
        q_ids[128 * row : 128 * row + 128, :] = turned[:, row : row + 1]
    padded_ids[: TOKENS // 128, :] = ids[...]
    padded_ids[TOKENS // 128 :, :] = jnp.full((40 - TOKENS // 128, 128), TOKENS, jnp.int32)
    for chunk in range(HEADS):
        first = pl.multiple_of((4 * chunk + group) * TOK, 8)
        row = lax.div(first, 128)
        column = q_ids[pl.ds(first, TOK), :]
        seen = jnp.zeros((TOK, 128), F32)
        for behind in range(5):
            seen = seen + jnp.where(padded_ids[pl.ds(row + behind, 1), :] <= column, 1.0, 0.0)
        count = jnp.sum(seen, axis=-1, keepdims=True).astype(jnp.int32)
        q_end[TOK * chunk : TOK * chunk + TOK, :] = count + 128 * row
    lane = lax.broadcasted_iota(jnp.int32, (1, CLASS_ROWS), 1)
    skipped = jnp.zeros((1, CLASS_ROWS), jnp.int32)
    for chunk in range(1, HEADS + 1):
        skipped = skipped + jnp.where(lane >= TOK * chunk, 3 * TOK, 0)
    for place_of, apart in enumerate((0, 3, 1, 2)):
        tokens[place_of] = lane + skipped + TOK * lax.rem(group + apart, 4)
    for block in range(8):
        at = pl.ds(128 * block, 128)
        normed_turned[at, :] = jnp.transpose(normed[:, at].astype(F32)).astype(BF)
    own[1].wait()
    loop(1, HEADS, lambda k: q_copy(k).wait_recv())
    short = left[:LONG]
    for a in range(4):
        parts = []
        for chunk in (2 * a, 2 * a + 1):
            q = q_in[chunk].astype(F32)
            parts += [jnp.where(short, q, 0.0), jnp.where(short, swap(q), 0.0)[: TOK - LONG]]
        q_all[2 * TOK * a : 2 * TOK * (a + 1), :] = jnp.concatenate(parts, axis=0).astype(BF)

    def tiles(a):
        whole = [(512 * part, min(512, 256 * a - 512 * part), False) for part in range(-(-a // 2))]
        return whole + [(256 * a, 384 if a == 3 else 512, True)]

    def pair_rows(a):
        return pl.ds(2 * TOK * a, 2 * TOK)

    def shown(a, place_of, first, width):
        return tokens[place_of][:, first : first + width] < q_end[pair_rows(a), :]

    def att_copy(chunk):
        k = lax.rem(chunk - mine + HEADS, HEADS)
        return remote(out_pack.at[chunk], att_all.at[mine], att_send.at[k], att_recv.at[k], 4 * chunk + group)

    summed[...] = jnp.zeros_like(summed)
    mass[...] = jnp.zeros_like(mass)

    def attend(place_of):
        @pl.when(place_of == 1)
        def _():
            def pass_on(chunk):
                z_copy(chunk, 0).wait_recv()
                f_copy(chunk, 0).start()
                z_copy(chunk + 4, 1).wait_recv()
                f_copy(chunk + 4, 1).start()

            loop(0, 4, pass_on)
            loop(4, 8, lambda chunk: z_copy(chunk, 0).wait_recv())

        @pl.when(place_of == 2)
        def _():
            loop(0, 4, lambda chunk: z_copy(chunk, 1).wait_recv())

        add_class(place_of, None)

    def add_class(place_of, then):
        for a in range(4):
            rows = pair_rows(a)
            q = q_all[rows, :]
            for first, width, masked in tiles(a):
                block = kv[place_of, first : first + width, :]
                p = jnp.exp(dot_t(q, block))
                if masked:
                    p = jnp.where(shown(a, place_of, first, width), p, 0.0)
                part_mass = p[:, :128]
                for part in range(1, width // 128):
                    part_mass = part_mass + p[:, 128 * part : 128 * part + 128]
                mass[rows, :] += part_mass
                summed[rows, :] += dot(p.astype(BF), block)
            if then is not None:
                then(a)

    def hand_over(a):
        rows = pair_rows(a)
        one_over = 1.0 / jnp.sum(mass[rows, :], axis=-1, keepdims=True)
        result = summed[rows, :] * one_over
        out[rows, :] = result.astype(BF)
        inverse[rows, :] = one_over
        for half in range(2):
            chunk = 2 * a + half
            value = result[TOK * half : TOK * half + TOK]
            out_pack[chunk] = packed(swap(value), value, left)

            @pl.when(mine != chunk)
            def _():
                att_copy(chunk).start()

            @pl.when(mine == chunk)
            def _():
                pltpu.make_async_copy(out_pack.at[chunk], att_all.at[mine], local.at[0]).start()

    loop(0, 3, attend)
    loop(0, 4, lambda chunk: (f_copy(chunk, 0).wait_recv(), f_copy(chunk + 4, 1).wait_recv()))
    add_class(3, hand_over)

    loads[4].wait()
    loads[5].wait()
    pltpu.make_async_copy(out_pack.at[mine], att_all.at[mine], local.at[0]).wait()

    def att_arrived(k):
        peer = lax.rem(mine + k, HEADS)
        att_copy(peer).wait_recv()

    loop(1, HEADS, att_arrived)
    for pair in range(HEADS // 2):
        slab = unpacked_pair(att_all[2 * pair], att_all[2 * pair + 1], left)
        att[:, 128 * pair : 128 * pair + 128] = slab.astype(BF)
        att_turned[128 * pair : 128 * pair + 128, :] = jnp.transpose(slab).astype(BF)
    for block in range(4):
        columns = pl.ds(256 * block, 256)
        behind = pl.ds(D + 256 * block, 256)
        shift = dot(att[...], wo[:, columns])
        factor = jnp.exp(-dot(att[...], wo[:, behind]))
        upstream = up[:, columns].astype(F32)
        latent = (act[:, columns].astype(F32) - shift) * factor
        scaled = upstream * factor
        carry_part[:, columns] = scaled
        affine_grad[:, columns] = (-scaled).astype(BF)
        affine_grad[:, behind] = (1.0 - upstream * latent).astype(BF)

    def g_copy(head):
        k = lax.rem(head - mine + HEADS, HEADS)
        return remote(g_pack.at[head], g_in.at[mine], g_send.at[k], g_recv.at[k], 4 * head + group)

    def g_own():
        return pltpu.make_async_copy(g_pack.at[mine], g_in.at[mine], local.at[1])

    for block in range(2):
        g = dot_t(affine_grad[...], wo[pl.ds(256 * block, 256), :])
        for half in range(2):
            head = 4 * block + 2 * half
            slab = g[:, 128 * half : 128 * half + 128]
            turned_slab = swap(slab)
            g_pack[head] = packed(slab, turned_slab, left)
            g_pack[head + 1] = packed(turned_slab, slab, left)
        for head in range(4 * block, 4 * block + 4):

            @pl.when(mine != head)
            def _():
                g_copy(head).start()

    g_own().start()
    for block in range(8):
        columns = pl.ds(256 * block, 256)
        term = dot(att_turned[...], affine_grad[:, columns]).astype(BF)
        for owner in range(N_SEQ):
            for half in range(2):
                stream, row = OUT_PLACES[2 * block + half]
                out_sum.terms[stream][slot(FLAT_FIRST[stream], owner, bits), row : row + 16, :] = term[
                    16 * owner : 16 * owner + 16, 128 * half : 128 * half + 128
                ]
    for stream in out_sum.streams:
        out_sum.start(stream, 0)

    g_own().wait()
    loop(1, HEADS, lambda k: g_copy(lax.rem(mine + k, HEADS)).wait_recv())

    for a in range(4):
        rows = pair_rows(a)
        parts = []
        for chunk in (2 * a, 2 * a + 1):
            g = g_in[chunk].astype(F32)
            parts += [jnp.where(short, 0.0, swap(g)), jnp.where(short, 0.0, g)[: TOK - LONG]]
        g = jnp.concatenate(parts, axis=0)
        g_all[rows, :] = g.astype(BF)
        correction[rows, :] = jnp.sum(g * out[rows, :].astype(F32), axis=-1, keepdims=True)
        q_turned[a] = jnp.transpose(q_all[rows, :].astype(F32))[:HEAD_DIM].astype(BF)
        g_turned[a] = jnp.transpose(g)[HEAD_DIM:].astype(BF)
    summed[...] = jnp.zeros_like(summed)

    def dq_copy(chunk):
        k = lax.rem(chunk - mine + HEADS, HEADS)
        return remote(dq.at[chunk], dq_all.at[mine], dq_send.at[k], dq_recv.at[k], 4 * chunk + group)

    def dq_own():
        return pltpu.make_async_copy(dq.at[mine], dq_all.at[mine], local.at[2])

    halves = (pl.ds(0, LOW), pl.ds(LOW, CLASS - LOW))

    def far_copy(way):
        return remote(
            dkv.at[3, halves[way]], far_half[way], back_send.at[way], back_recv.at[way], z_back if way else z_next
        )

    def class_copy(place_of, half):
        at = 2 * place_of + half
        target, peer = (from_next, z_back) if place_of == 1 else (from_back, z_next)
        return remote(dkv.at[place_of, halves[half]], target.at[halves[half]], back_send.at[at], back_recv.at[at], peer)

    def dkv_copy(k):
        peer = lax.rem(mine + k, HEADS)
        return remote(dkv.at[0, chunk_rows(peer)], dkv_all.at[mine], dkv_send.at[k], dkv_recv.at[k], 4 * peer + group)

    def dkv_own():
        return pltpu.make_async_copy(dkv.at[0, chunk_rows(mine)], dkv_all.at[mine], local.at[3])

    def send_keys(chunk):
        @pl.when(mine != chunk)
        def _():
            dkv_copy(lax.rem(chunk - mine + HEADS, HEADS)).start()

        @pl.when(mine == chunk)
        def _():
            dkv_own().start()

    blocks = [(128 * part, 128) for part in range(8)] + [(1024, CLASS - 1024)]

    def settle(place_of, parts, extra):
        for first, width in parts:
            value = jnp.transpose(total[:, first : first + 128])[:width]
            for source, begin in extra:
                value = value + source[first - begin : first - begin + width, :].astype(F32)
            dkv[place_of, first : first + width, :] = value.astype(BF)

    def spans(a, half):
        low, high = ((0, LOW), (LOW, CLASS_ROWS))[half]
        cut = min(max(256 * a, low), high)
        end = min(256 * a + (384 if a == 3 else 512), high)
        return [(low, cut - low, False)] * (cut > low) + [(cut, end - cut, True)] * (end > cut)

    def back_class(place_of, half, then):
        spread = {0: (0, LOW), 1: (LOW, CLASS_ROWS), None: (0, CLASS_ROWS)}[half]
        total[:, spread[0] : spread[1]] = jnp.zeros((128, spread[1] - spread[0]), F32)
        for a in (3, 2, 1, 0):
            rows = pair_rows(a)
            q = q_all[rows, :]
            g = g_all[rows, :]
            one_over = inverse[rows, :]
            corr = correction[rows, :]
            for first, width, masked in tiles(a) if half is None else spans(a, half):
                block = kv[place_of, first : first + width, :]
                p = jnp.exp(dot_t(q, block)) * one_over
                if masked:
                    p = jnp.where(shown(a, place_of, first, width), p, 0.0)
                ds = (p * (dot_t(g, block) - corr)).astype(BF)
                total[:HEAD_DIM, first : first + width] += dot(q_turned[a], ds)
                total[HEAD_DIM:, first : first + width] += dot(g_turned[a], p.astype(BF))
                summed[rows, :] += dot(ds, block)
            if then is not None:
                then(a)

    def send_dq(a):
        result = summed[pair_rows(a), :] * 0.125
        for half in range(2):
            chunk = 2 * a + half
            value = result[TOK * half : TOK * half + TOK]
            dq[chunk] = packed(value, swap(value), left)

            @pl.when(mine != chunk)
            def _():
                dq_copy(chunk).start()

            @pl.when(mine == chunk)
            def _():
                dq_own().start()

    lower, upper = blocks[:4], blocks[4:]
    back_class(3, 0, None)
    settle(3, lower, [])
    far_copy(0).start()
    back_class(3, 1, None)
    settle(3, upper, [])
    far_copy(1).start()
    back_class(1, 0, None)
    settle(1, lower, [])
    class_copy(1, 0).start()
    back_class(2, 1, None)
    settle(2, upper, [])
    class_copy(2, 1).start()
    back_class(2, 0, None)
    far_copy(0).wait_recv()
    settle(2, lower, [(far_half[0], 0)])
    class_copy(2, 0).start()
    out_sum.advance(0)
    back_class(1, 1, None)
    far_copy(1).wait_recv()
    settle(1, upper, [(far_half[1], LOW)])
    class_copy(1, 1).start()
    back_class(0, None, send_dq)
    for half in (1, 0):
        for place_of in (2, 1):
            class_copy(place_of, half).wait_recv()
        settle(0, upper if half else lower, [(from_back, 0), (from_next, 0)])
        for chunk in range(4, 8) if half else range(4):
            send_keys(chunk)
    out_sum.advance(1)

    def unit_back(grad, raw):
        scale = unit_scale(raw, left)
        unit = raw * scale
        return scale * (grad - unit * (per_head_sum(grad * unit, left) * (1.0 / HEAD_DIM)))

    def keys_of(head):
        return dkv_all[head].astype(F32)

    def term_of(which):
        places, into, first = (Q_PLACES, q_sum, 0) if which == 0 else (KV_PLACES, kv_sum, 8 * (which - 1))
        for block in range(2):
            term = dot(normed_turned[...], grads[which, :, 256 * block : 256 * block + 256]).astype(BF)
            for owner in range(N_SEQ):
                for part in range(4):
                    slab, half = part // 2, part % 2
                    stream, row = places[first + 4 * block + 2 * slab + half]
                    top = 32 * owner + 16 * half
                    into.terms[stream][slot(ALL_LINKS[stream], owner, bits), row : row + 16, :] = term[
                        top : top + 16, 128 * slab : 128 * slab + 128
                    ]

    dq_own().wait()
    loop(1, HEADS, lambda k: dq_copy(lax.rem(mine + k, HEADS)).wait_recv())
    for pair in range(HEADS // 2):
        at = pl.ds(128 * pair, 128)
        q_grad = unpacked_pair(dq_all[2 * pair], dq_all[2 * pair + 1], left)
        grads[0, :, at] = unit_back(q_grad, q_raw[:, at]).astype(BF)
    term_of(0)
    for stream in range(5):
        q_sum.start(stream, 0)
    out_sum.advance(2)
    for block in range(4):
        at = pl.ds(256 * block, 256)
        gn[:, at] = dot_t(grads[0], wq[at, :])
    dkv_own().wait()
    loop(1, HEADS, lambda k: dkv_copy(k).wait_recv())
    for pair in range(HEADS // 2):
        at = pl.ds(128 * pair, 128)
        low, high = keys_of(2 * pair), keys_of(2 * pair + 1)
        grads[1, :, at] = unit_back(jnp.where(left, low, swap(high)), k_raw[:, at]).astype(BF)
        grads[2, :, at] = jnp.where(left, swap(low), high).astype(BF)
    term_of(1)
    for stream in range(2):
        kv_sum.start(stream, 0)
    term_of(2)
    for stream in range(2, 5):
        kv_sum.start(stream, 0)
    q_sum.advance(0)
    out_sum.advance(3)
    for block in range(4):
        at = pl.ds(256 * block, 256)
        gn[:, at] += dot_t(grads[1], wk[at, :]) + dot_t(grads[2], wv[at, :])
    field = act[...].astype(F32)
    row_scale = lax.rsqrt(jnp.mean(field * field, axis=-1, keepdims=True) + EPSILON)
    unit = field * row_scale
    grad_normed = gn[...]
    mean = jnp.mean(grad_normed * unit, axis=-1, keepdims=True)
    grad_input[...] = (carry_part[...] + row_scale * (grad_normed - unit * mean)).astype(BF)
    carry = pltpu.make_async_remote_copy(
        src_ref=grad_input, dst_ref=moved, send_sem=carry_sem.at[0], recv_sem=carry_sem.at[1],
        device_id={"section": before, "seq": across}, device_id_type=MESH,
    )
    carry.start()
    q_sum.advance(1)
    kv_sum.advance(0)
    q_sum.advance(2)
    for stream in out_sum.streams:
        result = out_sum.result(stream)
        for part in range(16):
            if OUT_PLACES[part][0] == stream:
                row = OUT_PLACES[part][1]
                sum_out[:, 128 * part : 128 * part + 128] = result[row : row + 16]
    kv_sum.advance(1)
    q_sum.advance(3)

    def deliver(halving, places, targets):
        for stream in range(5):
            result = halving.result(stream)
            for part in range(8 * len(targets)):
                if places[part][0] == stream:
                    row = places[part][1]
                    column, top = 128 * (part % 8 // 2), 16 * (part % 2)
                    targets[part // 8][top : top + 16, column : column + 128] = result[row : row + 16]

    kv_sum.advance(2)
    deliver(q_sum, Q_PLACES, (sum_q,))
    kv_sum.advance(3)
    deliver(kv_sum, KV_PLACES, (sum_k, sum_v))
    carry.wait()

    def left_all(k):
        kv_copy(k).wait_send()
        q_copy(k).wait_send()
        att_copy(lax.rem(mine + k, HEADS)).wait_send()
        g_copy(lax.rem(mine + k, HEADS)).wait_send()
        dq_copy(lax.rem(mine + k, HEADS)).wait_send()
        dkv_copy(k).wait_send()

    loop(1, HEADS, left_all)

    def left_z(chunk):
        for way in range(2):
            z_copy(chunk, way).wait_send()

    loop(0, HEADS, left_z)
    loop(0, 4, lambda chunk: (f_copy(chunk, 0).wait_send(), f_copy(chunk + 4, 1).wait_send()))
    for way in range(2):
        far_copy(way).wait_send()
        for place_of in (1, 2):
            class_copy(place_of, way).wait_send()
    out_sum.drain()
    q_sum.drain()
    kv_sum.drain()


def whole_layer(*operands):
    eight, full, short = (HEADS * TOK, 128), (TOK, D), (HEADS, LONG, 128)
    scratch = [
        (full, BF), (full, BF), ((D, INNER), BF), ((D, INNER), BF), ((D, INNER), BF), ((INNER, 2 * D), BF),
        (full, BF), ((D, TOK), BF), ((TOK, INNER), F32), ((TOK, INNER), F32), (short, BF), ((HEADS, TOK, 128), BF),
        ((4, CLASS_ROWS, 128), BF), (eight, BF), (eight, BF), ((TOKENS, 1), jnp.int32), (eight, BF), ((CLASS, 1), F32),
        (short, BF), ((TOK, INNER), BF), ((INNER, TOK), BF), ((TOK, 2 * D), BF), (short, BF), (full, F32),
        ((128, CLASS_ROWS), F32), ((4, CLASS, 128), BF), (short, BF), ((HEADS, TOK, 128), BF), (short, BF),
        ((3, TOK, INNER), BF), (full, F32), (full, BF),
        ((40, 128), jnp.int32), ((CLASS, 1), jnp.int32), ((4, 1, CLASS_ROWS), jnp.int32), (eight, F32), (eight, F32),
        ((4, HEAD_DIM, 2 * TOK), BF), ((4, HEAD_DIM, 2 * TOK), BF), ((CLASS, 1), F32), (eight, BF), (eight, BF),
        ((LOW, 128), BF), ((CLASS - LOW, 128), BF), (short, BF), (short, BF), (short, BF),
    ]
    dma = pltpu.SemaphoreType.DMA
    return pl.pallas_call(
        layer_body,
        out_shape=[jax.ShapeDtypeStruct((32, INNER), F32)] * 3
        + [jax.ShapeDtypeStruct((16, 2 * D), F32), jax.ShapeDtypeStruct((TOK, D), BF)],
        in_specs=[ANY] * 6 + [VMEM],
        out_specs=[VMEM] * 5,
        scratch_shapes=[pltpu.VMEM(shape, dtype) for shape, dtype in scratch]
        + halving_scratch(OUT_ROWS)
        + halving_scratch(Q_ROWS)
        + halving_scratch(KV_ROWS)
        + [dma((6,)), dma((8,)), dma((8,)), dma((8,)), dma((8,)), dma((2, 8)), dma((2, 8)), dma((8,)), dma((8,))]
        + [dma((8,))] * 8
        + [dma((4,)), dma((2,)), dma((6,)), dma((6,))],
        compiler_params=pltpu.CompilerParams(collective_id=1, has_side_effects=True, vmem_limit_bytes=BIG),
        name="layer",
    )(*operands)


def hand_out_body(sum_q, sum_k, sum_v, sum_out, moved, flip, carry, out_q, out_k, out_v, out_out):
    out_q[...] = sum_q[...]
    out_k[...] = sum_k[...]
    out_v[...] = sum_v[...]
    out_out[...] = sum_out[...]
    turned = (flip[...] == lax.broadcasted_iota(jnp.int32, (TOK, TOK), 0)).astype(F32)
    chosen = jnp.transpose(turned).astype(BF)
    last = (lax.axis_index("section") + jnp.zeros((TOK, 1), jnp.int32)) == 3
    for block in range(4):
        at = pl.ds(256 * block, 256)
        carry[:, at] = jnp.where(last, 0.0, dot(chosen, moved[:, at])).astype(BF)


def hand_out(*operands):
    return pl.pallas_call(
        hand_out_body,
        out_shape=[jax.ShapeDtypeStruct((TOK, D), BF)]
        + [jax.ShapeDtypeStruct((32, INNER), F32)] * 3
        + [jax.ShapeDtypeStruct((16, 2 * D), F32)],
        in_specs=[VMEM] * 6,
        out_specs=[VMEM] * 5,
        name="hand_out",
    )(*operands)


def shards(activations, incoming, w_query, w_key, w_value, w_out, block_ids, flip_order):
    sums = whole_layer(
        activations[0], incoming[0], w_query[0], w_key[0], w_value[0], w_out[0], block_ids.reshape(TOKENS // 128, 128)
    )
    results = hand_out(*sums, flip_order)
    return tuple(result[None] for result in results)


def solution(mesh):
    by_both = P("section", "seq", None)
    by_layer = P("section", None, None)
    in_specs = (by_both, by_both, by_layer, by_layer, by_layer, by_layer, P(), P("section", None))
    return jax.shard_map(shards, mesh=mesh, in_specs=in_specs, out_specs=(by_both,) * 5, check_vma=False)
```

```python
import jax
import jax.numpy as jnp
from jax import lax
from jax.experimental import pallas as pl
from jax.experimental.pallas import tpu as pltpu
from jax.sharding import PartitionSpec as P

HEADS = 8
HEAD_DIM = 64
EPSILON = 1e-06
N_SEQ = 32
TOK = 136
TOKENS = 4352
D = 1024
INNER = 512
CLASS = 8 * TOK
CLASS_ROWS = 1152
LOW = 512
LONG = 80
BF = jnp.bfloat16
F32 = jnp.float32
MESH = pl.DeviceIdType.MESH
VMEM = pl.BlockSpec(memory_space=pltpu.VMEM)
ANY = pl.BlockSpec(memory_space=pl.ANY)
BIG = 60 * 1024 * 1024


def dot(a, b):
    return jnp.dot(a, b, preferred_element_type=F32)


def dot_t(a, b):
    return lax.dot_general(a, b, (((1,), (1,)), ((), ())), preferred_element_type=F32)


def left_half(shape):
    return lax.broadcasted_iota(jnp.int32, shape, 1) < HEAD_DIM


def swap(slab):
    return pltpu.roll(slab, HEAD_DIM, 1)


def per_head_sum(slab, left):
    low = jnp.sum(jnp.where(left, slab, 0.0), axis=-1, keepdims=True)
    high = jnp.sum(jnp.where(left, 0.0, slab), axis=-1, keepdims=True)
    return jnp.where(left, low, high)


def packed(near, far, left):
    rest = jnp.concatenate([far[LONG:], jnp.zeros((2 * LONG - TOK, 128), F32)], axis=0)
    return jnp.where(left[:LONG], near[:LONG], rest).astype(BF)


def unpacked_pair(low, high, left):
    low, high = low.astype(F32), high.astype(F32)
    top = jnp.where(left[:LONG], low, swap(high))
    rest = jnp.where(left[:LONG], swap(low), high)[: TOK - LONG]
    return jnp.concatenate([top, rest], axis=0)


def unit_scale(slab, left):
    return lax.rsqrt(per_head_sum(slab * slab, left) * (1.0 / HEAD_DIM) + EPSILON)


def place():
    me = lax.axis_index("seq")
    x, z = lax.rem(lax.div(me, 4), 4), lax.rem(me, 4)
    return ring_bits(lax.div(me, 16), x, z)


def ring_bits(y, x, z):
    return (y, lax.rem(lax.div(x + 1, 2), 2), lax.div(x, 2), lax.rem(lax.div(z + 1, 2), 2), lax.div(z, 2))


def neighbours():
    me = lax.axis_index("seq")
    x, z = lax.rem(lax.div(me, 4), 4), lax.rem(me, 4)
    return (
        lax.rem(me + 16, N_SEQ),
        me + 4 * (1 - 2 * lax.rem(x, 2)),
        me + 4 * (3 - 2 * x),
        me + 1 - 2 * lax.rem(z, 2),
        me + 3 - 2 * z,
    )


ALL_LINKS = tuple(tuple((first + step) % 5 for step in range(5)) for first in range(5))
FLAT_FIRST = ((0, 1, 2, 3, 4), (1, 2, 0, 4, 3), (2, 0, 1, 3, 4))


def spread_out(groups, orders):
    streams = len(orders)
    counts = [groups // streams + (1 if stream < groups % streams else 0) for stream in range(streams)]
    places = [(stream, 16 * row) for stream in range(streams) for row in range(counts[stream])]
    return [16 * count for count in counts], places


Q_ROWS, Q_PLACES = spread_out(8, ALL_LINKS)
KV_ROWS, KV_PLACES = spread_out(16, ALL_LINKS)
OUT_ROWS, OUT_PLACES = spread_out(16, FLAT_FIRST)


def slot(order, owner, bits):
    y, x, z = owner // 16, owner // 4 % 4, owner % 4
    theirs = (y, (x + 1) // 2 % 2, x // 2, (z + 1) // 2 % 2, z // 2)
    at = 0
    for step, split in enumerate(order):
        apart = 1 - bits[split] if theirs[split] else bits[split]
        at = at + apart * (16 >> step)
    return at


class Halving:
    def __init__(self, refs, orders, near):
        count = len(orders)
        self.terms, self.acc, self.got = refs[:count], refs[count : 2 * count], refs[2 * count : 3 * count]
        self.send, self.recv = refs[3 * count :]
        self.orders, self.near, self.streams = orders, near, range(count)

    def hop(self, stream, step, part):
        half = 16 >> step
        first, size = (half // 2 * (1 - part), half // 2) if step < 4 else (0, 1)
        return pltpu.make_async_remote_copy(
            src_ref=(self.acc if step else self.terms)[stream].at[pl.ds(half + first, size)],
            dst_ref=self.got[stream].at[pl.ds(32 - (32 >> step) + first, size)],
            send_sem=self.send.at[stream, step, part],
            recv_sem=self.recv.at[stream, step, part],
            device_id={"seq": self.near[self.orders[stream][step]]},
            device_id_type=MESH,
        )

    def start(self, stream, step):
        for part in range(2 if step < 4 else 1):
            self.hop(stream, step, part).start()

    def add(self, stream, step, first, count):
        mine = (self.acc if step else self.terms)[stream]
        acc, got = self.acc[stream], self.got[stream]
        behind = 32 - (32 >> step)
        width = min(count, 4)

        def one(i, _):
            at = first + width * i
            total = mine[pl.ds(at, width)].astype(F32) + got[pl.ds(behind + at, width)].astype(F32)
            acc[pl.ds(at, width)] = total.astype(BF)
            return 0

        if count == width:
            one(0, 0)
        else:
            lax.fori_loop(0, count // width, one, 0)

    def advance(self, step):
        half = 8 >> step
        for stream in self.streams:
            self.hop(stream, step, 0).wait_recv()
            self.add(stream, step, half, half)
            self.start(stream, step + 1)
        for stream in self.streams:
            self.hop(stream, step, 1).wait_recv()
            self.add(stream, step, 0, half)

    def result(self, stream):
        self.hop(stream, 4, 0).wait_recv()
        return self.acc[stream][0].astype(F32) + self.got[stream][30].astype(F32)

    def drain(self):
        for step in range(5):
            for stream in self.streams:
                for part in range(2 if step < 4 else 1):
                    self.hop(stream, step, part).wait_send()


def halving_scratch(rows):
    return (
        [pltpu.VMEM((N_SEQ, count, 128), BF) for count in rows]
        + [pltpu.VMEM((16, count, 128), BF) for count in rows]
        + [pltpu.VMEM((31, count, 128), BF) for count in rows]
        + [pltpu.SemaphoreType.DMA((len(rows), 5, 2)), pltpu.SemaphoreType.DMA((len(rows), 5, 2))]
    )


def chunk_rows(index):
    return pl.ds(pl.multiple_of(index * TOK, 8), TOK)


def layer_body(*refs):
    refs = list(refs)

    def take(count):
        taken = refs[:count]
        del refs[:count]
        return taken

    act_in, up_in, wq_in, wk_in, wv_in, wo_in, ids = take(7)
    sum_q, sum_k, sum_v, sum_out, moved = take(5)
    act, up, wq, wk, wv, wo = take(6)
    normed, normed_turned, q_raw, k_raw, q_pack, kv_pack = take(6)
    kv, q_all, g_all, q_ids, out, inverse, att_all, att, att_turned, affine_grad, g_pack, carry_part = take(12)
    total, dkv, dq, dkv_all, dq_all, grads, gn, grad_input = take(8)
    padded_ids, q_end, tokens, summed, mass, q_turned, g_turned, correction = take(8)
    from_back, from_next, class_sum = take(2), take(2), take(2)
    far_half = take(2)
    q_in, g_in, out_pack = take(3)
    out_refs, q_refs, kv_refs = take(11), take(17), take(17)
    (load, kv_send, kv_recv, q_send, q_recv, z_send, z_recv, f_send, f_recv, att_send, att_recv,
     g_send, g_recv, dq_send, dq_recv, dkv_send, dkv_recv, local, carry_sem, back_send, back_recv) = refs

    me = lax.axis_index("seq")
    section = lax.axis_index("section")
    mine, group = lax.div(me, 4), lax.rem(me, 4)
    near, bits = neighbours(), place()
    across = N_SEQ - 1 - me
    before, after = lax.rem(section + 3, 4), lax.rem(section + 1, 4)
    z_next, z_back = 4 * mine + lax.rem(group + 1, 4), 4 * mine + lax.rem(group + 3, 4)

    loads = [
        pltpu.make_async_copy(source, target, load.at[i])
        for i, (source, target) in enumerate(
            ((act_in, act), (wq_in, wq), (wk_in, wk), (wv_in, wv), (wo_in, wo), (up_in, up))
        )
    ]
    for copy in loads:
        copy.start()

    barrier = pltpu.get_barrier_semaphore()

    def greet(k, _):
        peer = 4 * lax.rem(mine + k, HEADS) + group
        pl.semaphore_signal(barrier, inc=1, device_id={"seq": peer}, device_id_type=MESH)
        return 0

    lax.fori_loop(1, HEADS, greet, 0)
    for peer in (z_next, z_back):
        pl.semaphore_signal(barrier, inc=1, device_id={"seq": peer}, device_id_type=MESH)
    for other in (before, after):
        pl.semaphore_signal(barrier, inc=1, device_id={"section": other, "seq": across}, device_id_type=MESH)

    def remote(source, target, send, recv, peer):
        return pltpu.make_async_remote_copy(
            src_ref=source, dst_ref=target, send_sem=send, recv_sem=recv,
            device_id={"seq": peer}, device_id_type=MESH,
        )

    def loop(first, end, do):
        def one(k, c):
            do(k)
            return c

        lax.fori_loop(first, end, one, 0)

    left = left_half((TOK, 128))
    out_sum = Halving(out_refs, FLAT_FIRST, near)
    q_sum = Halving(q_refs, ALL_LINKS, near)
    kv_sum = Halving(kv_refs, ALL_LINKS, near)

    loads[0].wait()
    field = act[...].astype(F32)
    row_scale = lax.rsqrt(jnp.mean(field * field, axis=-1, keepdims=True) + EPSILON)
    normed[...] = (field * row_scale).astype(BF)
    for copy in loads[1:4]:
        copy.wait()
    for block in range(2):
        columns = pl.ds(256 * block, 256)
        q = dot(normed[...], wq[:, columns])
        k = dot(normed[...], wk[:, columns])
        v = dot(normed[...], wv[:, columns])
        q_raw[:, columns] = q
        k_raw[:, columns] = k
        for half in range(2):
            head = 4 * block + 2 * half
            q_slab = q[:, 128 * half : 128 * half + 128]
            k_slab = k[:, 128 * half : 128 * half + 128]
            v_slab = v[:, 128 * half : 128 * half + 128]
            q_slab = (q_slab * unit_scale(q_slab, left)).astype(BF).astype(F32) * 0.125
            k_slab = k_slab * unit_scale(k_slab, left)
            q_swap = swap(q_slab)
            q_pack[head] = packed(q_slab, q_swap, left)
            q_pack[head + 1] = packed(q_swap, q_slab, left)
            kv_pack[head] = jnp.where(left, k_slab, swap(v_slab)).astype(BF)
            kv_pack[head + 1] = jnp.where(left, swap(k_slab), v_slab).astype(BF)
    pl.semaphore_wait(barrier, HEADS + 3)

    def kv_copy(k):
        peer = lax.rem(mine + k, HEADS)
        return remote(kv_pack.at[peer], kv.at[0, chunk_rows(mine)], kv_send.at[k], kv_recv.at[k], 4 * peer + group)

    def q_copy(k):
        peer = lax.rem(mine + k, HEADS)
        return remote(q_pack.at[peer], q_in.at[mine], q_send.at[k], q_recv.at[k], 4 * peer + group)

    loop(1, HEADS, lambda k: kv_copy(k).start())
    own = [
        pltpu.make_async_copy(kv_pack.at[mine], kv.at[0, chunk_rows(mine)], local.at[0]),
        pltpu.make_async_copy(q_pack.at[mine], q_in.at[mine], local.at[1]),
    ]
    for copy in own:
        copy.start()
    loop(1, HEADS, lambda k: q_copy(k).start())
    for place_of in range(4):
        kv[place_of, CLASS:, :] = jnp.zeros((CLASS_ROWS - CLASS, 128), BF)
    own[0].wait()

    def z_copy(chunk, way):
        return remote(
            kv.at[0, chunk_rows(chunk)], kv.at[1 + way, chunk_rows(chunk)],
            z_send.at[way, chunk], z_recv.at[way, chunk], z_back if way else z_next,
        )

    def f_copy(chunk, way):
        return remote(
            kv.at[1 + way, chunk_rows(chunk)], kv.at[3, chunk_rows(chunk)],
            f_send.at[chunk], f_recv.at[chunk], z_back if way else z_next,
        )

    def relay(chunk):
        for way in range(2):
            z_copy(chunk, way).start()

    relay(mine)

    def pipe(k):
        kv_copy(k).wait_recv()
        relay(lax.rem(mine - k + HEADS, HEADS))

    loop(1, HEADS, pipe)

    turned = jnp.transpose(ids[...].astype(F32)).astype(jnp.int32)
    for row in range(TOKENS // 128):
        q_ids[128 * row : 128 * row + 128, :] = turned[:, row : row + 1]
    padded_ids[: TOKENS // 128, :] = ids[...]
    padded_ids[TOKENS // 128 :, :] = jnp.full((40 - TOKENS // 128, 128), TOKENS, jnp.int32)
    for chunk in range(HEADS):
        first = pl.multiple_of((4 * chunk + group) * TOK, 8)
        row = lax.div(first, 128)
        column = q_ids[pl.ds(first, TOK), :]
        seen = jnp.zeros((TOK, 128), F32)
        for behind in range(5):
            seen = seen + jnp.where(padded_ids[pl.ds(row + behind, 1), :] <= column, 1.0, 0.0)
        count = jnp.sum(seen, axis=-1, keepdims=True).astype(jnp.int32)
        q_end[TOK * chunk : TOK * chunk + TOK, :] = count + 128 * row
    lane = lax.broadcasted_iota(jnp.int32, (1, CLASS_ROWS), 1)
    skipped = jnp.zeros((1, CLASS_ROWS), jnp.int32)
    for chunk in range(1, HEADS + 1):
        skipped = skipped + jnp.where(lane >= TOK * chunk, 3 * TOK, 0)
    for place_of, apart in enumerate((0, 3, 1, 2)):
        tokens[place_of] = lane + skipped + TOK * lax.rem(group + apart, 4)
    for block in range(8):
        at = pl.ds(128 * block, 128)
        normed_turned[at, :] = jnp.transpose(normed[:, at].astype(F32)).astype(BF)
    own[1].wait()
    loop(1, HEADS, lambda k: q_copy(k).wait_recv())
    short = left[:LONG]
    for a in range(4):
        parts = []
        for chunk in (2 * a, 2 * a + 1):
            q = q_in[chunk].astype(F32)
            parts += [jnp.where(short, q, 0.0), jnp.where(short, swap(q), 0.0)[: TOK - LONG]]
        q_all[2 * TOK * a : 2 * TOK * (a + 1), :] = jnp.concatenate(parts, axis=0).astype(BF)

    def tiles(a):
        whole = [(512 * part, min(512, 256 * a - 512 * part), False) for part in range(-(-a // 2))]
        return whole + [(256 * a, 384 if a == 3 else 512, True)]

    def pair_rows(a):
        return pl.ds(2 * TOK * a, 2 * TOK)

    def shown(a, place_of, first, width):
        return tokens[place_of][:, first : first + width] < q_end[pair_rows(a), :]

    def att_copy(chunk):
        k = lax.rem(chunk - mine + HEADS, HEADS)
        return remote(out_pack.at[chunk], att_all.at[mine], att_send.at[k], att_recv.at[k], 4 * chunk + group)

    summed[...] = jnp.zeros_like(summed)
    mass[...] = jnp.zeros_like(mass)

    def attend(place_of):
        @pl.when(place_of == 1)
        def _():
            def pass_on(chunk):
                z_copy(chunk, 0).wait_recv()
                f_copy(chunk, 0).start()
                z_copy(chunk + 4, 1).wait_recv()
                f_copy(chunk + 4, 1).start()

            loop(0, 4, pass_on)
            loop(4, 8, lambda chunk: z_copy(chunk, 0).wait_recv())

        @pl.when(place_of == 2)
        def _():
            loop(0, 4, lambda chunk: z_copy(chunk, 1).wait_recv())

        add_class(place_of, None)

    def add_class(place_of, then):
        for a in range(4):
            rows = pair_rows(a)
            q = q_all[rows, :]
            for first, width, masked in tiles(a):
                block = kv[place_of, first : first + width, :]
                p = jnp.exp(dot_t(q, block))
                if masked:
                    p = jnp.where(shown(a, place_of, first, width), p, 0.0)
                part_mass = p[:, :128]
                for part in range(1, width // 128):
                    part_mass = part_mass + p[:, 128 * part : 128 * part + 128]
                mass[rows, :] += part_mass
                summed[rows, :] += dot(p.astype(BF), block)
            if then is not None:
                then(a)

    def hand_over(a):
        rows = pair_rows(a)
        one_over = 1.0 / jnp.sum(mass[rows, :], axis=-1, keepdims=True)
        result = summed[rows, :] * one_over
        out[rows, :] = result.astype(BF)
        inverse[rows, :] = one_over
        for half in range(2):
            chunk = 2 * a + half
            value = result[TOK * half : TOK * half + TOK]
            out_pack[chunk] = packed(swap(value), value, left)

            @pl.when(mine != chunk)
            def _():
                att_copy(chunk).start()

            @pl.when(mine == chunk)
            def _():
                pltpu.make_async_copy(out_pack.at[chunk], att_all.at[mine], local.at[0]).start()

    loop(0, 3, attend)
    loop(0, 4, lambda chunk: (f_copy(chunk, 0).wait_recv(), f_copy(chunk + 4, 1).wait_recv()))
    add_class(3, hand_over)

    loads[4].wait()
    loads[5].wait()
    pltpu.make_async_copy(out_pack.at[mine], att_all.at[mine], local.at[0]).wait()

    def att_arrived(k):
        peer = lax.rem(mine + k, HEADS)
        att_copy(peer).wait_recv()

    loop(1, HEADS, att_arrived)
    for pair in range(HEADS // 2):
        slab = unpacked_pair(att_all[2 * pair], att_all[2 * pair + 1], left)
        att[:, 128 * pair : 128 * pair + 128] = slab.astype(BF)
        att_turned[128 * pair : 128 * pair + 128, :] = jnp.transpose(slab).astype(BF)
    for block in range(4):
        columns = pl.ds(256 * block, 256)
        behind = pl.ds(D + 256 * block, 256)
        shift = dot(att[...], wo[:, columns])
        factor = jnp.exp(-dot(att[...], wo[:, behind]))
        upstream = up[:, columns].astype(F32)
        latent = (act[:, columns].astype(F32) - shift) * factor
        scaled = upstream * factor
        carry_part[:, columns] = scaled
        affine_grad[:, columns] = (-scaled).astype(BF)
        affine_grad[:, behind] = (1.0 - upstream * latent).astype(BF)

    def g_copy(head):
        k = lax.rem(head - mine + HEADS, HEADS)
        return remote(g_pack.at[head], g_in.at[mine], g_send.at[k], g_recv.at[k], 4 * head + group)

    def g_own():
        return pltpu.make_async_copy(g_pack.at[mine], g_in.at[mine], local.at[1])

    for block in range(2):
        g = dot_t(affine_grad[...], wo[pl.ds(256 * block, 256), :])
        for half in range(2):
            head = 4 * block + 2 * half
            slab = g[:, 128 * half : 128 * half + 128]
            turned_slab = swap(slab)
            g_pack[head] = packed(slab, turned_slab, left)
            g_pack[head + 1] = packed(turned_slab, slab, left)
        for head in range(4 * block, 4 * block + 4):

            @pl.when(mine != head)
            def _():
                g_copy(head).start()

    g_own().start()
    for block in range(8):
        columns = pl.ds(256 * block, 256)
        term = dot(att_turned[...], affine_grad[:, columns]).astype(BF)
        for owner in range(N_SEQ):
            for half in range(2):
                stream, row = OUT_PLACES[2 * block + half]
                out_sum.terms[stream][slot(FLAT_FIRST[stream], owner, bits), row : row + 16, :] = term[
                    16 * owner : 16 * owner + 16, 128 * half : 128 * half + 128
                ]
    for stream in out_sum.streams:
        out_sum.start(stream, 0)

    for a in range(4):
        q_turned[a] = jnp.transpose(q_all[pair_rows(a), :].astype(F32))[:HEAD_DIM].astype(BF)
    g_own().wait()
    loop(1, HEADS, lambda k: g_copy(lax.rem(mine + k, HEADS)).wait_recv())

    for a in range(4):
        rows = pair_rows(a)
        parts = []
        for chunk in (2 * a, 2 * a + 1):
            g = g_in[chunk].astype(F32)
            parts += [jnp.where(short, 0.0, swap(g)), jnp.where(short, 0.0, g)[: TOK - LONG]]
        g = jnp.concatenate(parts, axis=0)
        g_all[rows, :] = g.astype(BF)
        correction[rows, :] = jnp.sum(g * out[rows, :].astype(F32), axis=-1, keepdims=True)
        g_turned[a] = jnp.transpose(g)[HEAD_DIM:].astype(BF)
    summed[...] = jnp.zeros_like(summed)

    def dq_copy(chunk):
        k = lax.rem(chunk - mine + HEADS, HEADS)
        return remote(dq.at[chunk], dq_all.at[mine], dq_send.at[k], dq_recv.at[k], 4 * chunk + group)

    def dq_own():
        return pltpu.make_async_copy(dq.at[mine], dq_all.at[mine], local.at[2])

    def far_copy(way):
        return remote(
            class_sum[way].at[2], far_half[way], back_send.at[way], back_recv.at[way], z_back if way else z_next
        )

    def class_copy(place_of, half):
        at = 2 * place_of + half
        target, peer = (from_next, z_back) if place_of == 1 else (from_back, z_next)
        return remote(class_sum[half].at[place_of - 1], target[half], back_send.at[at], back_recv.at[at], peer)

    def dkv_copy(k):
        peer = lax.rem(mine + k, HEADS)
        return remote(dkv.at[chunk_rows(peer)], dkv_all.at[mine], dkv_send.at[k], dkv_recv.at[k], 4 * peer + group)

    def dkv_own():
        return pltpu.make_async_copy(dkv.at[chunk_rows(mine)], dkv_all.at[mine], local.at[3])

    def send_keys(chunk):
        @pl.when(mine != chunk)
        def _():
            dkv_copy(lax.rem(chunk - mine + HEADS, HEADS)).start()

        @pl.when(mine == chunk)
        def _():
            dkv_own().start()

    columns_of = (slice(0, LOW), slice(LOW, CLASS_ROWS))

    def settle(place_of, half, extra):
        value = total[:, columns_of[half]]
        if extra is not None:
            value = value + extra[...].astype(F32)
        class_sum[half][place_of - 1] = value.astype(BF)

    def settle_own(half):
        for first in range(0, LOW, 128) if half == 0 else range(LOW, CLASS, 128):
            begin = first - LOW * half
            at = slice(begin, begin + 128)
            value = total[:, first : first + 128]
            value = value + from_back[half][:, at].astype(F32) + from_next[half][:, at].astype(F32)
            width = min(128, CLASS - first)
            dkv[first : first + width, :] = jnp.transpose(value)[:width].astype(BF)

    def spans(a, half):
        low, high = ((0, LOW), (LOW, CLASS_ROWS))[half]
        cut = min(max(256 * a, low), high)
        end = min(256 * a + (384 if a == 3 else 512), high)
        return [(low, cut - low, False)] * (cut > low) + [(cut, end - cut, True)] * (end > cut)

    def back_class(place_of, half, then):
        spread = {0: (0, LOW), 1: (LOW, CLASS_ROWS), None: (0, CLASS_ROWS)}[half]
        total[:, spread[0] : spread[1]] = jnp.zeros((128, spread[1] - spread[0]), F32)
        for a in (3, 2, 1, 0):
            rows = pair_rows(a)
            q = q_all[rows, :]
            g = g_all[rows, :]
            one_over = inverse[rows, :]
            corr = correction[rows, :]
            pieces = tiles(a) if half is None else spans(a, half)
            if pieces:
                first = pieces[0][0]
                width = sum(piece[1] for piece in pieces)
                block = kv[place_of, first : first + width, :]
                p = jnp.exp(dot_t(q, block)) * one_over
                parts = []
                for begin, size, masked in pieces:
                    part = p[:, begin - first : begin - first + size]
                    parts.append(jnp.where(shown(a, place_of, begin, size), part, 0.0) if masked else part)
                p = jnp.concatenate(parts, axis=1) if len(parts) > 1 else parts[0]
                ds = (p * (dot_t(g, block) - corr)).astype(BF)
                total[:HEAD_DIM, first : first + width] += dot(q_turned[a], ds)
                total[HEAD_DIM:, first : first + width] += dot(g_turned[a], p.astype(BF))
                summed[rows, :] += dot(ds, block)
            if then is not None:
                then(a)

    def send_dq(a):
        result = summed[pair_rows(a), :] * 0.125
        for half in range(2):
            chunk = 2 * a + half
            value = result[TOK * half : TOK * half + TOK]
            dq[chunk] = packed(value, swap(value), left)

            @pl.when(mine != chunk)
            def _():
                dq_copy(chunk).start()

            @pl.when(mine == chunk)
            def _():
                dq_own().start()

    back_class(3, None, None)
    settle(3, 0, None)
    far_copy(0).start()
    settle(3, 1, None)
    far_copy(1).start()
    back_class(1, 0, None)
    settle(1, 0, None)
    class_copy(1, 0).start()
    back_class(2, 1, None)
    settle(2, 1, None)
    class_copy(2, 1).start()
    back_class(2, 0, None)
    far_copy(0).wait_recv()
    settle(2, 0, far_half[0])
    class_copy(2, 0).start()
    out_sum.advance(0)
    back_class(1, 1, None)
    far_copy(1).wait_recv()
    settle(1, 1, far_half[1])
    class_copy(1, 1).start()
    back_class(0, None, send_dq)
    for half in (1, 0):
        for place_of in (2, 1):
            class_copy(place_of, half).wait_recv()
        settle_own(half)
        for chunk in range(4, 8) if half else range(4):
            send_keys(chunk)
    out_sum.advance(1)

    def unit_back(grad, raw):
        scale = unit_scale(raw, left)
        unit = raw * scale
        return scale * (grad - unit * (per_head_sum(grad * unit, left) * (1.0 / HEAD_DIM)))

    def keys_of(head):
        return dkv_all[head].astype(F32)

    def term_of(which):
        places, into, first = (Q_PLACES, q_sum, 0) if which == 0 else (KV_PLACES, kv_sum, 8 * (2 - which))
        for block in range(2):
            term = dot(normed_turned[...], grads[which, :, 256 * block : 256 * block + 256]).astype(BF)
            for owner in range(N_SEQ):
                for part in range(4):
                    slab, half = part // 2, part % 2
                    stream, row = places[first + 4 * block + 2 * slab + half]
                    top = 32 * owner + 16 * half
                    into.terms[stream][slot(ALL_LINKS[stream], owner, bits), row : row + 16, :] = term[
                        top : top + 16, 128 * slab : 128 * slab + 128
                    ]

    dq_own().wait()
    loop(1, HEADS, lambda k: dq_copy(lax.rem(mine + k, HEADS)).wait_recv())
    for pair in range(HEADS // 2):
        at = pl.ds(128 * pair, 128)
        q_grad = unpacked_pair(dq_all[2 * pair], dq_all[2 * pair + 1], left)
        grads[0, :, at] = unit_back(q_grad, q_raw[:, at]).astype(BF)
    term_of(0)
    for stream in range(5):
        q_sum.start(stream, 0)
    out_sum.advance(2)
    for block in range(4):
        at = pl.ds(256 * block, 256)
        gn[:, at] = dot_t(grads[0], wq[at, :])
    dkv_own().wait()
    loop(1, HEADS, lambda k: dkv_copy(k).wait_recv())
    for pair in range(HEADS // 2):
        low, high = keys_of(2 * pair), keys_of(2 * pair + 1)
        grads[2, :, 128 * pair : 128 * pair + 128] = jnp.where(left, swap(low), high).astype(BF)
    term_of(2)
    for stream in range(2):
        kv_sum.start(stream, 0)
    for pair in range(HEADS // 2):
        at = pl.ds(128 * pair, 128)
        low, high = keys_of(2 * pair), keys_of(2 * pair + 1)
        grads[1, :, at] = unit_back(jnp.where(left, low, swap(high)), k_raw[:, at]).astype(BF)
    term_of(1)
    for stream in range(2, 5):
        kv_sum.start(stream, 0)
    q_sum.advance(0)
    out_sum.advance(3)
    for block in range(4):
        at = pl.ds(256 * block, 256)
        gn[:, at] += dot_t(grads[1], wk[at, :]) + dot_t(grads[2], wv[at, :])
    field = act[...].astype(F32)
    row_scale = lax.rsqrt(jnp.mean(field * field, axis=-1, keepdims=True) + EPSILON)
    unit = field * row_scale
    grad_normed = gn[...]
    mean = jnp.mean(grad_normed * unit, axis=-1, keepdims=True)
    grad_input[...] = (carry_part[...] + row_scale * (grad_normed - unit * mean)).astype(BF)

    def carry(piece):
        first, count = ((0, 48), (48, 32), (80, 32), (112, 24))[piece]
        rows = pl.ds(first, count)
        return pltpu.make_async_remote_copy(
            src_ref=grad_input.at[rows], dst_ref=moved.at[rows], send_sem=carry_sem.at[0, piece],
            recv_sem=carry_sem.at[1, piece], device_id={"section": before, "seq": across}, device_id_type=MESH,
        )

    carry(0).start()
    q_sum.advance(1)
    kv_sum.advance(0)
    carry(1).start()
    q_sum.advance(2)
    for stream in out_sum.streams:
        result = out_sum.result(stream)
        for part in range(16):
            if OUT_PLACES[part][0] == stream:
                row = OUT_PLACES[part][1]
                sum_out[:, 128 * part : 128 * part + 128] = result[row : row + 16]
    kv_sum.advance(1)
    carry(2).start()
    carry(3).start()
    q_sum.advance(3)

    def deliver(halving, places, targets):
        for stream in range(5):
            result = halving.result(stream)
            for part in range(8 * len(targets)):
                if places[part][0] == stream:
                    row = places[part][1]
                    column, top = 128 * (part % 8 // 2), 16 * (part % 2)
                    targets[part // 8][top : top + 16, column : column + 128] = result[row : row + 16]

    kv_sum.advance(2)
    deliver(q_sum, Q_PLACES, (sum_q,))
    kv_sum.advance(3)
    deliver(kv_sum, KV_PLACES, (sum_v, sum_k))
    for piece in range(4):
        carry(piece).wait()

    def left_all(k):
        kv_copy(k).wait_send()
        q_copy(k).wait_send()
        att_copy(lax.rem(mine + k, HEADS)).wait_send()
        g_copy(lax.rem(mine + k, HEADS)).wait_send()
        dq_copy(lax.rem(mine + k, HEADS)).wait_send()
        dkv_copy(k).wait_send()

    loop(1, HEADS, left_all)

    def left_z(chunk):
        for way in range(2):
            z_copy(chunk, way).wait_send()

    loop(0, HEADS, left_z)
    loop(0, 4, lambda chunk: (f_copy(chunk, 0).wait_send(), f_copy(chunk + 4, 1).wait_send()))
    for way in range(2):
        far_copy(way).wait_send()
        for place_of in (1, 2):
            class_copy(place_of, way).wait_send()
    out_sum.drain()
    q_sum.drain()
    kv_sum.drain()


def whole_layer(*operands):
    eight, full, short = (HEADS * TOK, 128), (TOK, D), (HEADS, LONG, 128)
    low, high = (128, LOW), (128, CLASS_ROWS - LOW)
    scratch = [
        (full, BF), (full, BF), ((D, INNER), BF), ((D, INNER), BF), ((D, INNER), BF), ((INNER, 2 * D), BF),
        (full, BF), ((D, TOK), BF), ((TOK, INNER), F32), ((TOK, INNER), F32), (short, BF), ((HEADS, TOK, 128), BF),
        ((4, CLASS_ROWS, 128), BF), (eight, BF), (eight, BF), ((TOKENS, 1), jnp.int32), (eight, BF), ((CLASS, 1), F32),
        (short, BF), ((TOK, INNER), BF), ((INNER, TOK), BF), ((TOK, 2 * D), BF), (short, BF), (full, F32),
        ((128, CLASS_ROWS), F32), (eight, BF), (short, BF), ((HEADS, TOK, 128), BF), (short, BF),
        ((3, TOK, INNER), BF), (full, F32), (full, BF),
        ((40, 128), jnp.int32), ((CLASS, 1), jnp.int32), ((4, 1, CLASS_ROWS), jnp.int32), (eight, F32), (eight, F32),
        ((4, HEAD_DIM, 2 * TOK), BF), ((4, HEAD_DIM, 2 * TOK), BF), ((CLASS, 1), F32),
        (low, BF), (high, BF), (low, BF), (high, BF), ((3, *low), BF), ((3, *high), BF),
        (low, BF), (high, BF), (short, BF), (short, BF), (short, BF),
    ]
    dma = pltpu.SemaphoreType.DMA
    return pl.pallas_call(
        layer_body,
        out_shape=[jax.ShapeDtypeStruct((32, INNER), F32)] * 3
        + [jax.ShapeDtypeStruct((16, 2 * D), F32), jax.ShapeDtypeStruct((TOK, D), BF)],
        in_specs=[ANY] * 6 + [VMEM],
        out_specs=[VMEM] * 5,
        scratch_shapes=[pltpu.VMEM(shape, dtype) for shape, dtype in scratch]
        + halving_scratch(OUT_ROWS)
        + halving_scratch(Q_ROWS)
        + halving_scratch(KV_ROWS)
        + [dma((6,)), dma((8,)), dma((8,)), dma((8,)), dma((8,)), dma((2, 8)), dma((2, 8)), dma((8,)), dma((8,))]
        + [dma((8,))] * 8
        + [dma((4,)), dma((2, 4)), dma((6,)), dma((6,))],
        compiler_params=pltpu.CompilerParams(collective_id=1, has_side_effects=True, vmem_limit_bytes=BIG),
        name="layer",
    )(*operands)


def hand_out_body(sum_q, sum_k, sum_v, sum_out, moved, flip, carry, out_q, out_k, out_v, out_out):
    out_q[...] = sum_q[...]
    out_k[...] = sum_k[...]
    out_v[...] = sum_v[...]
    out_out[...] = sum_out[...]
    turned = (flip[...] == lax.broadcasted_iota(jnp.int32, (TOK, TOK), 0)).astype(F32)
    chosen = jnp.transpose(turned).astype(BF)
    last = (lax.axis_index("section") + jnp.zeros((TOK, 1), jnp.int32)) == 3
    for block in range(4):
        at = pl.ds(256 * block, 256)
        carry[:, at] = jnp.where(last, 0.0, dot(chosen, moved[:, at])).astype(BF)


def hand_out(*operands):
    return pl.pallas_call(
        hand_out_body,
        out_shape=[jax.ShapeDtypeStruct((TOK, D), BF)]
        + [jax.ShapeDtypeStruct((32, INNER), F32)] * 3
        + [jax.ShapeDtypeStruct((16, 2 * D), F32)],
        in_specs=[VMEM] * 6,
        out_specs=[VMEM] * 5,
        name="hand_out",
    )(*operands)


def shards(activations, incoming, w_query, w_key, w_value, w_out, block_ids, flip_order):
    sums = whole_layer(
        activations[0], incoming[0], w_query[0], w_key[0], w_value[0], w_out[0], block_ids.reshape(TOKENS // 128, 128)
    )
    results = hand_out(*sums, flip_order)
    return tuple(result[None] for result in results)


def solution(mesh):
    by_both = P("section", "seq", None)
    by_layer = P("section", None, None)
    in_specs = (by_both, by_both, by_layer, by_layer, by_layer, by_layer, P(), P("section", None))
    return jax.shard_map(shards, mesh=mesh, in_specs=in_specs, out_specs=(by_both,) * 5, check_vma=False)
```

```python
import jax
import jax.numpy as jnp
from jax import lax
from jax.experimental import pallas as pl
from jax.experimental.pallas import tpu as pltpu
from jax.sharding import PartitionSpec as P

HEADS = 8
HEAD_DIM = 64
EPSILON = 1e-06
N_SEQ = 32
TOK = 136
TOKENS = 4352
D = 1024
INNER = 512
CLASS = 8 * TOK
CLASS_ROWS = 1152
LOW = 512
LONG = 80
BF = jnp.bfloat16
F32 = jnp.float32
MESH = pl.DeviceIdType.MESH
VMEM = pl.BlockSpec(memory_space=pltpu.VMEM)
ANY = pl.BlockSpec(memory_space=pl.ANY)
BIG = 60 * 1024 * 1024


def dot(a, b):
    return jnp.dot(a, b, preferred_element_type=F32)


def dot_t(a, b):
    return lax.dot_general(a, b, (((1,), (1,)), ((), ())), preferred_element_type=F32)


def left_half(shape):
    return lax.broadcasted_iota(jnp.int32, shape, 1) < HEAD_DIM


def swap(slab):
    return pltpu.roll(slab, HEAD_DIM, 1)


def per_head_sum(slab, left):
    low = jnp.sum(jnp.where(left, slab, 0.0), axis=-1, keepdims=True)
    high = jnp.sum(jnp.where(left, 0.0, slab), axis=-1, keepdims=True)
    return jnp.where(left, low, high)


def packed(near, far, left):
    rest = jnp.concatenate([far[LONG:], jnp.zeros((2 * LONG - TOK, 128), F32)], axis=0)
    return jnp.where(left[:LONG], near[:LONG], rest).astype(BF)


def unpacked_pair(low, high, left):
    low, high = low.astype(F32), high.astype(F32)
    top = jnp.where(left[:LONG], low, swap(high))
    rest = jnp.where(left[:LONG], swap(low), high)[: TOK - LONG]
    return jnp.concatenate([top, rest], axis=0)


def unit_scale(slab, left):
    return lax.rsqrt(per_head_sum(slab * slab, left) * (1.0 / HEAD_DIM) + EPSILON)


def place():
    me = lax.axis_index("seq")
    x, z = lax.rem(lax.div(me, 4), 4), lax.rem(me, 4)
    return ring_bits(lax.div(me, 16), x, z)


def ring_bits(y, x, z):
    return (y, lax.rem(lax.div(x + 1, 2), 2), lax.div(x, 2), lax.rem(lax.div(z + 1, 2), 2), lax.div(z, 2))


def neighbours():
    me = lax.axis_index("seq")
    x, z = lax.rem(lax.div(me, 4), 4), lax.rem(me, 4)
    return (
        lax.rem(me + 16, N_SEQ),
        me + 4 * (1 - 2 * lax.rem(x, 2)),
        me + 4 * (3 - 2 * x),
        me + 1 - 2 * lax.rem(z, 2),
        me + 3 - 2 * z,
    )


ALL_LINKS = tuple(tuple((first + step) % 5 for step in range(5)) for first in (0, 2, 4, 1, 3))
FLAT_FIRST = ((0, 1, 2, 3, 4), (1, 2, 0, 4, 3), (2, 0, 1, 3, 4))


def spread_out(counts):
    places = [(stream, 16 * row) for stream, count in enumerate(counts) for row in range(count)]
    return [16 * count for count in counts], places


Q_ROWS, Q_PLACES = spread_out((2, 1, 1, 2, 2))
KV_ROWS, KV_PLACES = spread_out((3, 3, 2, 4, 4))
OUT_ROWS, OUT_PLACES = spread_out((6, 5, 5))


def slot(order, owner, bits):
    y, x, z = owner // 16, owner // 4 % 4, owner % 4
    theirs = (y, (x + 1) // 2 % 2, x // 2, (z + 1) // 2 % 2, z // 2)
    at = 0
    for step, split in enumerate(order):
        apart = 1 - bits[split] if theirs[split] else bits[split]
        at = at + apart * (16 >> step)
    return at


class Halving:
    def __init__(self, refs, orders, near):
        count = len(orders)
        self.terms, self.acc, self.got = refs[:count], refs[count : 2 * count], refs[2 * count : 3 * count]
        self.send, self.recv = refs[3 * count :]
        self.orders, self.near, self.streams = orders, near, range(count)

    def hop(self, stream, step, part):
        half = 16 >> step
        first, size = (half // 2 * (1 - part), half // 2) if step < 4 else (0, 1)
        return pltpu.make_async_remote_copy(
            src_ref=(self.acc if step else self.terms)[stream].at[pl.ds(half + first, size)],
            dst_ref=self.got[stream].at[pl.ds(32 - (32 >> step) + first, size)],
            send_sem=self.send.at[stream, step, part],
            recv_sem=self.recv.at[stream, step, part],
            device_id={"seq": self.near[self.orders[stream][step]]},
            device_id_type=MESH,
        )

    def start(self, stream, step):
        for part in range(2 if step < 4 else 1):
            self.hop(stream, step, part).start()

    def add(self, stream, step, first, count):
        mine = (self.acc if step else self.terms)[stream]
        acc, got = self.acc[stream], self.got[stream]
        behind = 32 - (32 >> step)
        width = min(count, 4)

        def one(i, _):
            at = first + width * i
            total = mine[pl.ds(at, width)].astype(F32) + got[pl.ds(behind + at, width)].astype(F32)
            acc[pl.ds(at, width)] = total.astype(BF)
            return 0

        if count == width:
            one(0, 0)
        else:
            lax.fori_loop(0, count // width, one, 0)

    def advance(self, step):
        half = 8 >> step
        for stream in self.streams:
            self.hop(stream, step, 0).wait_recv()
            self.add(stream, step, half, half)
            self.start(stream, step + 1)
        for stream in self.streams:
            self.hop(stream, step, 1).wait_recv()
            self.add(stream, step, 0, half)

    def result(self, stream):
        self.hop(stream, 4, 0).wait_recv()
        return self.acc[stream][0].astype(F32) + self.got[stream][30].astype(F32)

    def drain(self):
        for step in range(5):
            for stream in self.streams:
                for part in range(2 if step < 4 else 1):
                    self.hop(stream, step, part).wait_send()


def halving_scratch(rows):
    return (
        [pltpu.VMEM((N_SEQ, count, 128), BF) for count in rows]
        + [pltpu.VMEM((16, count, 128), BF) for count in rows]
        + [pltpu.VMEM((31, count, 128), BF) for count in rows]
        + [pltpu.SemaphoreType.DMA((len(rows), 5, 2)), pltpu.SemaphoreType.DMA((len(rows), 5, 2))]
    )


def chunk_rows(index):
    return pl.ds(pl.multiple_of(index * TOK, 8), TOK)


def layer_body(*refs):
    refs = list(refs)

    def take(count):
        taken = refs[:count]
        del refs[:count]
        return taken

    act_in, up_in, wq_in, wk_in, wv_in, wo_in, ids = take(7)
    sum_q, sum_k, sum_v, sum_out, moved = take(5)
    act, up, wq, wk, wv, wo = take(6)
    normed, normed_turned, q_raw, k_raw, q_pack, kv_pack = take(6)
    kv, q_all, g_all, q_ids, out, inverse, att_all, att, att_turned, affine_grad, g_pack, carry_part = take(12)
    total, dkv, dq, dkv_all, dq_all, grads, gn, grad_input = take(8)
    padded_ids, q_end, tokens, summed, mass, q_turned, g_turned, correction = take(8)
    from_back, from_next, class_sum = take(2), take(2), take(2)
    far_half = take(2)
    q_in, g_in, out_pack = take(3)
    out_refs, q_refs, kv_refs = take(11), take(17), take(17)
    (load, kv_send, kv_recv, q_send, q_recv, z_send, z_recv, f_send, f_recv, att_send, att_recv,
     g_send, g_recv, dq_send, dq_recv, dkv_send, dkv_recv, local, carry_sem, back_send, back_recv) = refs

    me = lax.axis_index("seq")
    section = lax.axis_index("section")
    mine, group = lax.div(me, 4), lax.rem(me, 4)
    near, bits = neighbours(), place()
    across = N_SEQ - 1 - me
    before, after = lax.rem(section + 3, 4), lax.rem(section + 1, 4)
    z_next, z_back = 4 * mine + lax.rem(group + 1, 4), 4 * mine + lax.rem(group + 3, 4)

    loads = [
        pltpu.make_async_copy(source, target, load.at[i])
        for i, (source, target) in enumerate(
            ((act_in, act), (wq_in, wq), (wk_in, wk), (wv_in, wv), (wo_in, wo), (up_in, up))
        )
    ]
    for copy in loads:
        copy.start()

    barrier = pltpu.get_barrier_semaphore()

    def greet(k, _):
        peer = 4 * lax.rem(mine + k, HEADS) + group
        pl.semaphore_signal(barrier, inc=1, device_id={"seq": peer}, device_id_type=MESH)
        return 0

    lax.fori_loop(1, HEADS, greet, 0)
    for peer in (z_next, z_back):
        pl.semaphore_signal(barrier, inc=1, device_id={"seq": peer}, device_id_type=MESH)
    for other in (before, after):
        pl.semaphore_signal(barrier, inc=1, device_id={"section": other, "seq": across}, device_id_type=MESH)

    def remote(source, target, send, recv, peer):
        return pltpu.make_async_remote_copy(
            src_ref=source, dst_ref=target, send_sem=send, recv_sem=recv,
            device_id={"seq": peer}, device_id_type=MESH,
        )

    def loop(first, end, do):
        def one(k, c):
            do(k)
            return c

        lax.fori_loop(first, end, one, 0)

    left = left_half((TOK, 128))
    out_sum = Halving(out_refs, FLAT_FIRST, near)
    q_sum = Halving(q_refs, ALL_LINKS, near)
    kv_sum = Halving(kv_refs, ALL_LINKS, near)

    loads[0].wait()
    field = act[...].astype(F32)
    row_scale = lax.rsqrt(jnp.mean(field * field, axis=-1, keepdims=True) + EPSILON)
    normed[...] = (field * row_scale).astype(BF)
    for copy in loads[1:4]:
        copy.wait()
    for block in range(2):
        columns = pl.ds(256 * block, 256)
        q = dot(normed[...], wq[:, columns])
        k = dot(normed[...], wk[:, columns])
        v = dot(normed[...], wv[:, columns])
        q_raw[:, columns] = q
        k_raw[:, columns] = k
        for half in range(2):
            head = 4 * block + 2 * half
            q_slab = q[:, 128 * half : 128 * half + 128]
            k_slab = k[:, 128 * half : 128 * half + 128]
            v_slab = v[:, 128 * half : 128 * half + 128]
            q_slab = (q_slab * unit_scale(q_slab, left)).astype(BF).astype(F32) * 0.125
            k_slab = k_slab * unit_scale(k_slab, left)
            q_swap = swap(q_slab)
            q_pack[head] = packed(q_slab, q_swap, left)
            q_pack[head + 1] = packed(q_swap, q_slab, left)
            kv_pack[head] = jnp.where(left, k_slab, swap(v_slab)).astype(BF)
            kv_pack[head + 1] = jnp.where(left, swap(k_slab), v_slab).astype(BF)
    pl.semaphore_wait(barrier, HEADS + 3)

    def kv_copy(k):
        peer = lax.rem(mine + k, HEADS)
        return remote(kv_pack.at[peer], kv.at[0, chunk_rows(mine)], kv_send.at[k], kv_recv.at[k], 4 * peer + group)

    def q_copy(k):
        peer = lax.rem(mine + k, HEADS)
        return remote(q_pack.at[peer], q_in.at[mine], q_send.at[k], q_recv.at[k], 4 * peer + group)

    loop(1, HEADS, lambda k: kv_copy(k).start())
    own = [
        pltpu.make_async_copy(kv_pack.at[mine], kv.at[0, chunk_rows(mine)], local.at[0]),
        pltpu.make_async_copy(q_pack.at[mine], q_in.at[mine], local.at[1]),
    ]
    for copy in own:
        copy.start()
    loop(1, HEADS, lambda k: q_copy(k).start())
    for place_of in range(4):
        kv[place_of, CLASS:, :] = jnp.zeros((CLASS_ROWS - CLASS, 128), BF)
    own[0].wait()

    def z_copy(chunk, way):
        return remote(
            kv.at[0, chunk_rows(chunk)], kv.at[1 + way, chunk_rows(chunk)],
            z_send.at[way, chunk], z_recv.at[way, chunk], z_back if way else z_next,
        )

    def f_copy(chunk, way):
        return remote(
            kv.at[1 + way, chunk_rows(chunk)], kv.at[3, chunk_rows(chunk)],
            f_send.at[chunk], f_recv.at[chunk], z_back if way else z_next,
        )

    def relay(chunk):
        for way in range(2):
            z_copy(chunk, way).start()

    relay(mine)

    def pipe(k):
        kv_copy(k).wait_recv()
        relay(lax.rem(mine - k + HEADS, HEADS))

    loop(1, HEADS, pipe)

    turned = jnp.transpose(ids[...].astype(F32)).astype(jnp.int32)
    for row in range(TOKENS // 128):
        q_ids[128 * row : 128 * row + 128, :] = turned[:, row : row + 1]
    padded_ids[: TOKENS // 128, :] = ids[...]
    padded_ids[TOKENS // 128 :, :] = jnp.full((40 - TOKENS // 128, 128), TOKENS, jnp.int32)
    for chunk in range(HEADS):
        first = pl.multiple_of((4 * chunk + group) * TOK, 8)
        row = lax.div(first, 128)
        column = q_ids[pl.ds(first, TOK), :]
        seen = jnp.zeros((TOK, 128), F32)
        for behind in range(5):
            seen = seen + jnp.where(padded_ids[pl.ds(row + behind, 1), :] <= column, 1.0, 0.0)
        count = jnp.sum(seen, axis=-1, keepdims=True).astype(jnp.int32)
        q_end[TOK * chunk : TOK * chunk + TOK, :] = count + 128 * row
    lane = lax.broadcasted_iota(jnp.int32, (1, CLASS_ROWS), 1)
    skipped = jnp.zeros((1, CLASS_ROWS), jnp.int32)
    for chunk in range(1, HEADS + 1):
        skipped = skipped + jnp.where(lane >= TOK * chunk, 3 * TOK, 0)
    for place_of, apart in enumerate((0, 3, 1, 2)):
        tokens[place_of] = lane + skipped + TOK * lax.rem(group + apart, 4)
    for block in range(8):
        at = pl.ds(128 * block, 128)
        normed_turned[at, :] = jnp.transpose(normed[:, at].astype(F32)).astype(BF)
    own[1].wait()
    loop(1, HEADS, lambda k: q_copy(k).wait_recv())
    short = left[:LONG]
    for a in range(4):
        parts = []
        for chunk in (2 * a, 2 * a + 1):
            q = q_in[chunk].astype(F32)
            parts += [jnp.where(short, q, 0.0), jnp.where(short, swap(q), 0.0)[: TOK - LONG]]
        q_all[2 * TOK * a : 2 * TOK * (a + 1), :] = jnp.concatenate(parts, axis=0).astype(BF)

    def tiles(a):
        whole = [(512 * part, min(512, 256 * a - 512 * part), False) for part in range(-(-a // 2))]
        return whole + [(256 * a, 384 if a == 3 else 512, True)]

    def pair_rows(a):
        return pl.ds(2 * TOK * a, 2 * TOK)

    def shown(a, place_of, first, width):
        return tokens[place_of][:, first : first + width] < q_end[pair_rows(a), :]

    def att_copy(chunk):
        k = lax.rem(chunk - mine + HEADS, HEADS)
        return remote(out_pack.at[chunk], att_all.at[mine], att_send.at[k], att_recv.at[k], 4 * chunk + group)

    summed[...] = jnp.zeros_like(summed)
    mass[...] = jnp.zeros_like(mass)

    def attend(place_of):
        @pl.when(place_of == 1)
        def _():
            def pass_on(chunk):
                z_copy(chunk, 0).wait_recv()
                f_copy(chunk, 0).start()
                z_copy(chunk + 4, 1).wait_recv()
                f_copy(chunk + 4, 1).start()

            loop(0, 4, pass_on)
            loop(4, 8, lambda chunk: z_copy(chunk, 0).wait_recv())

        @pl.when(place_of == 2)
        def _():
            loop(0, 4, lambda chunk: z_copy(chunk, 1).wait_recv())

        add_class(place_of, None)

    def add_class(place_of, then):
        for a in range(4):
            rows = pair_rows(a)
            q = q_all[rows, :]
            for first, width, masked in tiles(a):
                block = kv[place_of, first : first + width, :]
                p = jnp.exp(dot_t(q, block))
                if masked:
                    p = jnp.where(shown(a, place_of, first, width), p, 0.0)
                part_mass = p[:, :128]
                for part in range(1, width // 128):
                    part_mass = part_mass + p[:, 128 * part : 128 * part + 128]
                mass[rows, :] += part_mass
                summed[rows, :] += dot(p.astype(BF), block)
            if then is not None:
                then(a)

    def hand_over(a):
        rows = pair_rows(a)
        one_over = 1.0 / jnp.sum(mass[rows, :], axis=-1, keepdims=True)
        result = summed[rows, :] * one_over
        out[rows, :] = result.astype(BF)
        inverse[rows, :] = one_over
        for half in range(2):
            chunk = 2 * a + half
            value = result[TOK * half : TOK * half + TOK]
            out_pack[chunk] = packed(swap(value), value, left)

            @pl.when(mine != chunk)
            def _():
                att_copy(chunk).start()

            @pl.when(mine == chunk)
            def _():
                pltpu.make_async_copy(out_pack.at[chunk], att_all.at[mine], local.at[0]).start()

    loop(0, 3, attend)
    loop(0, 4, lambda chunk: (f_copy(chunk, 0).wait_recv(), f_copy(chunk + 4, 1).wait_recv()))
    add_class(3, hand_over)

    loads[4].wait()
    loads[5].wait()
    pltpu.make_async_copy(out_pack.at[mine], att_all.at[mine], local.at[0]).wait()

    def att_arrived(k):
        peer = lax.rem(mine + k, HEADS)
        att_copy(peer).wait_recv()

    loop(1, HEADS, att_arrived)
    for pair in range(HEADS // 2):
        slab = unpacked_pair(att_all[2 * pair], att_all[2 * pair + 1], left)
        att[:, 128 * pair : 128 * pair + 128] = slab.astype(BF)
        att_turned[128 * pair : 128 * pair + 128, :] = jnp.transpose(slab).astype(BF)
    for block in range(4):
        columns = pl.ds(256 * block, 256)
        behind = pl.ds(D + 256 * block, 256)
        shift = dot(att[...], wo[:, columns])
        factor = jnp.exp(-dot(att[...], wo[:, behind]))
        upstream = up[:, columns].astype(F32)
        latent = (act[:, columns].astype(F32) - shift) * factor
        scaled = upstream * factor
        carry_part[:, columns] = scaled
        affine_grad[:, columns] = (-scaled).astype(BF)
        affine_grad[:, behind] = (1.0 - upstream * latent).astype(BF)

    def g_copy(head):
        k = lax.rem(head - mine + HEADS, HEADS)
        return remote(g_pack.at[head], g_in.at[mine], g_send.at[k], g_recv.at[k], 4 * head + group)

    def g_own():
        return pltpu.make_async_copy(g_pack.at[mine], g_in.at[mine], local.at[1])

    for block in range(2):
        g = dot_t(affine_grad[...], wo[pl.ds(256 * block, 256), :])
        for half in range(2):
            head = 4 * block + 2 * half
            slab = g[:, 128 * half : 128 * half + 128]
            turned_slab = swap(slab)
            g_pack[head] = packed(slab, turned_slab, left)
            g_pack[head + 1] = packed(turned_slab, slab, left)
        for head in range(4 * block, 4 * block + 4):

            @pl.when(mine != head)
            def _():
                g_copy(head).start()

    g_own().start()
    for block in range(8):
        columns = pl.ds(256 * block, 256)
        term = dot(att_turned[...], affine_grad[:, columns]).astype(BF)
        for owner in range(N_SEQ):
            for half in range(2):
                stream, row = OUT_PLACES[2 * block + half]
                out_sum.terms[stream][slot(FLAT_FIRST[stream], owner, bits), row : row + 16, :] = term[
                    16 * owner : 16 * owner + 16, 128 * half : 128 * half + 128
                ]
    for stream in out_sum.streams:
        out_sum.start(stream, 0)

    for a in range(4):
        q_turned[a] = jnp.transpose(q_all[pair_rows(a), :].astype(F32))[:HEAD_DIM].astype(BF)
    g_own().wait()
    loop(1, HEADS, lambda k: g_copy(lax.rem(mine + k, HEADS)).wait_recv())

    for a in range(4):
        rows = pair_rows(a)
        parts = []
        for chunk in (2 * a, 2 * a + 1):
            g = g_in[chunk].astype(F32)
            parts += [jnp.where(short, 0.0, swap(g)), jnp.where(short, 0.0, g)[: TOK - LONG]]
        g = jnp.concatenate(parts, axis=0)
        g_all[rows, :] = g.astype(BF)
        correction[rows, :] = jnp.sum(g * out[rows, :].astype(F32), axis=-1, keepdims=True)
        g_turned[a] = jnp.transpose(g)[HEAD_DIM:].astype(BF)
    summed[...] = jnp.zeros_like(summed)

    def dq_copy(chunk):
        k = lax.rem(chunk - mine + HEADS, HEADS)
        return remote(dq.at[chunk], dq_all.at[mine], dq_send.at[k], dq_recv.at[k], 4 * chunk + group)

    def dq_own():
        return pltpu.make_async_copy(dq.at[mine], dq_all.at[mine], local.at[2])

    def far_copy(way):
        return remote(
            class_sum[way].at[2], far_half[way], back_send.at[way], back_recv.at[way], z_back if way else z_next
        )

    def class_copy(place_of, half):
        at = 2 * place_of + half
        target, peer = (from_next, z_back) if place_of == 1 else (from_back, z_next)
        return remote(class_sum[half].at[place_of - 1], target[half], back_send.at[at], back_recv.at[at], peer)

    def dkv_copy(k):
        peer = lax.rem(mine + k, HEADS)
        return remote(dkv.at[chunk_rows(peer)], dkv_all.at[mine], dkv_send.at[k], dkv_recv.at[k], 4 * peer + group)

    def dkv_own():
        return pltpu.make_async_copy(dkv.at[chunk_rows(mine)], dkv_all.at[mine], local.at[3])

    def send_keys(chunk):
        @pl.when(mine != chunk)
        def _():
            dkv_copy(lax.rem(chunk - mine + HEADS, HEADS)).start()

        @pl.when(mine == chunk)
        def _():
            dkv_own().start()

    columns_of = (slice(0, LOW), slice(LOW, CLASS_ROWS))

    def settle(place_of, half, extra):
        value = total[:, columns_of[half]]
        if extra is not None:
            value = value + extra[...].astype(F32)
        class_sum[half][place_of - 1] = value.astype(BF)

    def settle_own(half):
        for first in range(0, LOW, 128) if half == 0 else range(LOW, CLASS, 128):
            begin = first - LOW * half
            at = slice(begin, begin + 128)
            value = total[:, first : first + 128]
            value = value + from_back[half][:, at].astype(F32) + from_next[half][:, at].astype(F32)
            width = min(128, CLASS - first)
            dkv[first : first + width, :] = jnp.transpose(value)[:width].astype(BF)

    def spans(a, half):
        low, high = ((0, LOW), (LOW, CLASS_ROWS))[half]
        cut = min(max(256 * a, low), high)
        end = min(256 * a + (384 if a == 3 else 512), high)
        return [(low, cut - low, False)] * (cut > low) + [(cut, end - cut, True)] * (end > cut)

    def back_class(place_of, half, then):
        spread = {0: (0, LOW), 1: (LOW, CLASS_ROWS), None: (0, CLASS_ROWS)}[half]
        total[:, spread[0] : spread[1]] = jnp.zeros((128, spread[1] - spread[0]), F32)
        for a in (3, 2, 1, 0):
            rows = pair_rows(a)
            q = q_all[rows, :]
            g = g_all[rows, :]
            one_over = inverse[rows, :]
            corr = correction[rows, :]
            pieces = tiles(a) if half is None else spans(a, half)
            if pieces:
                first = pieces[0][0]
                width = sum(piece[1] for piece in pieces)
                block = kv[place_of, first : first + width, :]
                p = jnp.exp(dot_t(q, block)) * one_over
                parts = []
                for begin, size, masked in pieces:
                    part = p[:, begin - first : begin - first + size]
                    parts.append(jnp.where(shown(a, place_of, begin, size), part, 0.0) if masked else part)
                p = jnp.concatenate(parts, axis=1) if len(parts) > 1 else parts[0]
                ds = (p * (dot_t(g, block) - corr)).astype(BF)
                total[:HEAD_DIM, first : first + width] += dot(q_turned[a], ds)
                total[HEAD_DIM:, first : first + width] += dot(g_turned[a], p.astype(BF))
                summed[rows, :] += dot(ds, block)
            if then is not None:
                then(a)

    def send_dq(a):
        result = summed[pair_rows(a), :] * 0.125
        for half in range(2):
            chunk = 2 * a + half
            value = result[TOK * half : TOK * half + TOK]
            dq[chunk] = packed(value, swap(value), left)

            @pl.when(mine != chunk)
            def _():
                dq_copy(chunk).start()

            @pl.when(mine == chunk)
            def _():
                dq_own().start()

    back_class(3, None, None)
    settle(3, 0, None)
    far_copy(0).start()
    settle(3, 1, None)
    far_copy(1).start()
    back_class(1, 0, None)
    settle(1, 0, None)
    class_copy(1, 0).start()
    back_class(2, 1, None)
    settle(2, 1, None)
    class_copy(2, 1).start()
    back_class(2, 0, None)
    far_copy(0).wait_recv()
    settle(2, 0, far_half[0])
    class_copy(2, 0).start()
    out_sum.advance(0)
    back_class(1, 1, None)
    far_copy(1).wait_recv()
    settle(1, 1, far_half[1])
    class_copy(1, 1).start()
    back_class(0, None, send_dq)
    for half in (1, 0):
        for place_of in (2, 1):
            class_copy(place_of, half).wait_recv()
        settle_own(half)
        for chunk in range(4, 8) if half else range(4):
            send_keys(chunk)
    out_sum.advance(1)

    def unit_back(grad, raw):
        scale = unit_scale(raw, left)
        unit = raw * scale
        return scale * (grad - unit * (per_head_sum(grad * unit, left) * (1.0 / HEAD_DIM)))

    def keys_of(head):
        return dkv_all[head].astype(F32)

    def term_of(which):
        places, into, first = (Q_PLACES, q_sum, 0) if which == 0 else (KV_PLACES, kv_sum, 8 * (2 - which))
        for block in range(2):
            term = dot(normed_turned[...], grads[which, :, 256 * block : 256 * block + 256]).astype(BF)
            for owner in range(N_SEQ):
                for part in range(4):
                    slab, half = part // 2, part % 2
                    stream, row = places[first + 4 * block + 2 * slab + half]
                    top = 32 * owner + 16 * half
                    into.terms[stream][slot(ALL_LINKS[stream], owner, bits), row : row + 16, :] = term[
                        top : top + 16, 128 * slab : 128 * slab + 128
                    ]

    dq_own().wait()
    loop(1, HEADS, lambda k: dq_copy(lax.rem(mine + k, HEADS)).wait_recv())
    for pair in range(HEADS // 2):
        at = pl.ds(128 * pair, 128)
        q_grad = unpacked_pair(dq_all[2 * pair], dq_all[2 * pair + 1], left)
        grads[0, :, at] = unit_back(q_grad, q_raw[:, at]).astype(BF)
    term_of(0)
    for stream in range(5):
        q_sum.start(stream, 0)
    out_sum.advance(2)
    for block in range(4):
        at = pl.ds(256 * block, 256)
        gn[:, at] = dot_t(grads[0], wq[at, :])
    dkv_own().wait()
    loop(1, HEADS, lambda k: dkv_copy(k).wait_recv())
    for pair in range(HEADS // 2):
        low, high = keys_of(2 * pair), keys_of(2 * pair + 1)
        grads[2, :, 128 * pair : 128 * pair + 128] = jnp.where(left, swap(low), high).astype(BF)
    term_of(2)
    for stream in range(3):
        kv_sum.start(stream, 0)
    for pair in range(HEADS // 2):
        at = pl.ds(128 * pair, 128)
        low, high = keys_of(2 * pair), keys_of(2 * pair + 1)
        grads[1, :, at] = unit_back(jnp.where(left, low, swap(high)), k_raw[:, at]).astype(BF)
    term_of(1)
    for stream in range(3, 5):
        kv_sum.start(stream, 0)
    q_sum.advance(0)
    out_sum.advance(3)
    for block in range(4):
        at = pl.ds(256 * block, 256)
        gn[:, at] += dot_t(grads[1], wk[at, :]) + dot_t(grads[2], wv[at, :])
    field = act[...].astype(F32)
    row_scale = lax.rsqrt(jnp.mean(field * field, axis=-1, keepdims=True) + EPSILON)
    unit = field * row_scale
    grad_normed = gn[...]
    mean = jnp.mean(grad_normed * unit, axis=-1, keepdims=True)
    grad_input[...] = (carry_part[...] + row_scale * (grad_normed - unit * mean)).astype(BF)

    def carry(piece):
        first, count = ((0, 48), (48, 32), (80, 32), (112, 24))[piece]
        rows = pl.ds(first, count)
        return pltpu.make_async_remote_copy(
            src_ref=grad_input.at[rows], dst_ref=moved.at[rows], send_sem=carry_sem.at[0, piece],
            recv_sem=carry_sem.at[1, piece], device_id={"section": before, "seq": across}, device_id_type=MESH,
        )

    carry(0).start()
    q_sum.advance(1)
    kv_sum.advance(0)
    carry(1).start()
    q_sum.advance(2)
    for stream in out_sum.streams:
        result = out_sum.result(stream)
        for part in range(16):
            if OUT_PLACES[part][0] == stream:
                row = OUT_PLACES[part][1]
                sum_out[:, 128 * part : 128 * part + 128] = result[row : row + 16]
    kv_sum.advance(1)
    carry(2).start()
    carry(3).start()
    q_sum.advance(3)

    def deliver(halving, places, targets):
        for stream in range(5):
            result = halving.result(stream)
            for part in range(8 * len(targets)):
                if places[part][0] == stream:
                    row = places[part][1]
                    column, top = 128 * (part % 8 // 2), 16 * (part % 2)
                    targets[part // 8][top : top + 16, column : column + 128] = result[row : row + 16]

    kv_sum.advance(2)
    deliver(q_sum, Q_PLACES, (sum_q,))
    kv_sum.advance(3)
    deliver(kv_sum, KV_PLACES, (sum_v, sum_k))
    for piece in range(4):
        carry(piece).wait()

    def left_all(k):
        kv_copy(k).wait_send()
        q_copy(k).wait_send()
        att_copy(lax.rem(mine + k, HEADS)).wait_send()
        g_copy(lax.rem(mine + k, HEADS)).wait_send()
        dq_copy(lax.rem(mine + k, HEADS)).wait_send()
        dkv_copy(k).wait_send()

    loop(1, HEADS, left_all)

    def left_z(chunk):
        for way in range(2):
            z_copy(chunk, way).wait_send()

    loop(0, HEADS, left_z)
    loop(0, 4, lambda chunk: (f_copy(chunk, 0).wait_send(), f_copy(chunk + 4, 1).wait_send()))
    for way in range(2):
        far_copy(way).wait_send()
        for place_of in (1, 2):
            class_copy(place_of, way).wait_send()
    out_sum.drain()
    q_sum.drain()
    kv_sum.drain()


def whole_layer(*operands):
    eight, full, short = (HEADS * TOK, 128), (TOK, D), (HEADS, LONG, 128)
    low, high = (128, LOW), (128, CLASS_ROWS - LOW)
    scratch = [
        (full, BF), (full, BF), ((D, INNER), BF), ((D, INNER), BF), ((D, INNER), BF), ((INNER, 2 * D), BF),
        (full, BF), ((D, TOK), BF), ((TOK, INNER), F32), ((TOK, INNER), F32), (short, BF), ((HEADS, TOK, 128), BF),
        ((4, CLASS_ROWS, 128), BF), (eight, BF), (eight, BF), ((TOKENS, 1), jnp.int32), (eight, BF), ((CLASS, 1), F32),
        (short, BF), ((TOK, INNER), BF), ((INNER, TOK), BF), ((TOK, 2 * D), BF), (short, BF), (full, F32),
        ((128, CLASS_ROWS), F32), (eight, BF), (short, BF), ((HEADS, TOK, 128), BF), (short, BF),
        ((3, TOK, INNER), BF), (full, F32), (full, BF),
        ((40, 128), jnp.int32), ((CLASS, 1), jnp.int32), ((4, 1, CLASS_ROWS), jnp.int32), (eight, F32), (eight, F32),
        ((4, HEAD_DIM, 2 * TOK), BF), ((4, HEAD_DIM, 2 * TOK), BF), ((CLASS, 1), F32),
        (low, BF), (high, BF), (low, BF), (high, BF), ((3, *low), BF), ((3, *high), BF),
        (low, BF), (high, BF), (short, BF), (short, BF), (short, BF),
    ]
    dma = pltpu.SemaphoreType.DMA
    return pl.pallas_call(
        layer_body,
        out_shape=[jax.ShapeDtypeStruct((32, INNER), F32)] * 3
        + [jax.ShapeDtypeStruct((16, 2 * D), F32), jax.ShapeDtypeStruct((TOK, D), BF)],
        in_specs=[ANY] * 6 + [VMEM],
        out_specs=[VMEM] * 5,
        scratch_shapes=[pltpu.VMEM(shape, dtype) for shape, dtype in scratch]
        + halving_scratch(OUT_ROWS)
        + halving_scratch(Q_ROWS)
        + halving_scratch(KV_ROWS)
        + [dma((6,)), dma((8,)), dma((8,)), dma((8,)), dma((8,)), dma((2, 8)), dma((2, 8)), dma((8,)), dma((8,))]
        + [dma((8,))] * 8
        + [dma((4,)), dma((2, 4)), dma((6,)), dma((6,))],
        compiler_params=pltpu.CompilerParams(collective_id=1, has_side_effects=True, vmem_limit_bytes=BIG),
        name="layer",
    )(*operands)


def hand_out_body(sum_q, sum_k, sum_v, sum_out, moved, flip, carry, out_q, out_k, out_v, out_out):
    out_q[...] = sum_q[...]
    out_k[...] = sum_k[...]
    out_v[...] = sum_v[...]
    out_out[...] = sum_out[...]
    turned = (flip[...] == lax.broadcasted_iota(jnp.int32, (TOK, TOK), 0)).astype(F32)
    chosen = jnp.transpose(turned).astype(BF)
    last = (lax.axis_index("section") + jnp.zeros((TOK, 1), jnp.int32)) == 3
    for block in range(4):
        at = pl.ds(256 * block, 256)
        carry[:, at] = jnp.where(last, 0.0, dot(chosen, moved[:, at])).astype(BF)


def hand_out(*operands):
    return pl.pallas_call(
        hand_out_body,
        out_shape=[jax.ShapeDtypeStruct((TOK, D), BF)]
        + [jax.ShapeDtypeStruct((32, INNER), F32)] * 3
        + [jax.ShapeDtypeStruct((16, 2 * D), F32)],
        in_specs=[VMEM] * 6,
        out_specs=[VMEM] * 5,
        name="hand_out",
    )(*operands)


def shards(activations, incoming, w_query, w_key, w_value, w_out, block_ids, flip_order):
    sums = whole_layer(
        activations[0], incoming[0], w_query[0], w_key[0], w_value[0], w_out[0], block_ids.reshape(TOKENS // 128, 128)
    )
    results = hand_out(*sums, flip_order)
    return tuple(result[None] for result in results)


def solution(mesh):
    by_both = P("section", "seq", None)
    by_layer = P("section", None, None)
    in_specs = (by_both, by_both, by_layer, by_layer, by_layer, by_layer, P(), P("section", None))
    return jax.shard_map(shards, mesh=mesh, in_specs=in_specs, out_specs=(by_both,) * 5, check_vma=False)
```

```python
import jax
import jax.numpy as jnp
from jax import lax
from jax.experimental import pallas as pl
from jax.experimental.pallas import tpu as pltpu
from jax.sharding import PartitionSpec as P

HEADS = 8
HEAD_DIM = 64
EPSILON = 1e-06
N_SEQ = 32
TOK = 136
TOKENS = 4352
D = 1024
INNER = 512
CLASS = 8 * TOK
CLASS_ROWS = 1152
LOW = 512
LONG = 80
BF = jnp.bfloat16
F32 = jnp.float32
MESH = pl.DeviceIdType.MESH
VMEM = pl.BlockSpec(memory_space=pltpu.VMEM)
ANY = pl.BlockSpec(memory_space=pl.ANY)
BIG = 60 * 1024 * 1024


def dot(a, b):
    return jnp.dot(a, b, preferred_element_type=F32)


def dot_t(a, b):
    return lax.dot_general(a, b, (((1,), (1,)), ((), ())), preferred_element_type=F32)


def left_half(shape):
    return lax.broadcasted_iota(jnp.int32, shape, 1) < HEAD_DIM


def swap(slab):
    return pltpu.roll(slab, HEAD_DIM, 1)


def per_head_sum(slab, left):
    low = jnp.sum(jnp.where(left, slab, 0.0), axis=-1, keepdims=True)
    high = jnp.sum(jnp.where(left, 0.0, slab), axis=-1, keepdims=True)
    return jnp.where(left, low, high)


def packed(near, far, left):
    rest = jnp.concatenate([far[LONG:], jnp.zeros((2 * LONG - TOK, 128), F32)], axis=0)
    return jnp.where(left[:LONG], near[:LONG], rest).astype(BF)


def unpacked_pair(low, high, left):
    low, high = low.astype(F32), high.astype(F32)
    top = jnp.where(left[:LONG], low, swap(high))
    rest = jnp.where(left[:LONG], swap(low), high)[: TOK - LONG]
    return jnp.concatenate([top, rest], axis=0)


def unit_scale(slab, left):
    return lax.rsqrt(per_head_sum(slab * slab, left) * (1.0 / HEAD_DIM) + EPSILON)


def place():
    me = lax.axis_index("seq")
    x, z = lax.rem(lax.div(me, 4), 4), lax.rem(me, 4)
    return ring_bits(lax.div(me, 16), x, z)


def ring_bits(y, x, z):
    return (y, lax.rem(lax.div(x + 1, 2), 2), lax.div(x, 2), lax.rem(lax.div(z + 1, 2), 2), lax.div(z, 2))


def neighbours():
    me = lax.axis_index("seq")
    x, z = lax.rem(lax.div(me, 4), 4), lax.rem(me, 4)
    return (
        lax.rem(me + 16, N_SEQ),
        me + 4 * (1 - 2 * lax.rem(x, 2)),
        me + 4 * (3 - 2 * x),
        me + 1 - 2 * lax.rem(z, 2),
        me + 3 - 2 * z,
    )


ALL_LINKS = tuple(tuple((first + step) % 5 for step in range(5)) for first in (0, 2, 4, 1, 3))
FLAT_FIRST = ((0, 1, 2, 3, 4), (1, 2, 0, 4, 3), (2, 0, 1, 3, 4))


def spread_out(counts):
    places = [(stream, 16 * row) for stream, count in enumerate(counts) for row in range(count)]
    return [16 * count for count in counts], places


Q_ROWS, Q_PLACES = spread_out((2, 1, 1, 2, 2))
KV_ROWS, KV_PLACES = spread_out((3, 3, 2, 4, 4))
OUT_ROWS, OUT_PLACES = spread_out((6, 5, 5))


def slot(order, owner, bits):
    y, x, z = owner // 16, owner // 4 % 4, owner % 4
    theirs = (y, (x + 1) // 2 % 2, x // 2, (z + 1) // 2 % 2, z // 2)
    at = 0
    for step, split in enumerate(order):
        apart = 1 - bits[split] if theirs[split] else bits[split]
        at = at + apart * (16 >> step)
    return at


class Halving:
    def __init__(self, refs, orders, near):
        count = len(orders)
        self.terms, self.acc, self.got = refs[:count], refs[count : 2 * count], refs[2 * count : 3 * count]
        self.send, self.recv = refs[3 * count :]
        self.orders, self.near, self.streams = orders, near, range(count)

    def hop(self, stream, step, part):
        half = 16 >> step
        first, size = (half // 2 * (1 - part), half // 2) if step < 4 else (0, 1)
        return pltpu.make_async_remote_copy(
            src_ref=(self.acc if step else self.terms)[stream].at[pl.ds(half + first, size)],
            dst_ref=self.got[stream].at[pl.ds(32 - (32 >> step) + first, size)],
            send_sem=self.send.at[stream, step, part],
            recv_sem=self.recv.at[stream, step, part],
            device_id={"seq": self.near[self.orders[stream][step]]},
            device_id_type=MESH,
        )

    def start(self, stream, step):
        for part in range(2 if step < 4 else 1):
            self.hop(stream, step, part).start()

    def add(self, stream, step, first, count):
        mine = (self.acc if step else self.terms)[stream]
        acc, got = self.acc[stream], self.got[stream]
        behind = 32 - (32 >> step)
        width = min(count, 4)

        def one(i, _):
            at = first + width * i
            total = mine[pl.ds(at, width)].astype(F32) + got[pl.ds(behind + at, width)].astype(F32)
            acc[pl.ds(at, width)] = total.astype(BF)
            return 0

        if count == width:
            one(0, 0)
        else:
            lax.fori_loop(0, count // width, one, 0)

    def advance(self, step):
        half = 8 >> step
        for stream in self.streams:
            self.hop(stream, step, 0).wait_recv()
            self.add(stream, step, half, half)
            self.start(stream, step + 1)
        for stream in self.streams:
            self.hop(stream, step, 1).wait_recv()
            self.add(stream, step, 0, half)

    def result(self, stream):
        self.hop(stream, 4, 0).wait_recv()
        return self.acc[stream][0].astype(F32) + self.got[stream][30].astype(F32)

    def drain(self):
        for step in range(5):
            for stream in self.streams:
                for part in range(2 if step < 4 else 1):
                    self.hop(stream, step, part).wait_send()


def halving_scratch(rows):
    return (
        [pltpu.VMEM((N_SEQ, count, 128), BF) for count in rows]
        + [pltpu.VMEM((16, count, 128), BF) for count in rows]
        + [pltpu.VMEM((31, count, 128), BF) for count in rows]
        + [pltpu.SemaphoreType.DMA((len(rows), 5, 2)), pltpu.SemaphoreType.DMA((len(rows), 5, 2))]
    )


def chunk_rows(index):
    return pl.ds(pl.multiple_of(index * TOK, 8), TOK)


def layer_body(*refs):
    refs = list(refs)

    def take(count):
        taken = refs[:count]
        del refs[:count]
        return taken

    act_in, up_in, wq_in, wk_in, wv_in, wo_in, ids = take(7)
    sum_q, sum_k, sum_v, sum_out, moved = take(5)
    act, up, wq, wk, wv, wo = take(6)
    normed, normed_turned, q_raw, k_raw, q_pack, kv_pack = take(6)
    kv, q_all, g_all, q_ids, out, inverse, att_all, att, att_turned, affine_grad, g_pack, carry_part = take(12)
    total, dkv, dq, dkv_all, dq_all, grads, gn, grad_input = take(8)
    padded_ids, q_end, tokens, summed, mass, q_turned, g_turned, correction = take(8)
    from_back, from_next, class_sum = take(2), take(2), take(2)
    far_half = take(2)
    q_in, g_in, out_pack = take(3)
    out_refs, q_refs, kv_refs = take(11), take(17), take(17)
    (load, kv_send, kv_recv, q_send, q_recv, z_send, z_recv, f_send, f_recv, att_send, att_recv,
     g_send, g_recv, dq_send, dq_recv, dkv_send, dkv_recv, local, carry_sem, back_send, back_recv) = refs

    me = lax.axis_index("seq")
    section = lax.axis_index("section")
    mine, group = lax.div(me, 4), lax.rem(me, 4)
    near, bits = neighbours(), place()
    across = N_SEQ - 1 - me
    before, after = lax.rem(section + 3, 4), lax.rem(section + 1, 4)
    z_next, z_back = 4 * mine + lax.rem(group + 1, 4), 4 * mine + lax.rem(group + 3, 4)

    loads = [
        pltpu.make_async_copy(source, target, load.at[i])
        for i, (source, target) in enumerate(
            ((act_in, act), (wq_in, wq), (wk_in, wk), (wv_in, wv), (wo_in, wo), (up_in, up))
        )
    ]
    for copy in loads:
        copy.start()

    barrier = pltpu.get_barrier_semaphore()

    def greet(k, _):
        peer = 4 * lax.rem(mine + k, HEADS) + group
        pl.semaphore_signal(barrier, inc=1, device_id={"seq": peer}, device_id_type=MESH)
        return 0

    lax.fori_loop(1, HEADS, greet, 0)
    for peer in (z_next, z_back):
        pl.semaphore_signal(barrier, inc=1, device_id={"seq": peer}, device_id_type=MESH)
    for other in (before, after):
        pl.semaphore_signal(barrier, inc=1, device_id={"section": other, "seq": across}, device_id_type=MESH)

    def remote(source, target, send, recv, peer):
        return pltpu.make_async_remote_copy(
            src_ref=source, dst_ref=target, send_sem=send, recv_sem=recv,
            device_id={"seq": peer}, device_id_type=MESH,
        )

    def loop(first, end, do):
        def one(k, c):
            do(k)
            return c

        lax.fori_loop(first, end, one, 0)

    left = left_half((TOK, 128))
    out_sum = Halving(out_refs, FLAT_FIRST, near)
    q_sum = Halving(q_refs, ALL_LINKS, near)
    kv_sum = Halving(kv_refs, ALL_LINKS, near)

    loads[0].wait()
    field = act[...].astype(F32)
    row_scale = lax.rsqrt(jnp.mean(field * field, axis=-1, keepdims=True) + EPSILON)
    normed[...] = (field * row_scale).astype(BF)
    for copy in loads[1:4]:
        copy.wait()
    for block in range(2):
        columns = pl.ds(256 * block, 256)
        q = dot(normed[...], wq[:, columns])
        k = dot(normed[...], wk[:, columns])
        v = dot(normed[...], wv[:, columns])
        q_raw[:, columns] = q
        k_raw[:, columns] = k
        for half in range(2):
            head = 4 * block + 2 * half
            q_slab = q[:, 128 * half : 128 * half + 128]
            k_slab = k[:, 128 * half : 128 * half + 128]
            v_slab = v[:, 128 * half : 128 * half + 128]
            q_slab = (q_slab * unit_scale(q_slab, left)).astype(BF).astype(F32) * 0.125
            k_slab = k_slab * unit_scale(k_slab, left)
            q_swap = swap(q_slab)
            q_pack[head] = packed(q_slab, q_swap, left)
            q_pack[head + 1] = packed(q_swap, q_slab, left)
            kv_pack[head] = jnp.where(left, k_slab, swap(v_slab)).astype(BF)
            kv_pack[head + 1] = jnp.where(left, swap(k_slab), v_slab).astype(BF)
    pl.semaphore_wait(barrier, HEADS + 3)

    def kv_copy(k):
        peer = lax.rem(mine + k, HEADS)
        return remote(kv_pack.at[peer], kv.at[0, chunk_rows(mine)], kv_send.at[k], kv_recv.at[k], 4 * peer + group)

    def q_copy(k):
        peer = lax.rem(mine + k, HEADS)
        return remote(q_pack.at[peer], q_in.at[mine], q_send.at[k], q_recv.at[k], 4 * peer + group)

    loop(1, HEADS, lambda k: kv_copy(k).start())
    own = [
        pltpu.make_async_copy(kv_pack.at[mine], kv.at[0, chunk_rows(mine)], local.at[0]),
        pltpu.make_async_copy(q_pack.at[mine], q_in.at[mine], local.at[1]),
    ]
    for copy in own:
        copy.start()
    loop(1, HEADS, lambda k: q_copy(k).start())
    for place_of in range(4):
        kv[place_of, CLASS:, :] = jnp.zeros((CLASS_ROWS - CLASS, 128), BF)
    own[0].wait()

    def z_copy(chunk, way):
        return remote(
            kv.at[0, chunk_rows(chunk)], kv.at[1 + way, chunk_rows(chunk)],
            z_send.at[way, chunk], z_recv.at[way, chunk], z_back if way else z_next,
        )

    def f_copy(chunk, way):
        return remote(
            kv.at[1 + way, chunk_rows(chunk)], kv.at[3, chunk_rows(chunk)],
            f_send.at[chunk], f_recv.at[chunk], z_back if way else z_next,
        )

    def relay(chunk):
        for way in range(2):
            z_copy(chunk, way).start()

    relay(mine)

    def pipe(k):
        kv_copy(k).wait_recv()
        relay(lax.rem(mine - k + HEADS, HEADS))

    loop(1, HEADS, pipe)

    turned = jnp.transpose(ids[...].astype(F32)).astype(jnp.int32)
    for row in range(TOKENS // 128):
        q_ids[128 * row : 128 * row + 128, :] = turned[:, row : row + 1]
    padded_ids[: TOKENS // 128, :] = ids[...]
    padded_ids[TOKENS // 128 :, :] = jnp.full((40 - TOKENS // 128, 128), TOKENS, jnp.int32)
    for chunk in range(HEADS):
        first = pl.multiple_of((4 * chunk + group) * TOK, 8)
        row = lax.div(first, 128)
        column = q_ids[pl.ds(first, TOK), :]
        seen = jnp.zeros((TOK, 128), F32)
        for behind in range(5):
            seen = seen + jnp.where(padded_ids[pl.ds(row + behind, 1), :] <= column, 1.0, 0.0)
        count = jnp.sum(seen, axis=-1, keepdims=True).astype(jnp.int32)
        q_end[TOK * chunk : TOK * chunk + TOK, :] = count + 128 * row
    lane = lax.broadcasted_iota(jnp.int32, (1, CLASS_ROWS), 1)
    skipped = jnp.zeros((1, CLASS_ROWS), jnp.int32)
    for chunk in range(1, HEADS + 1):
        skipped = skipped + jnp.where(lane >= TOK * chunk, 3 * TOK, 0)
    for place_of, apart in enumerate((0, 3, 1, 2)):
        tokens[place_of] = lane + skipped + TOK * lax.rem(group + apart, 4)
    for block in range(8):
        at = pl.ds(128 * block, 128)
        normed_turned[at, :] = jnp.transpose(normed[:, at].astype(F32)).astype(BF)
    own[1].wait()
    loop(1, HEADS, lambda k: q_copy(k).wait_recv())
    short = left[:LONG]
    for a in range(4):
        parts = []
        for chunk in (2 * a, 2 * a + 1):
            q = q_in[chunk].astype(F32)
            parts += [jnp.where(short, q, 0.0), jnp.where(short, swap(q), 0.0)[: TOK - LONG]]
        q_all[2 * TOK * a : 2 * TOK * (a + 1), :] = jnp.concatenate(parts, axis=0).astype(BF)

    def tiles(a):
        whole = [(512 * part, min(512, 256 * a - 512 * part), False) for part in range(-(-a // 2))]
        return whole + [(256 * a, 384 if a == 3 else 512, True)]

    def pair_rows(a):
        return pl.ds(2 * TOK * a, 2 * TOK)

    def shown(a, place_of, first, width):
        return tokens[place_of][:, first : first + width] < q_end[pair_rows(a), :]

    def att_copy(chunk):
        k = lax.rem(chunk - mine + HEADS, HEADS)
        return remote(out_pack.at[chunk], att_all.at[mine], att_send.at[k], att_recv.at[k], 4 * chunk + group)

    summed[...] = jnp.zeros_like(summed)
    mass[...] = jnp.zeros_like(mass)

    def attend(place_of):
        @pl.when(place_of == 1)
        def _():
            def pass_on(chunk):
                z_copy(chunk, 0).wait_recv()
                f_copy(chunk, 0).start()
                z_copy(chunk + 4, 1).wait_recv()
                f_copy(chunk + 4, 1).start()

            loop(0, 4, pass_on)
            loop(4, 8, lambda chunk: z_copy(chunk, 0).wait_recv())

        @pl.when(place_of == 2)
        def _():
            loop(0, 4, lambda chunk: z_copy(chunk, 1).wait_recv())

        add_class(place_of, None)

    def add_class(place_of, then):
        for a in range(4):
            rows = pair_rows(a)
            q = q_all[rows, :]
            for first, width, masked in tiles(a):
                block = kv[place_of, first : first + width, :]
                p = jnp.exp(dot_t(q, block))
                if masked:
                    p = jnp.where(shown(a, place_of, first, width), p, 0.0)
                part_mass = p[:, :128]
                for part in range(1, width // 128):
                    part_mass = part_mass + p[:, 128 * part : 128 * part + 128]
                mass[rows, :] += part_mass
                summed[rows, :] += dot(p.astype(BF), block)
            if then is not None:
                then(a)

    def hand_over(a):
        rows = pair_rows(a)
        one_over = 1.0 / jnp.sum(mass[rows, :], axis=-1, keepdims=True)
        result = summed[rows, :] * one_over
        out[rows, :] = result.astype(BF)
        inverse[rows, :] = one_over
        for half in range(2):
            chunk = 2 * a + half
            value = result[TOK * half : TOK * half + TOK]
            out_pack[chunk] = packed(swap(value), value, left)

            @pl.when(mine != chunk)
            def _():
                att_copy(chunk).start()

            @pl.when(mine == chunk)
            def _():
                pltpu.make_async_copy(out_pack.at[chunk], att_all.at[mine], local.at[0]).start()

    loop(0, 3, attend)
    loop(0, 4, lambda chunk: (f_copy(chunk, 0).wait_recv(), f_copy(chunk + 4, 1).wait_recv()))
    add_class(3, hand_over)

    loads[4].wait()
    loads[5].wait()
    pltpu.make_async_copy(out_pack.at[mine], att_all.at[mine], local.at[0]).wait()

    def att_arrived(k):
        peer = lax.rem(mine + k, HEADS)
        att_copy(peer).wait_recv()

    loop(1, HEADS, att_arrived)
    for pair in range(HEADS // 2):
        slab = unpacked_pair(att_all[2 * pair], att_all[2 * pair + 1], left)
        att[:, 128 * pair : 128 * pair + 128] = slab.astype(BF)
        att_turned[128 * pair : 128 * pair + 128, :] = jnp.transpose(slab).astype(BF)
    for block in range(4):
        columns = pl.ds(256 * block, 256)
        behind = pl.ds(D + 256 * block, 256)
        shift = dot(att[...], wo[:, columns])
        factor = jnp.exp(-dot(att[...], wo[:, behind]))
        upstream = up[:, columns].astype(F32)
        latent = (act[:, columns].astype(F32) - shift) * factor
        scaled = upstream * factor
        carry_part[:, columns] = scaled
        affine_grad[:, columns] = (-scaled).astype(BF)
        affine_grad[:, behind] = (1.0 - upstream * latent).astype(BF)

    def g_copy(head):
        k = lax.rem(head - mine + HEADS, HEADS)
        return remote(g_pack.at[head], g_in.at[mine], g_send.at[k], g_recv.at[k], 4 * head + group)

    def g_own():
        return pltpu.make_async_copy(g_pack.at[mine], g_in.at[mine], local.at[1])

    for block in range(2):
        g = dot_t(affine_grad[...], wo[pl.ds(256 * block, 256), :])
        for half in range(2):
            head = 4 * block + 2 * half
            slab = g[:, 128 * half : 128 * half + 128]
            turned_slab = swap(slab)
            g_pack[head] = packed(slab, turned_slab, left)
            g_pack[head + 1] = packed(turned_slab, slab, left)
        for head in range(4 * block, 4 * block + 4):

            @pl.when(mine != head)
            def _():
                g_copy(head).start()

    g_own().start()
    for block in range(8):
        columns = pl.ds(256 * block, 256)
        term = dot(att_turned[...], affine_grad[:, columns]).astype(BF)
        for owner in range(N_SEQ):
            for half in range(2):
                stream, row = OUT_PLACES[2 * block + half]
                out_sum.terms[stream][slot(FLAT_FIRST[stream], owner, bits), row : row + 16, :] = term[
                    16 * owner : 16 * owner + 16, 128 * half : 128 * half + 128
                ]
    for stream in out_sum.streams:
        out_sum.start(stream, 0)

    for a in range(4):
        q_turned[a] = jnp.transpose(q_all[pair_rows(a), :].astype(F32))[:HEAD_DIM].astype(BF)
    g_own().wait()
    loop(1, HEADS, lambda k: g_copy(lax.rem(mine + k, HEADS)).wait_recv())

    for a in range(4):
        rows = pair_rows(a)
        parts = []
        for chunk in (2 * a, 2 * a + 1):
            g = g_in[chunk].astype(F32)
            parts += [jnp.where(short, 0.0, swap(g)), jnp.where(short, 0.0, g)[: TOK - LONG]]
        g = jnp.concatenate(parts, axis=0)
        g_all[rows, :] = g.astype(BF)
        correction[rows, :] = jnp.sum(g * out[rows, :].astype(F32), axis=-1, keepdims=True)
        g_turned[a] = jnp.transpose(g)[HEAD_DIM:].astype(BF)
    summed[...] = jnp.zeros_like(summed)

    def dq_copy(chunk):
        k = lax.rem(chunk - mine + HEADS, HEADS)
        return remote(dq.at[chunk], dq_all.at[mine], dq_send.at[k], dq_recv.at[k], 4 * chunk + group)

    def dq_own():
        return pltpu.make_async_copy(dq.at[mine], dq_all.at[mine], local.at[2])

    def far_copy(way):
        return remote(
            class_sum[way].at[2], far_half[way], back_send.at[way], back_recv.at[way], z_back if way else z_next
        )

    def class_copy(place_of, half):
        at = 2 * place_of + half
        target, peer = (from_next, z_back) if place_of == 1 else (from_back, z_next)
        return remote(class_sum[half].at[place_of - 1], target[half], back_send.at[at], back_recv.at[at], peer)

    def dkv_copy(k):
        peer = lax.rem(mine + k, HEADS)
        return remote(dkv.at[chunk_rows(peer)], dkv_all.at[mine], dkv_send.at[k], dkv_recv.at[k], 4 * peer + group)

    def dkv_own():
        return pltpu.make_async_copy(dkv.at[chunk_rows(mine)], dkv_all.at[mine], local.at[3])

    def send_keys(chunk):
        @pl.when(mine != chunk)
        def _():
            dkv_copy(lax.rem(chunk - mine + HEADS, HEADS)).start()

        @pl.when(mine == chunk)
        def _():
            dkv_own().start()

    columns_of = (slice(0, LOW), slice(LOW, CLASS_ROWS))

    def settle(place_of, half, extra):
        value = total[:, columns_of[half]]
        if extra is not None:
            value = value + extra[...].astype(F32)
        class_sum[half][place_of - 1] = value.astype(BF)

    def settle_own(half):
        for first in range(0, LOW, 128) if half == 0 else range(LOW, CLASS, 128):
            begin = first - LOW * half
            at = slice(begin, begin + 128)
            value = total[:, first : first + 128]
            value = value + from_back[half][:, at].astype(F32) + from_next[half][:, at].astype(F32)
            width = min(128, CLASS - first)
            dkv[first : first + width, :] = jnp.transpose(value)[:width].astype(BF)

    def spans(a, half):
        low, high = ((0, LOW), (LOW, CLASS_ROWS))[half]
        cut = min(max(256 * a, low), high)
        end = min(256 * a + (384 if a == 3 else 512), high)
        return [(low, cut - low, False)] * (cut > low) + [(cut, end - cut, True)] * (end > cut)

    def back_class(place_of, half, then):
        spread = {0: (0, LOW), 1: (LOW, CLASS_ROWS), None: (0, CLASS_ROWS)}[half]
        total[:, spread[0] : spread[1]] = jnp.zeros((128, spread[1] - spread[0]), F32)
        for a in (3, 2, 1, 0):
            rows = pair_rows(a)
            q = q_all[rows, :]
            g = g_all[rows, :]
            one_over = inverse[rows, :]
            corr = correction[rows, :]
            pieces = tiles(a) if half is None else spans(a, half)
            if pieces:
                first = pieces[0][0]
                width = sum(piece[1] for piece in pieces)
                block = kv[place_of, first : first + width, :]
                p = jnp.exp(dot_t(q, block)) * one_over
                parts = []
                for begin, size, masked in pieces:
                    part = p[:, begin - first : begin - first + size]
                    parts.append(jnp.where(shown(a, place_of, begin, size), part, 0.0) if masked else part)
                p = jnp.concatenate(parts, axis=1) if len(parts) > 1 else parts[0]
                ds = (p * (dot_t(g, block) - corr)).astype(BF)
                total[:HEAD_DIM, first : first + width] += dot(q_turned[a], ds)
                total[HEAD_DIM:, first : first + width] += dot(g_turned[a], p.astype(BF))
                summed[rows, :] += dot(ds, block)
            if then is not None:
                then(a)

    def send_dq(a):
        result = summed[pair_rows(a), :] * 0.125
        for half in range(2):
            chunk = 2 * a + half
            value = result[TOK * half : TOK * half + TOK]
            dq[chunk] = packed(value, swap(value), left)

            @pl.when(mine != chunk)
            def _():
                dq_copy(chunk).start()

            @pl.when(mine == chunk)
            def _():
                dq_own().start()

    back_class(3, None, None)
    settle(3, 0, None)
    far_copy(0).start()
    settle(3, 1, None)
    far_copy(1).start()
    back_class(1, 0, None)
    settle(1, 0, None)
    class_copy(1, 0).start()
    back_class(2, 1, None)
    settle(2, 1, None)
    class_copy(2, 1).start()
    back_class(2, 0, None)
    far_copy(0).wait_recv()
    settle(2, 0, far_half[0])
    class_copy(2, 0).start()
    out_sum.advance(0)
    back_class(1, 1, None)
    far_copy(1).wait_recv()
    settle(1, 1, far_half[1])
    class_copy(1, 1).start()
    back_class(0, None, send_dq)
    for half in (1, 0):
        for place_of in (2, 1):
            class_copy(place_of, half).wait_recv()
        settle_own(half)
        for chunk in range(4, 8) if half else range(4):
            send_keys(chunk)
    out_sum.advance(1)

    def unit_back(grad, raw):
        scale = unit_scale(raw, left)
        unit = raw * scale
        return scale * (grad - unit * (per_head_sum(grad * unit, left) * (1.0 / HEAD_DIM)))

    def keys_of(head):
        return dkv_all[head].astype(F32)

    def term_of(which):
        places, into, first = (Q_PLACES, q_sum, 0) if which == 0 else (KV_PLACES, kv_sum, 8 * (2 - which))
        for block in range(2):
            term = dot(normed_turned[...], grads[which, :, 256 * block : 256 * block + 256]).astype(BF)
            for owner in range(N_SEQ):
                for part in range(4):
                    slab, half = part // 2, part % 2
                    stream, row = places[first + 4 * block + 2 * slab + half]
                    top = 32 * owner + 16 * half
                    into.terms[stream][slot(ALL_LINKS[stream], owner, bits), row : row + 16, :] = term[
                        top : top + 16, 128 * slab : 128 * slab + 128
                    ]

    dq_own().wait()
    loop(1, HEADS, lambda k: dq_copy(lax.rem(mine + k, HEADS)).wait_recv())
    for pair in range(HEADS // 2):
        at = pl.ds(128 * pair, 128)
        q_grad = unpacked_pair(dq_all[2 * pair], dq_all[2 * pair + 1], left)
        grads[0, :, at] = unit_back(q_grad, q_raw[:, at]).astype(BF)
    term_of(0)
    for stream in range(5):
        q_sum.start(stream, 0)
    out_sum.advance(2)
    for block in range(4):
        at = pl.ds(256 * block, 256)
        gn[:, at] = dot_t(grads[0], wq[at, :])
    dkv_own().wait()
    loop(1, HEADS, lambda k: dkv_copy(k).wait_recv())
    for pair in range(HEADS // 2):
        low, high = keys_of(2 * pair), keys_of(2 * pair + 1)
        grads[2, :, 128 * pair : 128 * pair + 128] = jnp.where(left, swap(low), high).astype(BF)
    term_of(2)
    for stream in range(3):
        kv_sum.start(stream, 0)
    out_sum.advance(3)
    for pair in range(HEADS // 2):
        at = pl.ds(128 * pair, 128)
        low, high = keys_of(2 * pair), keys_of(2 * pair + 1)
        grads[1, :, at] = unit_back(jnp.where(left, low, swap(high)), k_raw[:, at]).astype(BF)
    term_of(1)
    for stream in range(3, 5):
        kv_sum.start(stream, 0)
    q_sum.advance(0)
    for block in range(4):
        at = pl.ds(256 * block, 256)
        gn[:, at] += dot_t(grads[1], wk[at, :]) + dot_t(grads[2], wv[at, :])
    field = act[...].astype(F32)
    row_scale = lax.rsqrt(jnp.mean(field * field, axis=-1, keepdims=True) + EPSILON)
    unit = field * row_scale
    grad_normed = gn[...]
    mean = jnp.mean(grad_normed * unit, axis=-1, keepdims=True)
    grad_input[...] = (carry_part[...] + row_scale * (grad_normed - unit * mean)).astype(BF)

    def carry(piece):
        first, count = ((0, 48), (48, 32), (80, 32), (112, 24))[piece]
        rows = pl.ds(first, count)
        return pltpu.make_async_remote_copy(
            src_ref=grad_input.at[rows], dst_ref=moved.at[rows], send_sem=carry_sem.at[0, piece],
            recv_sem=carry_sem.at[1, piece], device_id={"section": before, "seq": across}, device_id_type=MESH,
        )

    carry(0).start()
    q_sum.advance(1)
    kv_sum.advance(0)
    carry(1).start()
    q_sum.advance(2)
    for stream in out_sum.streams:
        result = out_sum.result(stream)
        for part in range(16):
            if OUT_PLACES[part][0] == stream:
                row = OUT_PLACES[part][1]
                sum_out[:, 128 * part : 128 * part + 128] = result[row : row + 16]
    kv_sum.advance(1)
    carry(2).start()
    carry(3).start()
    q_sum.advance(3)

    def deliver(halving, places, targets):
        for stream in range(5):
            result = halving.result(stream)
            for part in range(8 * len(targets)):
                if places[part][0] == stream:
                    row = places[part][1]
                    column, top = 128 * (part % 8 // 2), 16 * (part % 2)
                    targets[part // 8][top : top + 16, column : column + 128] = result[row : row + 16]

    kv_sum.advance(2)
    deliver(q_sum, Q_PLACES, (sum_q,))
    kv_sum.advance(3)
    deliver(kv_sum, KV_PLACES, (sum_v, sum_k))
    for piece in range(4):
        carry(piece).wait()

    def left_all(k):
        kv_copy(k).wait_send()
        q_copy(k).wait_send()
        att_copy(lax.rem(mine + k, HEADS)).wait_send()
        g_copy(lax.rem(mine + k, HEADS)).wait_send()
        dq_copy(lax.rem(mine + k, HEADS)).wait_send()
        dkv_copy(k).wait_send()

    loop(1, HEADS, left_all)

    def left_z(chunk):
        for way in range(2):
            z_copy(chunk, way).wait_send()

    loop(0, HEADS, left_z)
    loop(0, 4, lambda chunk: (f_copy(chunk, 0).wait_send(), f_copy(chunk + 4, 1).wait_send()))
    for way in range(2):
        far_copy(way).wait_send()
        for place_of in (1, 2):
            class_copy(place_of, way).wait_send()
    out_sum.drain()
    q_sum.drain()
    kv_sum.drain()


def whole_layer(*operands):
    eight, full, short = (HEADS * TOK, 128), (TOK, D), (HEADS, LONG, 128)
    low, high = (128, LOW), (128, CLASS_ROWS - LOW)
    scratch = [
        (full, BF), (full, BF), ((D, INNER), BF), ((D, INNER), BF), ((D, INNER), BF), ((INNER, 2 * D), BF),
        (full, BF), ((D, TOK), BF), ((TOK, INNER), F32), ((TOK, INNER), F32), (short, BF), ((HEADS, TOK, 128), BF),
        ((4, CLASS_ROWS, 128), BF), (eight, BF), (eight, BF), ((TOKENS, 1), jnp.int32), (eight, BF), ((CLASS, 1), F32),
        (short, BF), ((TOK, INNER), BF), ((INNER, TOK), BF), ((TOK, 2 * D), BF), (short, BF), (full, F32),
        ((128, CLASS_ROWS), F32), (eight, BF), (short, BF), ((HEADS, TOK, 128), BF), (short, BF),
        ((3, TOK, INNER), BF), (full, F32), (full, BF),
        ((40, 128), jnp.int32), ((CLASS, 1), jnp.int32), ((4, 1, CLASS_ROWS), jnp.int32), (eight, F32), (eight, F32),
        ((4, HEAD_DIM, 2 * TOK), BF), ((4, HEAD_DIM, 2 * TOK), BF), ((CLASS, 1), F32),
        (low, BF), (high, BF), (low, BF), (high, BF), ((3, *low), BF), ((3, *high), BF),
        (low, BF), (high, BF), (short, BF), (short, BF), (short, BF),
    ]
    dma = pltpu.SemaphoreType.DMA
    return pl.pallas_call(
        layer_body,
        out_shape=[jax.ShapeDtypeStruct((32, INNER), F32)] * 3
        + [jax.ShapeDtypeStruct((16, 2 * D), F32), jax.ShapeDtypeStruct((TOK, D), BF)],
        in_specs=[ANY] * 6 + [VMEM],
        out_specs=[VMEM] * 5,
        scratch_shapes=[pltpu.VMEM(shape, dtype) for shape, dtype in scratch]
        + halving_scratch(OUT_ROWS)
        + halving_scratch(Q_ROWS)
        + halving_scratch(KV_ROWS)
        + [dma((6,)), dma((8,)), dma((8,)), dma((8,)), dma((8,)), dma((2, 8)), dma((2, 8)), dma((8,)), dma((8,))]
        + [dma((8,))] * 8
        + [dma((4,)), dma((2, 4)), dma((6,)), dma((6,))],
        compiler_params=pltpu.CompilerParams(collective_id=1, has_side_effects=True, vmem_limit_bytes=BIG),
        name="layer",
    )(*operands)


def hand_out_body(sum_q, sum_k, sum_v, sum_out, moved, flip, carry, out_q, out_k, out_v, out_out):
    out_q[...] = sum_q[...]
    out_k[...] = sum_k[...]
    out_v[...] = sum_v[...]
    out_out[...] = sum_out[...]
    turned = (flip[...] == lax.broadcasted_iota(jnp.int32, (TOK, TOK), 0)).astype(F32)
    chosen = jnp.transpose(turned).astype(BF)
    last = (lax.axis_index("section") + jnp.zeros((TOK, 1), jnp.int32)) == 3
    for block in range(4):
        at = pl.ds(256 * block, 256)
        carry[:, at] = jnp.where(last, 0.0, dot(chosen, moved[:, at])).astype(BF)


def hand_out(*operands):
    return pl.pallas_call(
        hand_out_body,
        out_shape=[jax.ShapeDtypeStruct((TOK, D), BF)]
        + [jax.ShapeDtypeStruct((32, INNER), F32)] * 3
        + [jax.ShapeDtypeStruct((16, 2 * D), F32)],
        in_specs=[VMEM] * 6,
        out_specs=[VMEM] * 5,
        name="hand_out",
    )(*operands)


def shards(activations, incoming, w_query, w_key, w_value, w_out, block_ids, flip_order):
    sums = whole_layer(
        activations[0], incoming[0], w_query[0], w_key[0], w_value[0], w_out[0], block_ids.reshape(TOKENS // 128, 128)
    )
    results = hand_out(*sums, flip_order)
    return tuple(result[None] for result in results)


def solution(mesh):
    by_both = P("section", "seq", None)
    by_layer = P("section", None, None)
    in_specs = (by_both, by_both, by_layer, by_layer, by_layer, by_layer, P(), P("section", None))
    return jax.shard_map(shards, mesh=mesh, in_specs=in_specs, out_specs=(by_both,) * 5, check_vma=False)
```
